32 devices in a mesh: ctx: 8 (over y, x, core), wt: 4 (over z).
Axes of the slice: x: 2, y: 2, z: 4, core: 2. Of those that a mesh axis runs over, the one named last changes fastest.
Arguments:
- hidden_in: bfloat16 [4, 1024, 2048], P('wt', 'ctx'), may hold values from -6 to 6
- doc_lengths: int32 [4, 2], P('wt'), may hold values from 1 to 768, 1024 in all within a row
- routes: int32 [4, 1024, 8], P('wt', 'ctx'), may hold values from 0 to 31, all different within a row; in each aligned block of 128 rows (0 to 127, 128 to 255, ..., all dimensions but the last counted through in order) at most 64 rows name the same one
- gain_attn: float32 [2048], replicated, may hold values from 0.1 to 1.9
- w_query: bfloat16 [2048, 4096], P(('ctx', 'wt')), may hold values from -0.125 to 0.125
- key_weight: bfloat16 [2048, 512], P(('ctx', 'wt')), may hold values from -0.125 to 0.125
- value_weight: bfloat16 [2048, 512], P(('ctx', 'wt')), may hold values from -0.125 to 0.125
- gain_query: float32 [128], replicated, may hold values from 0.1 to 1.9
- gain_key: float32 [128], replicated, may hold values from 0.1 to 1.9
- w_out: bfloat16 [4096, 2048], P(('ctx', 'wt')), may hold values from -1.5 to 1.5
- gain_moe: float32 [2048], replicated, may hold values from 0.1 to 1.9
- w_router: bfloat16 [2048, 32], P(('ctx', 'wt')), may hold values from -0.0625 to 0.0625
- expert_gate: bfloat16 [32, 2048, 768], P(('ctx', 'wt')), may hold values from -0.125 to 0.125
- expert_up: bfloat16 [32, 2048, 768], P(('ctx', 'wt')), may hold values from -0.125 to 0.125
- expert_down: bfloat16 [32, 768, 2048], P(('ctx', 'wt')), may hold values from -0.625 to 0.625
- out_grad: bfloat16 [4, 1024, 2048], P('wt', 'ctx'), may hold values from -6 to 6
Outputs:
- hidden_out: float32 [4, 1024, 2048], P('wt', 'ctx')
- grad_in: float32 [4, 1024, 2048], P('wt', 'ctx')
- grad_gain_attn: float32 [2048], replicated
- grad_w_query: float32 [2048, 4096], P(('ctx', 'wt'))
- grad_w_key: float32 [2048, 512], P(('ctx', 'wt'))
- grad_w_value: float32 [2048, 512], P(('ctx', 'wt'))
- grad_gain_query: float32 [128], replicated
- grad_gain_key: float32 [128], replicated
- grad_w_out: float32 [4096, 2048], P(('ctx', 'wt'))
- grad_gain_moe: float32 [2048], replicated
- grad_w_router: float32 [2048, 32], P(('ctx', 'wt'))
- grad_expert_gate: float32 [32, 2048, 768], P(('ctx', 'wt'))
- grad_expert_up: float32 [32, 2048, 768], P(('ctx', 'wt'))
- grad_expert_down: float32 [32, 768, 2048], P(('ctx', 'wt'))
The draws below stay inside these ranges and needn't reach their ends.
Inputs may be any that keep to these rules, and one draw needn't show every extreme that they name: `doc_lengths`: the 2 lengths of a stream sum to 1024; the longest is at most 768. `routes`: A token names 8 different experts. Within the rows of one device, no expert is named more than 64 times; on some device an expert is named exactly 64 times.
All inputs are finite; a program needn't handle non-finite values.
Results may differ from the reference program's by a relative error of at most 0.018.
Values may be sent and summed in bfloat16 or wider, within the bound.
A program may use at most 256 MiB of HBM per device.

```python
import math
import jax
import jax.numpy as jnp
import numpy as np
from jax import lax

EMBED_WIDTH = 2048
QUERY_HEADS = 32
KEY_VALUE_HEADS = 4
HEAD_SIZE = 128
FFE = 768
TOPK = 8
TOK_DEV = 128
EXPERTS = 32
STREAM_TOKENS = 1024
STREAM_COUNT = 4
DOC_MOST = 768
DOCS = 2
SEND = 64
CAP = 256


def shard_levels(stream_key, dims, pieces, low, largest):
    def one(axis_at, shards_of):
        steps = jax.random.uniform(jax.random.fold_in(jax.random.fold_in(stream_key, 6), axis_at), (shards_of,), jnp.float32, low / len(pieces), largest / len(pieces))
        return jnp.repeat(jnp.exp(steps), dims[axis_at] // shards_of).reshape((-1,) + (1,) * (len(dims) - axis_at - 1))

    loudness = one(*pieces[0])
    for cut in pieces[1:]:
        loudness = loudness * one(*cut)
    return loudness


def length_profile(number_of, total, bound, slope):
    weights = [(1 << 20) // math.isqrt(standing ** slope) + 1 for standing in range(2, number_of + 1)]
    rest, given = total - bound - (number_of - 1), [1] * (number_of - 1)
    while rest > 0:
        free = [i for i in range(number_of - 1) if given[i] < bound]
        mass, budget = sum([weights[i] for i in free]), rest
        for i in free:
            more = min(bound - given[i], max(1, budget * weights[i] // mass), rest)
            given[i] = given[i] + more
            rest = rest - more
    return np.array([bound] + given)


def ragged(own_key, amount, total, reach, lean):
    if amount == 2:
        one = jax.random.randint(own_key, (), max(1, total - reach), min(reach, total - 1) + 1)
        return jnp.stack([one, total - one])
    sizes = jnp.asarray(length_profile(amount, total, reach, lean), jnp.int32)
    pairs = (amount - 1) // 2
    source_of, sink = sizes[1:1 + 2 * pairs:2], sizes[2:2 + 2 * pairs:2]
    room = jnp.minimum(source_of - 1, reach - sink)
    passed = jax.random.randint(jax.random.fold_in(own_key, 1), (pairs,), 0, 1 << 20) % (room + 1)
    sizes = sizes.at[1:1 + 2 * pairs:2].set(source_of - passed).at[2:2 + 2 * pairs:2].set(sink + passed)
    return sizes[jax.random.permutation(jax.random.fold_in(own_key, 2), amount)]


def assign_block(own_key, own, number, rows, count, top, limit, skew):
    ranking = jax.random.permutation(own_key, count)
    crowded, common = shares(count, rows * top, limit, skew, True), shares(count, rows * top, limit, skew, False)
    places = jnp.arange(count)

    def named(tallies, turn):
        used = int((tallies > 0).sum())
        fixed = max(1, used // 4)
        moved = fixed + (places - fixed + turn * (used - fixed)) % max(1, count - fixed)
        return jnp.zeros((count,), jnp.int32).at[ranking[jnp.where(places < fixed, places, moved)]].set(jnp.asarray(tallies, jnp.int32))

    tallies = jnp.where(number % 4 == 0, named(crowded, number // 4), named(common, number - number // 4 - 1))
    mixed = jax.random.permutation(jax.random.fold_in(own, 3), count)
    source_of, taker = mixed[0:count // 2 * 2:2], mixed[1:count // 2 * 2:2]
    slack = jnp.minimum(tallies[source_of] - 1, limit - tallies[taker]) // 2
    slack = jnp.where((source_of == ranking[0]) | (taker == ranking[0]) | (tallies[taker] == 0), 0, jnp.maximum(slack, 0))
    moved = jax.random.randint(jax.random.fold_in(own, 4), (count // 2,), 0, 1 << 20) % (slack + 1)
    tallies = tallies.at[source_of].add(-moved).at[taker].add(moved)
    items = jnp.searchsorted(jnp.cumsum(tallies), jnp.arange(rows * top), side="right").astype(jnp.int32)
    listing = items.reshape(top, rows).T
    listing = listing[jax.random.permutation(jax.random.fold_in(own, 1), rows)]
    turn = jax.random.randint(jax.random.fold_in(own, 2), (rows, 1), 0, top)
    return jnp.take_along_axis(listing, (jnp.arange(top)[None, :] + turn) % top, axis=1)


def shares(count, total, bound, slope, full):
    loads = [(1 << 20) // math.isqrt(rank ** slope) + 1 for rank in range(1, count + 1)]
    largest = bound if full else min(bound, max(-(-total // count), total * loads[0] // sum(loads)))
    least = 1 if total - largest >= count - 1 else 0
    counts, spare = [largest] + [least] * (count - 1), total - largest - least * (count - 1)
    while spare > 0:
        free = [i for i in range(1, count) if counts[i] < largest] or [i for i in range(1, count) if counts[i] < bound]
        mass, remaining = sum([loads[i] for i in free]), spare
        for i in free:
            more = min(bound - counts[i], max(1, remaining * loads[i] // mass), spare)
            counts[i] = counts[i] + more
            spare = spare - more
    return np.array(counts)


def scatter_about(own_key, dims, spread, bound, split=(), kind=jnp.bfloat16):
    level = shard_levels(own_key, dims, split, -0.22, 0.18) if split else 1.0
    values = jax.random.normal(own_key, dims, jnp.float32) * spread * level
    return jnp.minimum(jnp.maximum(values, -bound), bound).astype(kind)


def setup_inputs(seed: int = 0) -> dict:
    splits = jax.random.split(jax.random.key(seed), 17)
    hidden_in = scatter_about(splits[0], (STREAM_COUNT, STREAM_TOKENS, EMBED_WIDTH), 1.0, 6.0, ((0, 4), (1, 8)))
    doc_lengths = jax.vmap(lambda own: ragged(own, DOCS, STREAM_TOKENS, DOC_MOST, 2))(jax.random.split(splits[1], STREAM_COUNT)).reshape((STREAM_COUNT, DOCS)).astype(jnp.int32)
    routes_keys = jax.random.split(jax.random.fold_in(splits[2], 1), STREAM_COUNT * STREAM_TOKENS // TOK_DEV)
    routes_turns = jax.random.permutation(jax.random.fold_in(splits[2], 3), STREAM_COUNT * STREAM_TOKENS // TOK_DEV)
    routes = jax.vmap(lambda own, number: assign_block(jax.random.fold_in(splits[2], 2), own, number, TOK_DEV, EXPERTS, TOPK, SEND, 2))(routes_keys, routes_turns).reshape((STREAM_COUNT, STREAM_TOKENS, TOPK))
    gain_attn = jnp.clip(1.0 + 0.18 * jax.random.normal(splits[3], (EMBED_WIDTH,), jnp.float32), 0.1, 1.9)
    w_query = scatter_about(splits[4], (EMBED_WIDTH, QUERY_HEADS * HEAD_SIZE), EMBED_WIDTH ** -0.5, 0.125, ((0, 32),))
    key_weight = scatter_about(splits[5], (EMBED_WIDTH, KEY_VALUE_HEADS * HEAD_SIZE), EMBED_WIDTH ** -0.5, 0.125, ((0, 32),))
    value_weight = scatter_about(splits[6], (EMBED_WIDTH, KEY_VALUE_HEADS * HEAD_SIZE), EMBED_WIDTH ** -0.5, 0.125, ((0, 32),))
    gain_query = jnp.clip(1.0 + 0.18 * jax.random.normal(splits[7], (HEAD_SIZE,), jnp.float32), 0.1, 1.9)
    gain_key = jnp.clip(1.0 + 0.18 * jax.random.normal(splits[8], (HEAD_SIZE,), jnp.float32), 0.1, 1.9)
    w_out = scatter_about(splits[9], (QUERY_HEADS * HEAD_SIZE, EMBED_WIDTH), 16 ** -0.5, 1.5, ((0, 32),))
    gain_moe = jnp.clip(1.0 + 0.18 * jax.random.normal(splits[10], (EMBED_WIDTH,), jnp.float32), 0.1, 1.9)
    w_router = scatter_about(splits[11], (EMBED_WIDTH, EXPERTS), (4 * EMBED_WIDTH) ** -0.5, 0.0625, ((0, 32),))
    expert_gate = scatter_about(splits[12], (EXPERTS, EMBED_WIDTH, FFE), EMBED_WIDTH ** -0.5, 0.125, ((0, 32),))
    expert_up = scatter_about(splits[13], (EXPERTS, EMBED_WIDTH, FFE), EMBED_WIDTH ** -0.5, 0.125, ((0, 32),))
    expert_down = scatter_about(splits[14], (EXPERTS, FFE, EMBED_WIDTH), 96 ** -0.5, 0.625, ((0, 32),))
    out_grad = scatter_about(splits[15], (STREAM_COUNT, STREAM_TOKENS, EMBED_WIDTH), 1.0, 6.0, ((0, 4), (1, 8)))
    return {"hidden_in": hidden_in, "doc_lengths": doc_lengths, "routes": routes, "gain_attn": gain_attn, "w_query": w_query, "key_weight": key_weight, "value_weight": value_weight, "gain_query": gain_query, "gain_key": gain_key, "w_out": w_out, "gain_moe": gain_moe, "w_router": w_router, "expert_gate": expert_gate, "expert_up": expert_up, "expert_down": expert_down, "out_grad": out_grad}


@jax.custom_vjp
def reduced_precision(v):
    return lax.optimization_barrier(v.astype(jnp.bfloat16)).astype(jnp.float32)

@jax.custom_vjp
def reduced_backward(v):
    return v

def low_keep(v):
    return (reduced_precision(v), None)

def low_pass(kept, grad):
    return (grad,)

def back_keep(v):
    return (v, None)

def back_low(kept, grad):
    return (reduced_precision(grad),)
reduced_precision.defvjp(low_keep, low_pass)
reduced_backward.defvjp(back_keep, back_low)
EPS = 1e-06
THETA = 1000000.0
HIGH_PRECISION = lax.Precision.HIGHEST
MASKED = -1e+30

def norm_rows(value_rows, gain_vec):
    return value_rows * lax.rsqrt(lax.optimization_barrier(jnp.mean(value_rows * value_rows, axis=-1, keepdims=True)) + EPS) * gain_vec

def rotary_tables(positions, head_dim):
    half_dim = head_dim // 2
    frequency = jnp.exp(jnp.arange(half_dim, dtype=jnp.float32) * (-2.0 * math.log(THETA) / head_dim))
    angles = positions.astype(jnp.float32)[:, None] * frequency[None, :]
    angles = jnp.concatenate([angles, angles], axis=1)
    return (jnp.cos(angles)[:, None, :], jnp.sin(angles)[:, None, :])

def rotate(value_rows, cosine_table, sine_table):
    half_dim = value_rows.shape[-1] // 2
    turned = jnp.concatenate([-value_rows[..., half_dim:], value_rows[..., :half_dim]], axis=-1)
    return value_rows * cosine_table + turned * sine_table

def soft_rows(scores):
    row_peak = lax.optimization_barrier(jnp.max(scores, axis=-1, keepdims=True))
    exponent = jnp.exp(scores - row_peak)
    return exponent / lax.optimization_barrier(jnp.sum(exponent, axis=-1, keepdims=True))

def document_ids(lengths):
    doc_ends = jnp.cumsum(lengths).astype(jnp.int32)
    positions = jnp.arange(STREAM_TOKENS, dtype=jnp.int32)
    return lax.optimization_barrier(jnp.sum((doc_ends[None, :] <= positions[:, None]).astype(jnp.int32), axis=1)).astype(jnp.int32)

def attend(queries, key_rows, value_rows, documents):
    query_matrix = 512
    group_width = QUERY_HEADS // KEY_VALUE_HEADS
    positions = jnp.arange(STREAM_TOKENS, dtype=jnp.int32)
    block_count = STREAM_TOKENS // query_matrix

    def one_block(block_args):
        query_block, block_pos, block_doc = block_args
        head_grouped = query_block.reshape(query_matrix, KEY_VALUE_HEADS, group_width, HEAD_SIZE)
        scores = jnp.einsum('qkgd,skd->kgqs', head_grouped, key_rows, precision=HIGH_PRECISION) * HEAD_SIZE ** (-0.5)
        scores = reduced_backward(scores)
        allowed = (positions[None, :] <= block_pos[:, None]) & (documents[None, :] == block_doc[:, None])
        scores = jnp.where(allowed, scores, MASKED)
        weights = reduced_precision(soft_rows(scores))
        mixed = jnp.einsum('kgqs,skd->qkgd', weights, value_rows, precision=HIGH_PRECISION)
        return mixed.reshape(query_matrix, QUERY_HEADS * HEAD_SIZE)
    outputs = lax.map(jax.checkpoint(one_block), (queries.reshape(block_count, query_matrix, QUERY_HEADS, HEAD_SIZE), positions.reshape(block_count, query_matrix), documents.reshape(block_count, query_matrix)))
    return outputs.reshape(STREAM_TOKENS, QUERY_HEADS * HEAD_SIZE)

def reference(hidden_in, doc_lengths, routes, gain_attn, w_query, key_weight, value_weight, gain_query, gain_key, w_out, gain_moe, w_router, expert_gate, expert_up, expert_down, out_grad):
    cap_rows = STREAM_COUNT * CAP
    token_count = STREAM_COUNT * STREAM_TOKENS
    documents = jnp.stack([document_ids(doc_lengths[stream]) for stream in range(STREAM_COUNT)])
    positions = jnp.arange(STREAM_TOKENS, dtype=jnp.int32)
    cosine_table, sine_table = rotary_tables(positions, HEAD_SIZE)
    expert_ids = jnp.arange(EXPERTS, dtype=jnp.int32)
    picked = (routes[..., None] == expert_ids).astype(jnp.int32)
    expert_hits = lax.optimization_barrier(jnp.sum(picked, axis=2)).astype(jnp.int32)
    before = jnp.cumsum(expert_hits, axis=1).astype(jnp.int32) - expert_hits
    slot_index = lax.optimization_barrier(jnp.sum(picked * before[:, :, None, :], axis=3)).astype(jnp.int32)
    kept_mask = slot_index < CAP
    stream_ids = jnp.arange(STREAM_COUNT, dtype=jnp.int32)[:, None, None]
    row_index = jnp.where(kept_mask, stream_ids * CAP + slot_index, cap_rows).astype(jnp.int32)
    pair_token = jnp.broadcast_to(jnp.arange(token_count, dtype=jnp.int32).reshape(STREAM_COUNT, STREAM_TOKENS, 1), routes.shape)
    slot_table = jnp.full((EXPERTS, cap_rows), -1, jnp.int32).at[routes.reshape(-1), row_index.reshape(-1)].set(pair_token.reshape(-1), mode='drop')
    filled = slot_table >= 0
    source = jnp.maximum(slot_table, 0)
    flat_pick = jnp.where(kept_mask, routes * cap_rows + row_index, 0).astype(jnp.int32).reshape(token_count, TOPK)
    keep_float = kept_mask.astype(jnp.float32).reshape(token_count, TOPK)
    picked_float = picked.reshape(token_count, TOPK, EXPERTS).astype(jnp.float32)

    def forward(hidden, gain_a, wq_full, key_weight_whole, value_weight_whole, gain_q, gain_k, wo_full, gain_m, wr_full, gate_all, up_all, down_all):
        flat = hidden.reshape(token_count, EMBED_WIDTH)
        normalized_input = reduced_precision(norm_rows(flat, gain_a))
        queries = reduced_backward(jnp.dot(normalized_input, wq_full, precision=HIGH_PRECISION)).reshape(STREAM_COUNT, STREAM_TOKENS, QUERY_HEADS, HEAD_SIZE)
        key_rows = reduced_backward(jnp.dot(normalized_input, key_weight_whole, precision=HIGH_PRECISION)).reshape(STREAM_COUNT, STREAM_TOKENS, KEY_VALUE_HEADS, HEAD_SIZE)
        value_rows = reduced_precision(reduced_backward(jnp.dot(normalized_input, value_weight_whole, precision=HIGH_PRECISION))).reshape(STREAM_COUNT, STREAM_TOKENS, KEY_VALUE_HEADS, HEAD_SIZE)
        queries = reduced_precision(rotate(norm_rows(queries, gain_q), cosine_table, sine_table))
        key_rows = reduced_precision(rotate(norm_rows(key_rows, gain_k), cosine_table, sine_table))
        mixed = jnp.concatenate([attend(queries[stream], key_rows[stream], value_rows[stream], documents[stream]) for stream in range(STREAM_COUNT)], axis=0)
        mixed = reduced_precision(reduced_backward(mixed))
        attn = reduced_backward(jnp.dot(mixed, wo_full, precision=HIGH_PRECISION))
        resid = flat + attn
        normed_mid = reduced_precision(norm_rows(resid, gain_m))
        logits = reduced_backward(jnp.dot(normed_mid, wr_full, precision=HIGH_PRECISION))
        router_probs = soft_rows(logits)
        chosen = lax.optimization_barrier(jnp.sum(picked_float * router_probs[:, None, :], axis=2))
        gates = chosen / lax.optimization_barrier(jnp.sum(chosen, axis=1, keepdims=True)) * keep_float

        def one_expert(expert_args):
            gate_w, up_w, down_w, src_rows, used_rows = expert_args
            rows = reduced_backward(jnp.where(used_rows[:, None], normed_mid[src_rows], 0.0))
            gate_h = reduced_backward(jnp.dot(rows, gate_w, precision=HIGH_PRECISION))
            up_h = reduced_backward(jnp.dot(rows, up_w, precision=HIGH_PRECISION))
            hidden_h = reduced_precision(gate_h * jax.nn.sigmoid(gate_h) * up_h)
            return reduced_precision(reduced_backward(jnp.dot(hidden_h, down_w, precision=HIGH_PRECISION)))
        expert_outs = lax.map(jax.checkpoint(one_expert), (gate_all, up_all, down_all, source, filled))
        gathered = expert_outs.reshape(EXPERTS * cap_rows, EMBED_WIDTH)[flat_pick]
        combined = lax.optimization_barrier(jnp.sum(gates[:, :, None] * gathered, axis=1))
        return (resid + combined).reshape(STREAM_COUNT, STREAM_TOKENS, EMBED_WIDTH)
    primals = (hidden_in.astype(jnp.float32), gain_attn, w_query.astype(jnp.float32), key_weight.astype(jnp.float32), value_weight.astype(jnp.float32), gain_query, gain_key, w_out.astype(jnp.float32), gain_moe, w_router.astype(jnp.float32), expert_gate.astype(jnp.float32), expert_up.astype(jnp.float32), expert_down.astype(jnp.float32))
    result, pullback = jax.vjp(forward, *primals)
    grads = pullback(out_grad.astype(jnp.float32))
    return (result, grads[0], grads[1], grads[2], grads[3], grads[4], grads[5], grads[6], grads[7], grads[8], grads[9], grads[10], grads[11], grads[12])
```

```python
import math

import jax
import jax.numpy as jnp
from jax import lax
from jax.sharding import PartitionSpec as P

EPS = 1e-06
THETA = 1000000.0
MASKED = -1e30


def norm_rows(value_rows, gain_vec):
    return (
        value_rows
        * lax.rsqrt(jnp.mean(value_rows * value_rows, axis=-1, keepdims=True) + EPS)
        * gain_vec
    )


def norm_back(value_rows, gain_vec, upstream):
    factor = lax.rsqrt(jnp.mean(value_rows * value_rows, axis=-1, keepdims=True) + EPS)
    normalized_input = value_rows * factor
    weighted = upstream * gain_vec
    inner_mean = jnp.mean(weighted * normalized_input, axis=-1, keepdims=True)
    return (factor * (weighted - normalized_input * inner_mean), upstream * normalized_input)


def rotary_tables(positions, head_dim):
    half_dim = head_dim // 2
    frequency = jnp.exp(
        jnp.arange(half_dim, dtype=jnp.float32) * (-2.0 * math.log(THETA) / head_dim)
    )
    angles = positions.astype(jnp.float32)[:, None] * frequency[None, :]
    angles = jnp.concatenate([angles, angles], axis=1)
    return (jnp.cos(angles)[:, None, :], jnp.sin(angles)[:, None, :])


def rotate(value_rows, cosine_table, sine_table):
    half_dim = value_rows.shape[-1] // 2
    turned = jnp.concatenate([-value_rows[..., half_dim:], value_rows[..., :half_dim]], axis=-1)
    return value_rows * cosine_table + turned * sine_table


def matmul(left_side, right_side):
    return jnp.dot(left_side, right_side, preferred_element_type=jnp.float32)


def contract_rows(left_side, right_side):
    return lax.dot_general(
        left_side, right_side, (((0,), (0,)), ((), ())), preferred_element_type=jnp.float32
    )


def contract_cols(left_side, right_side):
    return lax.dot_general(
        left_side, right_side, (((1,), (1,)), ((), ())), preferred_element_type=jnp.float32
    )


def sum_everywhere(vector):
    devices = lax.axis_size("ctx") * lax.axis_size("wt")
    spread = jnp.broadcast_to(vector[None, :], (devices, vector.shape[0]))
    return jnp.sum(
        lax.all_to_all(spread, ("ctx", "wt"), split_axis=0, concat_axis=0, tiled=True), axis=0
    )


def on_device(
    hidden_in,
    doc_lengths,
    routes,
    gain_attn,
    w_query,
    key_weight,
    value_weight,
    gain_query,
    gain_key,
    w_out,
    gain_moe,
    w_router,
    expert_gate,
    expert_up,
    expert_down,
    out_grad,
):
    block_rows = 512
    tokens = hidden_in.shape[1]
    model_width = hidden_in.shape[2]
    ctx_size = lax.axis_size("ctx")
    wt_size = lax.axis_size("wt")
    devices = ctx_size * wt_size
    seq_len = tokens * ctx_size
    head_dim = gain_query.shape[0]
    q_width = w_query.shape[1]
    kv_width = key_weight.shape[1]
    query_heads = q_width // head_dim
    key_heads = kv_width // head_dim
    group_width = query_heads // key_heads
    expert_count = w_router.shape[1]
    top_count = routes.shape[2]
    assert expert_gate.shape[0] == 1 and expert_count == devices
    send_slots = 2 * tokens * top_count // expert_count
    capacity = tokens * top_count // wt_size
    score_scale = head_dim ** (-0.5)
    ctx_index = lax.axis_index("ctx")
    both = ("ctx", "wt")
    by_stream = ("wt", "ctx")

    def gather(value, axes):
        return lax.all_gather(value, axes, axis=0, tiled=True)

    def exchange(value, axes):
        return lax.all_to_all(value, axes, split_axis=0, concat_axis=0, tiled=True)

    doc_ends = jnp.cumsum(doc_lengths[0])
    all_positions = jnp.arange(seq_len, dtype=jnp.int32)
    doc_all = jnp.sum((doc_ends[None, :] <= all_positions[:, None]).astype(jnp.int32), axis=1)
    first_pos = ctx_index * tokens
    my_positions = first_pos + jnp.arange(tokens, dtype=jnp.int32)
    my_docs = lax.dynamic_slice_in_dim(doc_all, first_pos, tokens)
    cosine_table, sine_table = rotary_tables(my_positions, head_dim)

    expert_ids = jnp.arange(expert_count, dtype=jnp.int32)
    hits = jnp.sum((routes[0][:, :, None] == expert_ids[None, None, :]).astype(jnp.int32), axis=1)
    local_rank = jnp.cumsum(hits, axis=0) - hits
    counts = lax.all_gather(jnp.sum(hits, axis=0), "ctx")
    earlier = jnp.arange(ctx_size, dtype=jnp.int32)[:, None] < ctx_index
    offsets = jnp.sum(jnp.where(earlier, counts, 0), axis=0)
    kept = (hits > 0) & (local_rank + offsets[None, :] < capacity)
    keep_float = kept.astype(jnp.float32)
    hits_float = hits.astype(jnp.float32)

    def to_owner_rows(table):
        return table.reshape(tokens, ctx_size, wt_size).transpose(2, 1, 0).reshape(devices, tokens)

    def from_owner_rows(table):
        return table.reshape(wt_size, ctx_size, tokens).transpose(2, 1, 0).reshape(tokens, devices)

    hit_mine = exchange(to_owner_rows(hits), by_stream).reshape(wt_size, seq_len)
    slot_mine = jnp.cumsum(hit_mine, axis=1) - hit_mine
    slot_mine = jnp.where((hit_mine > 0) & (slot_mine < capacity), slot_mine, -1)
    block_hits = jnp.sum(hit_mine.reshape(wt_size, ctx_size, tokens), axis=2)
    block_first = jnp.cumsum(block_hits, axis=1) - block_hits
    slot_ids = jnp.arange(capacity, dtype=jnp.int32)
    place = slot_mine[:, None, :] == slot_ids[None, :, None]
    place_low = place.astype(jnp.bfloat16)
    send_ids = jnp.arange(send_slots, dtype=jnp.int32)
    send_slot = jnp.where(
        send_ids[None, None, :] < block_hits[:, :, None],
        block_first[:, :, None] + send_ids[None, None, :],
        -1,
    ).reshape(wt_size, ctx_size * send_slots)
    send_low = (send_slot[:, :, None] == slot_ids[None, None, :]).astype(jnp.bfloat16)

    resid_in = hidden_in[0].astype(jnp.float32)
    normed_in = norm_rows(resid_in, gain_attn).astype(jnp.bfloat16)
    router_pad = -expert_count % head_dim
    side_weights = gather(
        jnp.concatenate(
            [key_weight, value_weight, jnp.pad(w_router, ((0, 0), (0, router_pad)))], axis=1
        ),
        both,
    )
    query_full = gather(w_query, both)
    key_full = side_weights[:, :kv_width]
    value_full = side_weights[:, kv_width : 2 * kv_width]
    router_full = side_weights[:, 2 * kv_width : 2 * kv_width + expert_count]
    key_sum = matmul(normed_in, key_full).reshape(tokens, key_heads, head_dim)
    value_low = matmul(normed_in, value_full).astype(jnp.bfloat16)
    key_low = (
        rotate(norm_rows(key_sum, gain_key), cosine_table, sine_table)
        .reshape(tokens, kv_width)
        .astype(jnp.bfloat16)
    )
    pairs_all = gather(jnp.concatenate([key_low, value_low], axis=1), "ctx")
    keys_all = pairs_all[:, :kv_width]
    values_all = pairs_all[:, kv_width:]
    query_sum = matmul(normed_in, query_full).reshape(tokens, query_heads, head_dim)
    query_low = (
        rotate(norm_rows(query_sum, gain_query), cosine_table, sine_table)
        .reshape(tokens, q_width)
        .astype(jnp.bfloat16)
    )
    out_full = gather(w_out, both)
    head_grouped = query_low.reshape(tokens, key_heads, group_width, head_dim)
    block_count = seq_len // block_rows

    def block_scores(block_index):
        key_begin = block_index * block_rows
        key_block = lax.dynamic_slice_in_dim(keys_all, key_begin, block_rows, 0).reshape(
            block_rows, key_heads, head_dim
        )
        value_block = lax.dynamic_slice_in_dim(values_all, key_begin, block_rows, 0).reshape(
            block_rows, key_heads, head_dim
        )
        scores = (
            jnp.einsum(
                "qkgd,skd->kgqs", head_grouped, key_block, preferred_element_type=jnp.float32
            )
            * score_scale
        )
        key_pos = key_begin + jnp.arange(block_rows, dtype=jnp.int32)
        key_doc = lax.dynamic_slice_in_dim(doc_all, key_begin, block_rows)
        allowed = (key_pos[None, :] <= my_positions[:, None]) & (
            key_doc[None, :] == my_docs[:, None]
        )
        return (jnp.where(allowed, scores, MASKED), allowed, key_block, value_block)

    def lse_step(running, block_index):
        row_peak, row_total = running
        scores, allowed, key_block, value_block = block_scores(block_index)
        new_peak = jnp.maximum(row_peak, jnp.max(scores, axis=-1))
        weights = jnp.where(allowed, jnp.exp(scores - new_peak[..., None]), 0.0)
        return (
            (new_peak, row_total * jnp.exp(row_peak - new_peak) + jnp.sum(weights, axis=-1)),
            None,
        )

    stat_shape = (key_heads, group_width, tokens)
    (row_peak, row_total), unused = lax.scan(
        lse_step,
        (jnp.full(stat_shape, MASKED, jnp.float32), jnp.zeros(stat_shape, jnp.float32)),
        jnp.arange(block_count),
    )
    log_total = row_peak + jnp.log(row_total)

    def mix_step(running, block_index):
        scores, allowed, key_block, value_block = block_scores(block_index)
        weights = jnp.where(allowed, jnp.exp(scores - log_total[..., None]), 0.0).astype(
            jnp.bfloat16
        )
        return (
            running
            + jnp.einsum(
                "kgqs,skd->qkgd", weights, value_block, preferred_element_type=jnp.float32
            ),
            None,
        )

    mixed, unused = lax.scan(
        mix_step,
        jnp.zeros((tokens, key_heads, group_width, head_dim), jnp.float32),
        jnp.arange(block_count),
    )
    mixed_low = mixed.reshape(tokens, q_width).astype(jnp.bfloat16)
    resid_mid = resid_in + matmul(mixed_low, out_full)
    normed_mid = norm_rows(resid_mid, gain_moe).astype(jnp.bfloat16)

    mid_all = gather(normed_mid, by_stream).reshape(wt_size, seq_len, model_width)
    cot_all = gather(out_grad[0], by_stream).reshape(wt_size, seq_len, model_width)
    logits = matmul(normed_mid, router_full)
    logit_exp = jnp.exp(logits - jnp.max(logits, axis=-1, keepdims=True))
    router_probs = logit_exp / jnp.sum(logit_exp, axis=-1, keepdims=True)
    chosen_total = jnp.sum(hits_float * router_probs, axis=1, keepdims=True)
    gate_kept = jnp.where(kept, router_probs / chosen_total, 0.0)
    gate_mine = exchange(to_owner_rows(gate_kept), by_stream).reshape(wt_size, seq_len)

    def pick_rows(table):
        return (
            jnp.einsum("wkt,wtd->wkd", place_low, table, preferred_element_type=jnp.float32)
            .astype(jnp.bfloat16)
            .reshape(wt_size * capacity, model_width)
        )

    filled = pick_rows(mid_all)
    gate_h = matmul(filled, expert_gate[0])
    up_h = matmul(filled, expert_up[0])
    sigma_h = jax.nn.sigmoid(gate_h)
    hidden_h = (gate_h * sigma_h * up_h).astype(jnp.bfloat16)
    result_rows = matmul(hidden_h, expert_down[0]).astype(jnp.bfloat16)
    cot_rows = pick_rows(cot_all)
    gate_rows = jnp.sum(jnp.where(place, gate_mine[:, None, :], 0.0), axis=2).reshape(-1)
    gate_cot_rows = jnp.sum(
        result_rows.astype(jnp.float32) * cot_rows.astype(jnp.float32), axis=1
    ).reshape(wt_size, capacity)
    gate_cot_mine = jnp.sum(jnp.where(place, gate_cot_rows[:, :, None], 0.0), axis=1)
    out_rows_cot = (gate_rows[:, None] * cot_rows.astype(jnp.float32)).astype(jnp.bfloat16)
    hidden_cot = contract_cols(out_rows_cot, expert_down[0])
    grad_down = contract_rows(hidden_h, out_rows_cot)
    gate_cot_h = (hidden_cot * up_h * sigma_h * (1.0 + gate_h * (1.0 - sigma_h))).astype(
        jnp.bfloat16
    )
    up_cot_h = (hidden_cot * gate_h * sigma_h).astype(jnp.bfloat16)
    grad_gate = contract_rows(filled, gate_cot_h)
    grad_up = contract_rows(filled, up_cot_h)
    in_rows_cot = (
        contract_cols(gate_cot_h, expert_gate[0]) + contract_cols(up_cot_h, expert_up[0])
    ).astype(jnp.bfloat16)

    def to_tokens(rows):
        sent = jnp.einsum(
            "wjk,wkd->wjd",
            send_low,
            rows.reshape(wt_size, capacity, model_width),
            preferred_element_type=jnp.float32,
        ).astype(jnp.bfloat16)
        return exchange(
            sent.reshape(devices, send_slots, model_width), by_stream
        ).reshape(devices * send_slots, model_width)

    gate_cot = from_owner_rows(exchange(gate_cot_mine.reshape(devices, tokens), by_stream))
    returned_cot = to_tokens(in_rows_cot)
    returned = to_tokens(result_rows)

    def by_source(table):
        return table.reshape(tokens, ctx_size, wt_size).transpose(0, 2, 1).reshape(tokens, devices)

    where_kept = by_source(jnp.where(kept, local_rank, -1))[:, :, None] == send_ids[None, None, :]
    take = where_kept.astype(jnp.bfloat16).reshape(tokens, devices * send_slots)
    gates_wide = jnp.where(where_kept, by_source(gate_kept)[:, :, None], 0.0).reshape(
        tokens, devices * send_slots
    )
    gates_high = lax.reduce_precision(gates_wide, 8, 7)
    gates_low = (gates_wide - gates_high).astype(jnp.bfloat16)
    hidden_out = (
        resid_mid + matmul(gates_high.astype(jnp.bfloat16), returned) + matmul(gates_low, returned)
    )
    out_cot = out_grad[0].astype(jnp.float32)

    kept_cot = gate_cot * keep_float
    chosen_cot = kept_cot / chosen_total - jnp.sum(
        kept_cot * router_probs, axis=1, keepdims=True
    ) / (chosen_total * chosen_total)
    probs_cot = hits_float * chosen_cot
    logit_cot = (
        router_probs * (probs_cot - jnp.sum(router_probs * probs_cot, axis=1, keepdims=True))
    ).astype(jnp.bfloat16)
    mid_cot = matmul(take, returned_cot) + contract_cols(logit_cot, router_full)
    mid_norm_cot, gain_moe_terms = norm_back(resid_mid, gain_moe, mid_cot)
    resid_cot = out_cot + mid_norm_cot
    attn_cot = resid_cot.astype(jnp.bfloat16)
    router_parts = exchange(
        contract_rows(normed_mid, logit_cot).reshape(devices, -1), both
    )
    grad_w_router = jnp.sum(router_parts, axis=0).reshape(w_router.shape)

    def column_blocks(value):
        width = value.shape[1] // ctx_size
        blocks = value.reshape(tokens, ctx_size, width).transpose(1, 0, 2)
        return exchange(blocks, "ctx").reshape(seq_len, width)

    mixed_cot = contract_cols(attn_cot, out_full)
    attn_cot_all = gather(attn_cot, "ctx")
    mixed_columns = column_blocks(mixed_low)
    grad_w_out = lax.psum_scatter(
        contract_rows(mixed_columns, attn_cot_all).astype(jnp.bfloat16),
        "wt",
        scatter_dimension=0,
        tiled=True,
    ).astype(jnp.float32)

    cot_grouped = mixed_cot.astype(jnp.bfloat16).reshape(tokens, key_heads, group_width, head_dim)
    row_delta = jnp.sum(cot_grouped.astype(jnp.float32) * mixed, axis=-1).transpose(1, 2, 0)

    def back_step(query_cot, block_index):
        scores, allowed, key_block, value_block = block_scores(block_index)
        weights = jnp.where(allowed, jnp.exp(scores - log_total[..., None]), 0.0)
        value_cot = jnp.einsum(
            "kgqs,qkgd->skd",
            weights.astype(jnp.bfloat16),
            cot_grouped,
            preferred_element_type=jnp.float32,
        )
        weight_cot = jnp.einsum(
            "qkgd,skd->kgqs", cot_grouped, value_block, preferred_element_type=jnp.float32
        )
        score_cot = (weights * (weight_cot - row_delta[..., None])).astype(jnp.bfloat16)
        query_cot = (
            query_cot
            + jnp.einsum("kgqs,skd->qkgd", score_cot, key_block, preferred_element_type=jnp.float32)
            * score_scale
        )
        key_cot = (
            jnp.einsum(
                "kgqs,qkgd->skd", score_cot, head_grouped, preferred_element_type=jnp.float32
            )
            * score_scale
        )
        return (
            query_cot,
            jnp.concatenate(
                [key_cot.reshape(block_rows, kv_width), value_cot.reshape(block_rows, kv_width)],
                axis=1,
            ).astype(jnp.bfloat16),
        )

    query_cot, pair_cots = lax.scan(
        back_step,
        jnp.zeros((tokens, key_heads, group_width, head_dim), jnp.float32),
        jnp.arange(block_count),
    )
    pair_mine = lax.psum_scatter(
        pair_cots.reshape(seq_len, 2 * kv_width), "ctx", scatter_dimension=0, tiled=True
    )
    key_mine = pair_mine[:, :kv_width].astype(jnp.float32)
    value_cot_low = pair_mine[:, kv_width:]
    query_pre, gain_query_terms = norm_back(
        query_sum,
        gain_query,
        rotate(query_cot.reshape(tokens, query_heads, head_dim), cosine_table, -sine_table),
    )
    key_pre, gain_key_terms = norm_back(
        key_sum,
        gain_key,
        rotate(key_mine.reshape(tokens, key_heads, head_dim), cosine_table, -sine_table),
    )
    query_cot_low = query_pre.reshape(tokens, q_width).astype(jnp.bfloat16)
    key_cot_low = key_pre.reshape(tokens, kv_width).astype(jnp.bfloat16)
    pair_cot_low = jnp.concatenate([key_cot_low, value_cot_low], axis=1)

    normed_in_all = gather(normed_in, "ctx")

    def weight_grad(cots):
        width = cots.shape[1] // ctx_size
        block = contract_rows(normed_in_all, column_blocks(cots)).astype(jnp.bfloat16)
        block = block.reshape(ctx_size, wt_size, -1, width).transpose(1, 0, 2, 3)
        mine = lax.psum_scatter(
            block.reshape(model_width, width), "wt", scatter_dimension=0, tiled=True
        )
        rows = exchange(mine.reshape(ctx_size, -1, width), "ctx")
        return rows.transpose(1, 0, 2).reshape(-1, width * ctx_size).astype(jnp.float32)

    grad_w_query = weight_grad(query_cot_low)
    grad_pair = weight_grad(pair_cot_low)
    grad_w_key = grad_pair[:, :kv_width]
    grad_w_value = grad_pair[:, kv_width:]
    in_cot = contract_cols(query_cot_low, query_full) + contract_cols(
        pair_cot_low, side_weights[:, : 2 * kv_width]
    )
    in_norm_cot, gain_attn_terms = norm_back(resid_in, gain_attn, in_cot)
    grad_in = resid_cot + in_norm_cot
    gains = sum_everywhere(
        jnp.concatenate(
            [
                jnp.sum(gain_attn_terms, axis=0),
                jnp.sum(gain_query_terms, axis=(0, 1)),
                jnp.sum(gain_key_terms, axis=(0, 1)),
                jnp.sum(gain_moe_terms, axis=0),
            ]
        )
    )
    grad_gain_attn = gains[:model_width]
    grad_gain_query = gains[model_width : model_width + head_dim]
    grad_gain_key = gains[model_width + head_dim : model_width + 2 * head_dim]
    grad_gain_moe = gains[model_width + 2 * head_dim :]
    return (
        hidden_out[None],
        grad_in[None],
        grad_gain_attn,
        grad_w_query,
        grad_w_key,
        grad_w_value,
        grad_gain_query,
        grad_gain_key,
        grad_w_out,
        grad_gain_moe,
        grad_w_router,
        grad_gate[None],
        grad_up[None],
        grad_down[None],
    )


def solution(mesh):
    in_specs = (
        P("wt", "ctx", None),
        P("wt", None),
        P("wt", "ctx", None),
        P(),
        P(("ctx", "wt"), None),
        P(("ctx", "wt"), None),
        P(("ctx", "wt"), None),
        P(),
        P(),
        P(("ctx", "wt"), None),
        P(),
        P(("ctx", "wt"), None),
        P(("ctx", "wt"), None, None),
        P(("ctx", "wt"), None, None),
        P(("ctx", "wt"), None, None),
        P("wt", "ctx", None),
    )
    out_specs = (
        P("wt", "ctx", None),
        P("wt", "ctx", None),
        P(),
        P(("ctx", "wt"), None),
        P(("ctx", "wt"), None),
        P(("ctx", "wt"), None),
        P(),
        P(),
        P(("ctx", "wt"), None),
        P(),
        P(("ctx", "wt"), None),
        P(("ctx", "wt"), None, None),
        P(("ctx", "wt"), None, None),
        P(("ctx", "wt"), None, None),
    )
    return jax.shard_map(
        on_device, mesh=mesh, in_specs=in_specs, out_specs=out_specs, check_vma=False
    )
```

```python
import functools
import math

import jax
import jax.numpy as jnp
from jax import lax
from jax.experimental import pallas as pl
from jax.experimental.pallas import tpu as pltpu
from jax.sharding import PartitionSpec as P


EPS = 1e-06
THETA = 1000000.0
MASKED = -1e30


def norm_rows(value_rows, gain_vec):
    return (
        value_rows
        * lax.rsqrt(jnp.mean(value_rows * value_rows, axis=-1, keepdims=True) + EPS)
        * gain_vec
    )


def norm_back(value_rows, gain_vec, upstream):
    factor = lax.rsqrt(jnp.mean(value_rows * value_rows, axis=-1, keepdims=True) + EPS)
    normalized_input = value_rows * factor
    weighted = upstream * gain_vec
    inner_mean = jnp.mean(weighted * normalized_input, axis=-1, keepdims=True)
    return (factor * (weighted - normalized_input * inner_mean), upstream * normalized_input)


def rotary_tables(positions, head_dim):
    half_dim = head_dim // 2
    frequency = jnp.exp(
        jnp.arange(half_dim, dtype=jnp.float32) * (-2.0 * math.log(THETA) / head_dim)
    )
    angles = positions.astype(jnp.float32)[:, None] * frequency[None, :]
    angles = jnp.concatenate([angles, angles], axis=1)
    return (jnp.cos(angles)[:, None, :], jnp.sin(angles)[:, None, :])


def rotate(value_rows, cosine_table, sine_table):
    half_dim = value_rows.shape[-1] // 2
    turned = jnp.concatenate([-value_rows[..., half_dim:], value_rows[..., :half_dim]], axis=-1)
    return value_rows * cosine_table + turned * sine_table


def matmul(left_side, right_side):
    return jnp.dot(left_side, right_side, preferred_element_type=jnp.float32)


def contract_rows(left_side, right_side):
    return lax.dot_general(
        left_side, right_side, (((0,), (0,)), ((), ())), preferred_element_type=jnp.float32
    )


def contract_cols(left_side, right_side):
    return lax.dot_general(
        left_side, right_side, (((1,), (1,)), ((), ())), preferred_element_type=jnp.float32
    )


def after(value, earlier):
    return lax.optimization_barrier((value, earlier))[0]


def stack_heads(block, first, head_dim, count):
    return jnp.concatenate(
        [block[:, (first + h) * head_dim : (first + h + 1) * head_dim] for h in range(count)],
        axis=0,
    )


def attend_kernel(
    head_dim,
    together,
    query_ref,
    pairs_ref,
    gain_ref,
    cosine_ref,
    sine_ref,
    query_pos_ref,
    query_doc_ref,
    key_pos_ref,
    key_doc_ref,
    mixed_ref,
    query_low_ref,
    bias_ref,
):
    tokens = query_ref.shape[0]
    heads = query_ref.shape[1] // head_dim
    scale = head_dim ** (-0.5)

    @pl.when(pl.program_id(0) == 0)
    def _():
        allowed = (key_pos_ref[...] <= query_pos_ref[...]) & (
            key_doc_ref[...] == query_doc_ref[...]
        )
        bias_ref[...] = jnp.where(allowed, 0.0, MASKED)

    keys = pairs_ref[:, :head_dim]
    values = pairs_ref[:, head_dim:]
    for first in range(0, heads, together):
        for h in range(first, first + together):
            columns = slice(h * head_dim, (h + 1) * head_dim)
            rows = query_ref[:, columns]
            rows = norm_rows(rows, gain_ref[...])
            turned = pltpu.roll(rows, head_dim // 2, axis=1)
            rows = rows * cosine_ref[...] + turned * sine_ref[...]
            query_low_ref[:, columns] = rows.astype(jnp.bfloat16)
        queries = stack_heads(query_low_ref, first, head_dim, together)
        scores = contract_cols(queries, keys) * scale
        scores = scores + jnp.concatenate([bias_ref[...]] * together, axis=0)
        weights = jnp.exp(scores - jnp.max(scores, axis=1, keepdims=True))
        weights = weights / jnp.sum(weights, axis=1, keepdims=True)
        mixed = matmul(weights.astype(jnp.bfloat16), values)
        for h in range(together):
            columns = slice((first + h) * head_dim, (first + h + 1) * head_dim)
            mixed_ref[:, columns] = mixed[h * tokens : (h + 1) * tokens].astype(jnp.bfloat16)


def attend_back_kernel(
    head_dim,
    together,
    query_ref,
    query_low_ref,
    cot_ref,
    pairs_ref,
    gain_ref,
    cosine_ref,
    sine_ref,
    query_pos_ref,
    query_doc_ref,
    key_pos_ref,
    key_doc_ref,
    query_cot_ref,
    pair_cot_ref,
    gain_cot_ref,
    bias_ref,
    key_sum_ref,
    value_sum_ref,
):
    tokens = query_ref.shape[0]
    heads = query_ref.shape[1] // head_dim
    scale = head_dim ** (-0.5)

    @pl.when(pl.program_id(0) == 0)
    def _():
        allowed = (key_pos_ref[...] <= query_pos_ref[...]) & (
            key_doc_ref[...] == query_doc_ref[...]
        )
        bias_ref[...] = jnp.where(allowed, 0.0, MASKED)

    keys = pairs_ref[:, :head_dim]
    values = pairs_ref[:, head_dim:]
    for first in range(0, heads, together):
        queries = stack_heads(query_low_ref, first, head_dim, together)
        cots = stack_heads(cot_ref, first, head_dim, together)
        scores = contract_cols(keys, queries) * scale
        scores = scores + jnp.concatenate([bias_ref[...]] * together, axis=1)
        weights = jnp.exp(scores - jnp.max(scores, axis=0, keepdims=True))
        weights = weights / jnp.sum(weights, axis=0, keepdims=True)
        weight_cot = contract_cols(values, cots)
        delta = jnp.sum(weights * weight_cot, axis=0, keepdims=True)
        score_cot = (weights * (weight_cot - delta)).astype(jnp.bfloat16)
        value_part = matmul(weights.astype(jnp.bfloat16), cots)
        key_part = matmul(score_cot, queries)
        if first:
            value_sum_ref[...] += value_part
            key_sum_ref[...] += key_part
        else:
            value_sum_ref[...] = value_part
            key_sum_ref[...] = key_part
        query_part = contract_rows(score_cot, keys) * scale
        for h in range(together):
            columns = slice((first + h) * head_dim, (first + h + 1) * head_dim)
            upstream = query_part[h * tokens : (h + 1) * tokens]
            turned = pltpu.roll(upstream, head_dim // 2, axis=1)
            upstream = upstream * cosine_ref[...] - turned * sine_ref[...]
            rows_cot, terms = norm_back(query_ref[:, columns], gain_ref[...], upstream)
            query_cot_ref[:, columns] = rows_cot.astype(jnp.bfloat16)
            gain_cot_ref[first + h : first + h + 1, :] = jnp.sum(terms, axis=0, keepdims=True)
    pair_cot_ref[:, :head_dim] = (key_sum_ref[...] * scale).astype(jnp.bfloat16)
    pair_cot_ref[:, head_dim:] = value_sum_ref[...].astype(jnp.bfloat16)


def attend(query_sum, pairs_all, gain, cosine, sine, query_pos, query_doc, key_pos, key_doc):
    tokens, q_width = query_sum.shape
    seq_len, pair_width = pairs_all.shape
    head_dim = gain.shape[0]
    key_heads = pair_width // (2 * head_dim)
    group = q_width // key_heads
    whole = lambda shape: pl.BlockSpec(shape, lambda g: (0, 0))
    flops = 4 * tokens * seq_len * q_width
    return pl.pallas_call(
        functools.partial(attend_kernel, head_dim, 2),
        grid=(key_heads,),
        in_specs=[
            pl.BlockSpec((tokens, group), lambda g: (0, g)),
            pl.BlockSpec((seq_len, 2 * head_dim), lambda g: (0, g)),
            whole((1, head_dim)),
            whole((tokens, head_dim)),
            whole((tokens, head_dim)),
            whole((tokens, 1)),
            whole((tokens, 1)),
            whole((1, seq_len)),
            whole((1, seq_len)),
        ],
        out_specs=[pl.BlockSpec((tokens, group), lambda g: (0, g))] * 2,
        out_shape=[jax.ShapeDtypeStruct((tokens, q_width), jnp.bfloat16)] * 2,
        scratch_shapes=[pltpu.VMEM((tokens, seq_len), jnp.float32)],
        compiler_params=pltpu.CompilerParams(vmem_limit_bytes=32 << 20),
        cost_estimate=pl.CostEstimate(
            flops=flops, bytes_accessed=8 * tokens * q_width, transcendentals=0
        ),
        name="attend",
    )(
        query_sum,
        pairs_all,
        gain[None, :],
        cosine,
        sine,
        query_pos[:, None],
        query_doc[:, None],
        key_pos[None, :],
        key_doc[None, :],
    )


def attend_back(
    query_sum,
    query_low,
    cots,
    pairs_all,
    gain,
    cosine,
    sine,
    query_pos,
    query_doc,
    key_pos,
    key_doc,
):
    tokens, q_width = query_sum.shape
    seq_len, pair_width = pairs_all.shape
    head_dim = gain.shape[0]
    key_heads = pair_width // (2 * head_dim)
    group = q_width // key_heads
    heads = group // head_dim
    whole = lambda shape: pl.BlockSpec(shape, lambda g: (0, 0))
    flops = 10 * tokens * seq_len * q_width
    return pl.pallas_call(
        functools.partial(attend_back_kernel, head_dim, 2),
        grid=(key_heads,),
        in_specs=[
            pl.BlockSpec((tokens, group), lambda g: (0, g)),
            pl.BlockSpec((tokens, group), lambda g: (0, g)),
            pl.BlockSpec((tokens, group), lambda g: (0, g)),
            pl.BlockSpec((seq_len, 2 * head_dim), lambda g: (0, g)),
            whole((1, head_dim)),
            whole((tokens, head_dim)),
            whole((tokens, head_dim)),
            whole((1, tokens)),
            whole((1, tokens)),
            whole((seq_len, 1)),
            whole((seq_len, 1)),
        ],
        out_specs=[
            pl.BlockSpec((tokens, group), lambda g: (0, g)),
            pl.BlockSpec((seq_len, 2 * head_dim), lambda g: (0, g)),
            pl.BlockSpec((heads, head_dim), lambda g: (g, 0)),
        ],
        out_shape=[
            jax.ShapeDtypeStruct((tokens, q_width), jnp.bfloat16),
            jax.ShapeDtypeStruct((seq_len, pair_width), jnp.bfloat16),
            jax.ShapeDtypeStruct((key_heads * heads, head_dim), jnp.float32),
        ],
        scratch_shapes=[
            pltpu.VMEM((seq_len, tokens), jnp.float32),
            pltpu.VMEM((seq_len, head_dim), jnp.float32),
            pltpu.VMEM((seq_len, head_dim), jnp.float32),
        ],
        compiler_params=pltpu.CompilerParams(vmem_limit_bytes=48 << 20),
        cost_estimate=pl.CostEstimate(
            flops=flops, bytes_accessed=12 * tokens * q_width, transcendentals=0
        ),
        name="attend_back",
    )(
        query_sum,
        query_low,
        cots,
        pairs_all,
        gain[None, :],
        cosine,
        sine,
        query_pos[None, :],
        query_doc[None, :],
        key_pos[:, None],
        key_doc[:, None],
    )


def sum_everywhere(vector):
    devices = lax.axis_size("ctx") * lax.axis_size("wt")
    spread = jnp.broadcast_to(vector[None, :], (devices, vector.shape[0]))
    return jnp.sum(
        lax.all_to_all(spread, ("ctx", "wt"), split_axis=0, concat_axis=0, tiled=True), axis=0
    )


def on_device(
    hidden_in,
    doc_lengths,
    routes,
    gain_attn,
    w_query,
    key_weight,
    value_weight,
    gain_query,
    gain_key,
    w_out,
    gain_moe,
    w_router,
    expert_gate,
    expert_up,
    expert_down,
    out_grad,
):
    tokens = hidden_in.shape[1]
    model_width = hidden_in.shape[2]
    ctx_size = lax.axis_size("ctx")
    wt_size = lax.axis_size("wt")
    devices = ctx_size * wt_size
    seq_len = tokens * ctx_size
    head_dim = gain_query.shape[0]
    kv_width = key_weight.shape[1]
    key_heads = kv_width // head_dim
    expert_count = w_router.shape[1]
    top_count = routes.shape[2]
    assert expert_gate.shape[0] == 1 and expert_count == devices
    capacity = tokens * top_count // wt_size
    ctx_index = lax.axis_index("ctx")
    wt_index = lax.axis_index("wt")
    both = ("ctx", "wt")
    by_stream = ("wt", "ctx")

    def gather(value, axes):
        return lax.all_gather(value, axes, axis=0, tiled=True)

    def exchange(value, axes):
        return lax.all_to_all(value, axes, split_axis=0, concat_axis=0, tiled=True)

    def scatter_sum(value, axes):
        return lax.psum_scatter(value, axes, scatter_dimension=0, tiled=True)

    doc_ends = jnp.cumsum(doc_lengths[0])
    all_positions = jnp.arange(seq_len, dtype=jnp.int32)
    doc_all = jnp.sum((doc_ends[None, :] <= all_positions[:, None]).astype(jnp.int32), axis=1)
    first_pos = ctx_index * tokens
    my_positions = first_pos + jnp.arange(tokens, dtype=jnp.int32)
    my_docs = lax.dynamic_slice_in_dim(doc_all, first_pos, tokens)
    cosine_table, sine_table = rotary_tables(my_positions, head_dim)
    cosine_rows = cosine_table[:, 0, :]
    first_half = jnp.arange(head_dim) < head_dim // 2
    sine_rows = jnp.where(first_half[None, :], -sine_table[:, 0, :], sine_table[:, 0, :])

    expert_ids = jnp.arange(expert_count, dtype=jnp.int32)
    hits = jnp.sum((routes[0][:, :, None] == expert_ids[None, None, :]).astype(jnp.int32), axis=1)
    local_rank = jnp.cumsum(hits, axis=0) - hits
    counts = lax.all_gather(jnp.sum(hits, axis=0), "ctx")
    earlier = jnp.arange(ctx_size, dtype=jnp.int32)[:, None] < ctx_index
    offsets = jnp.sum(jnp.where(earlier, counts, 0), axis=0)
    kept = (hits > 0) & (local_rank + offsets[None, :] < capacity)
    keep_float = kept.astype(jnp.float32)
    hits_float = hits.astype(jnp.float32)

    def to_owner_rows(table):
        return table.reshape(tokens, ctx_size, wt_size).transpose(2, 1, 0).reshape(devices, tokens)

    def from_owner_rows(table):
        return table.reshape(wt_size, ctx_size, tokens).transpose(2, 1, 0).reshape(tokens, devices)

    hit_mine = exchange(to_owner_rows(hits), by_stream).reshape(wt_size, seq_len)
    slot_mine = jnp.cumsum(hit_mine, axis=1) - hit_mine
    slot_mine = jnp.where((hit_mine > 0) & (slot_mine < capacity), slot_mine, -1)
    slot_ids = jnp.arange(capacity, dtype=jnp.int32)
    place = slot_mine[:, None, :] == slot_ids[None, :, None]
    place_low = place.astype(jnp.bfloat16)
    hit_plane = exchange(hits.T.reshape(ctx_size, wt_size, tokens), "ctx").transpose(1, 0, 2)
    hit_plane = hit_plane.reshape(wt_size, seq_len)[
        (wt_index - jnp.arange(wt_size)) % wt_size
    ]
    slot_plane = jnp.cumsum(hit_plane, axis=1) - hit_plane
    slot_plane = jnp.where((hit_plane > 0) & (slot_plane < capacity), slot_plane, -1)
    spread_low = (slot_plane[:, None, :] == slot_ids[None, :, None]).astype(jnp.bfloat16)

    resid_in = hidden_in[0].astype(jnp.float32)
    normed_in = norm_rows(resid_in, gain_attn).astype(jnp.bfloat16)
    router_pad = -expert_count % head_dim
    side_weights = gather(
        jnp.concatenate(
            [key_weight, value_weight, jnp.pad(w_router, ((0, 0), (0, router_pad)))], axis=1
        ),
        both,
    )
    query_full = gather(w_query, both)
    key_full = side_weights[:, :kv_width]
    value_full = side_weights[:, kv_width : 2 * kv_width]
    router_full = side_weights[:, 2 * kv_width : 2 * kv_width + expert_count]
    key_sum = matmul(normed_in, key_full).reshape(tokens, key_heads, head_dim)
    value_low = matmul(normed_in, value_full).astype(jnp.bfloat16)
    key_low = (
        rotate(norm_rows(key_sum, gain_key), cosine_table, sine_table)
        .reshape(tokens, kv_width)
        .astype(jnp.bfloat16)
    )

    def interleave(left, right):
        both_heads = jnp.stack(
            [side.reshape(-1, key_heads, head_dim) for side in (left, right)], axis=2
        )
        return both_heads.reshape(-1, 2 * kv_width)

    pairs_all = gather(interleave(key_low, value_low), "ctx")
    query_sum = lax.optimization_barrier(matmul(normed_in, query_full))
    out_full = gather(w_out, both)
    mixed_low, query_low = attend(
        query_sum,
        pairs_all,
        gain_query,
        cosine_rows,
        sine_rows,
        my_positions,
        my_docs,
        all_positions,
        doc_all,
    )
    resid_mid = resid_in + matmul(mixed_low, out_full)
    normed_mid = norm_rows(resid_mid, gain_moe).astype(jnp.bfloat16)

    mid_all = gather(normed_mid, by_stream).reshape(wt_size, seq_len, model_width)
    logits = matmul(normed_mid, router_full)
    logit_exp = jnp.exp(logits - jnp.max(logits, axis=-1, keepdims=True))
    router_probs = logit_exp / jnp.sum(logit_exp, axis=-1, keepdims=True)
    chosen_total = jnp.sum(hits_float * router_probs, axis=1, keepdims=True)
    gate_kept = jnp.where(kept, router_probs / chosen_total, 0.0)
    gate_mine = exchange(to_owner_rows(gate_kept), by_stream).reshape(wt_size, seq_len)

    def column_blocks(value):
        width = value.shape[1] // ctx_size
        blocks = value.reshape(tokens, ctx_size, width).transpose(1, 0, 2)
        return exchange(blocks, "ctx").reshape(seq_len, width)

    def pick_rows(table):
        return (
            jnp.einsum("wkt,wtd->wkd", place_low, table, preferred_element_type=jnp.float32)
            .astype(jnp.bfloat16)
            .reshape(wt_size * capacity, model_width)
        )

    filled = pick_rows(mid_all)
    gathered_bytes = 2 * devices * tokens * model_width
    own_cot = out_grad[0] if gathered_bytes <= 1 << 25 else after(out_grad[0], filled)
    cot_all = gather(own_cot, by_stream).reshape(wt_size, seq_len, model_width)
    normed_in_all = gather(after(normed_in, filled), "ctx")
    mixed_columns = column_blocks(after(mixed_low, filled))
    gate_h = matmul(filled, expert_gate[0])
    up_h = matmul(filled, expert_up[0])
    sigma_h = jax.nn.sigmoid(gate_h)
    hidden_h = (gate_h * sigma_h * up_h).astype(jnp.bfloat16)
    result_rows = matmul(hidden_h, expert_down[0]).astype(jnp.bfloat16)
    cot_rows = pick_rows(cot_all)
    gate_rows = jnp.sum(jnp.where(place, gate_mine[:, None, :], 0.0), axis=2).reshape(-1)
    gate_cot_rows = jnp.sum(
        result_rows.astype(jnp.float32) * cot_rows.astype(jnp.float32), axis=1
    ).reshape(wt_size, capacity)
    gate_cot_mine = jnp.sum(jnp.where(place, gate_cot_rows[:, :, None], 0.0), axis=1)
    out_rows_cot = (gate_rows[:, None] * cot_rows.astype(jnp.float32)).astype(jnp.bfloat16)
    hidden_cot = contract_cols(out_rows_cot, expert_down[0])
    grad_down = contract_rows(hidden_h, out_rows_cot)
    gate_cot_h = (hidden_cot * up_h * sigma_h * (1.0 + gate_h * (1.0 - sigma_h))).astype(
        jnp.bfloat16
    )
    up_cot_h = (hidden_cot * gate_h * sigma_h).astype(jnp.bfloat16)
    grad_gate = contract_rows(filled, gate_cot_h)
    grad_up = contract_rows(filled, up_cot_h)
    in_rows_cot = (
        contract_cols(gate_cot_h, expert_gate[0]) + contract_cols(up_cot_h, expert_up[0])
    ).astype(jnp.bfloat16)

    def turn(blocks):
        arrived = []
        for step in range(wt_size):
            block = lax.dynamic_index_in_dim(
                blocks, lax.rem(wt_index + step, wt_size), keepdims=False
            )
            if step:
                pairs = [(w, (w + step) % wt_size) for w in range(wt_size)]
                block = lax.ppermute(block, "wt", pairs)
            arrived.append(block)
        return arrived

    def add_pairs(table, stream_rows):
        partial = contract_rows(
            table.reshape(wt_size * capacity, seq_len), jnp.concatenate(stream_rows, axis=0)
        ).astype(jnp.bfloat16)
        return scatter_sum(partial, "ctx").astype(jnp.float32)

    gate_cot = from_owner_rows(exchange(gate_cot_mine.reshape(devices, tokens), by_stream))
    mixed_rows = (gate_rows[:, None] * result_rows.astype(jnp.float32)).astype(jnp.bfloat16)
    in_rows_cot, normed_in_all, mixed_columns = lax.optimization_barrier(
        (in_rows_cot, normed_in_all, mixed_columns)
    )
    blocks_shape = (wt_size, capacity, model_width)
    stream_cots = turn(in_rows_cot.reshape(blocks_shape))
    returned_cot = add_pairs(spread_low, stream_cots)
    stream_mixed = turn(after(mixed_rows, stream_cots).reshape(blocks_shape))
    out_cot = out_grad[0].astype(jnp.float32)

    kept_cot = gate_cot * keep_float
    chosen_cot = kept_cot / chosen_total - jnp.sum(
        kept_cot * router_probs, axis=1, keepdims=True
    ) / (chosen_total * chosen_total)
    probs_cot = hits_float * chosen_cot
    logit_cot = (
        router_probs * (probs_cot - jnp.sum(router_probs * probs_cot, axis=1, keepdims=True))
    ).astype(jnp.bfloat16)
    mid_cot = returned_cot + contract_cols(logit_cot, router_full)
    mid_norm_cot, gain_moe_terms = norm_back(resid_mid, gain_moe, mid_cot)
    resid_cot = out_cot + mid_norm_cot
    attn_cot = resid_cot.astype(jnp.bfloat16)
    router_parts = exchange(contract_rows(normed_mid, logit_cot).reshape(devices, -1), both)
    grad_w_router = jnp.sum(router_parts, axis=0).reshape(w_router.shape)

    mixed_cot = contract_cols(attn_cot, out_full)
    attn_cot_all = gather(attn_cot, "ctx")
    grad_w_out = scatter_sum(
        contract_rows(mixed_columns, attn_cot_all).astype(jnp.bfloat16), "wt"
    ).astype(jnp.float32)

    query_cot_low, pair_cots, gain_query_terms = attend_back(
        query_sum,
        query_low,
        mixed_cot.astype(jnp.bfloat16),
        pairs_all,
        gain_query,
        cosine_rows,
        sine_rows,
        my_positions,
        my_docs,
        all_positions,
        doc_all,
    )
    mixed_mine = add_pairs(after(spread_low, query_cot_low), stream_mixed)
    hidden_out = after(resid_mid, query_cot_low) + mixed_mine
    pair_mine = scatter_sum(pair_cots, "ctx").reshape(tokens, key_heads, 2, head_dim)
    key_mine = pair_mine[:, :, 0].astype(jnp.float32)
    value_cot_low = pair_mine[:, :, 1].reshape(tokens, kv_width)
    key_pre, gain_key_terms = norm_back(
        key_sum,
        gain_key,
        rotate(key_mine, cosine_table, -sine_table),
    )
    key_cot_low = key_pre.reshape(tokens, kv_width).astype(jnp.bfloat16)
    pair_cot_low = jnp.concatenate([key_cot_low, value_cot_low], axis=1)

    def weight_grad(cots):
        width = cots.shape[1] // ctx_size
        block = contract_rows(normed_in_all, column_blocks(cots)).astype(jnp.bfloat16)
        block = block.reshape(ctx_size, wt_size, -1, width).transpose(1, 0, 2, 3)
        mine = scatter_sum(block.reshape(model_width, width), "wt")
        rows = exchange(mine.reshape(ctx_size, -1, width), "ctx")
        return rows.transpose(1, 0, 2).reshape(-1, width * ctx_size).astype(jnp.float32)

    grad_w_query = weight_grad(query_cot_low)
    grad_pair = weight_grad(pair_cot_low)
    grad_w_key = grad_pair[:, :kv_width]
    grad_w_value = grad_pair[:, kv_width:]
    in_cot = contract_cols(query_cot_low, query_full) + contract_cols(
        pair_cot_low, side_weights[:, : 2 * kv_width]
    )
    in_norm_cot, gain_attn_terms = norm_back(resid_in, gain_attn, in_cot)
    grad_in = resid_cot + in_norm_cot
    gains = sum_everywhere(
        jnp.concatenate(
            [
                jnp.sum(gain_attn_terms, axis=0),
                jnp.sum(gain_query_terms, axis=0),
                jnp.sum(gain_key_terms, axis=(0, 1)),
                jnp.sum(gain_moe_terms, axis=0),
            ]
        )
    )
    grad_gain_attn = gains[:model_width]
    grad_gain_query = gains[model_width : model_width + head_dim]
    grad_gain_key = gains[model_width + head_dim : model_width + 2 * head_dim]
    grad_gain_moe = gains[model_width + 2 * head_dim :]
    return (
        hidden_out[None],
        grad_in[None],
        grad_gain_attn,
        grad_w_query,
        grad_w_key,
        grad_w_value,
        grad_gain_query,
        grad_gain_key,
        grad_w_out,
        grad_gain_moe,
        grad_w_router,
        grad_gate[None],
        grad_up[None],
        grad_down[None],
    )


def solution(mesh):
    in_specs = (
        P("wt", "ctx", None),
        P("wt", None),
        P("wt", "ctx", None),
        P(),
        P(("ctx", "wt"), None),
        P(("ctx", "wt"), None),
        P(("ctx", "wt"), None),
        P(),
        P(),
        P(("ctx", "wt"), None),
        P(),
        P(("ctx", "wt"), None),
        P(("ctx", "wt"), None, None),
        P(("ctx", "wt"), None, None),
        P(("ctx", "wt"), None, None),
        P("wt", "ctx", None),
    )
    out_specs = (
        P("wt", "ctx", None),
        P("wt", "ctx", None),
        P(),
        P(("ctx", "wt"), None),
        P(("ctx", "wt"), None),
        P(("ctx", "wt"), None),
        P(),
        P(),
        P(("ctx", "wt"), None),
        P(),
        P(("ctx", "wt"), None),
        P(("ctx", "wt"), None, None),
        P(("ctx", "wt"), None, None),
        P(("ctx", "wt"), None, None),
    )

    return jax.shard_map(
        on_device, mesh=mesh, in_specs=in_specs, out_specs=out_specs, check_vma=False
    )
```

```python
import functools
import math

import jax
import jax.numpy as jnp
from jax import lax
from jax.experimental import pallas as pl
from jax.experimental.pallas import tpu as pltpu
from jax.sharding import PartitionSpec as P


EPS = 1e-06
THETA = 1000000.0
MASKED = -1e30
MESH = pl.DeviceIdType.MESH


def norm_rows(value_rows, gain_vec):
    return (
        value_rows
        * lax.rsqrt(jnp.mean(value_rows * value_rows, axis=-1, keepdims=True) + EPS)
        * gain_vec
    )


def norm_back(value_rows, gain_vec, upstream):
    factor = lax.rsqrt(jnp.mean(value_rows * value_rows, axis=-1, keepdims=True) + EPS)
    normalized_input = value_rows * factor
    weighted = upstream * gain_vec
    inner_mean = jnp.mean(weighted * normalized_input, axis=-1, keepdims=True)
    return (factor * (weighted - normalized_input * inner_mean), upstream * normalized_input)


def rotary_tables(positions, head_dim):
    half_dim = head_dim // 2
    frequency = jnp.exp(
        jnp.arange(half_dim, dtype=jnp.float32) * (-2.0 * math.log(THETA) / head_dim)
    )
    angles = positions.astype(jnp.float32)[:, None] * frequency[None, :]
    angles = jnp.concatenate([angles, angles], axis=1)
    return (jnp.cos(angles)[:, None, :], jnp.sin(angles)[:, None, :])


def rotate(value_rows, cosine_table, sine_table):
    half_dim = value_rows.shape[-1] // 2
    turned = jnp.concatenate([-value_rows[..., half_dim:], value_rows[..., :half_dim]], axis=-1)
    return value_rows * cosine_table + turned * sine_table


def matmul(left_side, right_side):
    return jnp.dot(left_side, right_side, preferred_element_type=jnp.float32)


def contract_rows(left_side, right_side):
    return lax.dot_general(
        left_side, right_side, (((0,), (0,)), ((), ())), preferred_element_type=jnp.float32
    )


def contract_cols(left_side, right_side):
    return lax.dot_general(
        left_side, right_side, (((1,), (1,)), ((), ())), preferred_element_type=jnp.float32
    )


def spread_kernel(splits, streams_first, *refs):
    count = len(splits)
    ins, outs, stages = refs[:count], refs[count : 2 * count], refs[2 * count : 3 * count]
    send_sems, recv_sems, load_sems, store_sems = refs[3 * count :]
    ctx = lax.axis_index("ctx")
    z = lax.axis_index("wt")
    depth = lax.axis_size("wt")
    flip_y = ctx + 4 - 8 * (ctx // 4)
    step_x = 2 - 4 * ((ctx // 2) % 2)
    step_c = 1 - 2 * (ctx % 2)
    flip_x = ctx + step_x
    flip_xy = flip_y + step_x

    barrier = pltpu.get_barrier_semaphore()
    line = [lax.rem(z + d, depth) for d in range(1, depth)]
    for peer in line:
        pl.semaphore_signal(barrier, inc=1, device_id=(ctx, peer), device_id_type=MESH)
    for peer in (flip_x, flip_y, ctx + step_c):
        pl.semaphore_signal(barrier, inc=1, device_id=(peer, z), device_id_type=MESH)
    loads = []
    for k in range(count):
        loads.append(pltpu.make_async_copy(ins[k], stages[k], load_sems.at[k]))
        loads[k].start()
    pl.semaphore_wait(barrier, depth + 2)

    pieces = []
    for part in range(max(splits)):
        for k in range(count):
            if part < splits[k]:
                pieces.append((k, part))

    def group(k, owner, rows):
        view = outs[k]
        return view.at[:, owner, rows] if streams_first[k] else view.at[owner, :, rows]

    def block(k, rows):
        view = outs[k]
        return view.at[z, ctx, rows] if streams_first[k] else view.at[ctx, z, rows]

    def rows_of(k, part):
        size = ins[k].shape[0] // splits[k]
        return pl.ds(part * size, size)

    def send(number, slot, source, target, device):
        copy = pltpu.make_async_remote_copy(
            src_ref=source,
            dst_ref=target,
            send_sem=send_sems.at[number, slot],
            recv_sem=recv_sems.at[number, slot],
            device_id=device,
            device_id_type=MESH,
        )
        copy.start()
        return copy

    along = []
    for number, (k, part) in enumerate(pieces):
        rows = rows_of(k, part)
        along.append(
            [
                send(number, d, ins[k].at[rows], block(k, rows), (ctx, peer))
                for d, peer in enumerate(line)
            ]
        )
    stores = []
    for k in range(count):
        loads[k].wait()
        whole = pl.ds(0, ins[k].shape[0])
        stores.append(pltpu.make_async_copy(stages[k], block(k, whole), store_sems.at[k]))
        stores[k].start()
    for k in range(count):
        stores[k].wait()

    first_slot = depth - 1
    crossed, turned, shared = {}, {}, {}

    def owners(number):
        if number % 2:
            return flip_x, flip_y
        return flip_y, flip_x

    def cross(number):
        k, part = pieces[number]
        rows = rows_of(k, part)
        near, far = owners(number)
        for copy in along[number]:
            copy.wait_recv()
        mine = group(k, ctx, rows)
        crossed[number] = send(number, first_slot, mine, mine, (near, z))
        turned[number] = [send(number, first_slot + 1, mine, mine, (far, z))]
        shared[number] = [send(number, first_slot + 3, mine, mine, (ctx + step_c, z))]

    def turn_corner(number):
        k, part = pieces[number]
        rows = rows_of(k, part)
        near, far = owners(number)
        crossed[number].wait_recv()
        theirs = group(k, near, rows)
        turned[number].append(send(number, first_slot + 2, theirs, theirs, (far, z)))
        shared[number].append(send(number, first_slot + 4, theirs, theirs, (ctx + step_c, z)))

    def share(number):
        k, part = pieces[number]
        rows = rows_of(k, part)
        _, far = owners(number)
        for slot, (copy, owner) in enumerate(zip(turned[number], (far, flip_xy))):
            copy.wait_recv()
            theirs = group(k, owner, rows)
            shared[number].append(
                send(number, first_slot + 5 + slot, theirs, theirs, (ctx + step_c, z))
            )

    total = len(pieces)
    for step in range(total + 2):
        if step < total:
            cross(step)
        if 0 <= step - 1 < total:
            turn_corner(step - 1)
        if 0 <= step - 2 < total:
            share(step - 2)
    for number in range(total):
        for copy in shared[number]:
            copy.wait_recv()
        for copy in along[number] + [crossed[number]] + turned[number] + shared[number]:
            copy.wait_send()


def spread(values, splits, streams_first, channel):
    ctx_size, wt_size = lax.axis_size("ctx"), lax.axis_size("wt")
    total = sum(splits)
    heads = [(wt_size, ctx_size) if first else (ctx_size, wt_size) for first in streams_first]
    size = sum(value.size * value.dtype.itemsize for value in values)
    results = pl.pallas_call(
        functools.partial(spread_kernel, splits, streams_first),
        out_shape=[
            jax.ShapeDtypeStruct(head + value.shape, value.dtype)
            for head, value in zip(heads, values)
        ],
        in_specs=[pl.BlockSpec(memory_space=pl.ANY)] * len(values),
        out_specs=[pl.BlockSpec(memory_space=pl.ANY)] * len(values),
        scratch_shapes=[pltpu.VMEM(value.shape, value.dtype) for value in values]
        + [
            pltpu.SemaphoreType.DMA((total, wt_size + 6)),
            pltpu.SemaphoreType.DMA((total, wt_size + 6)),
            pltpu.SemaphoreType.DMA((len(values),)),
            pltpu.SemaphoreType.DMA((len(values),)),
        ],
        compiler_params=pltpu.CompilerParams(collective_id=channel, has_side_effects=True),
        cost_estimate=pl.CostEstimate(
            flops=0, bytes_accessed=2 * ctx_size * wt_size * size, transcendentals=0
        ),
    )(*values)
    return [result.reshape(-1, result.shape[-1]) for result in results]


def after(value, earlier):
    return lax.optimization_barrier((value, earlier))[0]


def stack_heads(block, first, head_dim, count):
    return jnp.concatenate(
        [block[:, (first + h) * head_dim : (first + h + 1) * head_dim] for h in range(count)],
        axis=0,
    )


def attend_kernel(
    head_dim,
    together,
    query_ref,
    pairs_ref,
    gain_ref,
    cosine_ref,
    sine_ref,
    query_pos_ref,
    query_doc_ref,
    key_pos_ref,
    key_doc_ref,
    mixed_ref,
    query_low_ref,
    bias_ref,
):
    tokens = query_ref.shape[0]
    heads = query_ref.shape[1] // head_dim
    scale = head_dim ** (-0.5)

    @pl.when(pl.program_id(0) == 0)
    def _():
        allowed = (key_pos_ref[...] <= query_pos_ref[...]) & (
            key_doc_ref[...] == query_doc_ref[...]
        )
        bias_ref[...] = jnp.where(allowed, 0.0, MASKED)

    keys = pairs_ref[:, :head_dim]
    values = pairs_ref[:, head_dim:]
    for first in range(0, heads, together):
        for h in range(first, first + together):
            columns = slice(h * head_dim, (h + 1) * head_dim)
            rows = query_ref[:, columns]
            rows = norm_rows(rows, gain_ref[...])
            turned = pltpu.roll(rows, head_dim // 2, axis=1)
            rows = rows * cosine_ref[...] + turned * sine_ref[...]
            query_low_ref[:, columns] = rows.astype(jnp.bfloat16)
        queries = stack_heads(query_low_ref, first, head_dim, together)
        scores = contract_cols(queries, keys) * scale
        scores = scores + jnp.concatenate([bias_ref[...]] * together, axis=0)
        weights = jnp.exp(scores - jnp.max(scores, axis=1, keepdims=True))
        weights = weights / jnp.sum(weights, axis=1, keepdims=True)
        mixed = matmul(weights.astype(jnp.bfloat16), values)
        for h in range(together):
            columns = slice((first + h) * head_dim, (first + h + 1) * head_dim)
            mixed_ref[:, columns] = mixed[h * tokens : (h + 1) * tokens].astype(jnp.bfloat16)


def attend_back_kernel(
    head_dim,
    together,
    query_ref,
    query_low_ref,
    cot_ref,
    pairs_ref,
    gain_ref,
    cosine_ref,
    sine_ref,
    query_pos_ref,
    query_doc_ref,
    key_pos_ref,
    key_doc_ref,
    query_cot_ref,
    pair_cot_ref,
    gain_cot_ref,
    bias_ref,
    key_sum_ref,
    value_sum_ref,
):
    tokens = query_ref.shape[0]
    heads = query_ref.shape[1] // head_dim
    scale = head_dim ** (-0.5)

    @pl.when(pl.program_id(0) == 0)
    def _():
        allowed = (key_pos_ref[...] <= query_pos_ref[...]) & (
            key_doc_ref[...] == query_doc_ref[...]
        )
        bias_ref[...] = jnp.where(allowed, 0.0, MASKED)

    keys = pairs_ref[:, :head_dim]
    values = pairs_ref[:, head_dim:]
    for first in range(0, heads, together):
        queries = stack_heads(query_low_ref, first, head_dim, together)
        cots = stack_heads(cot_ref, first, head_dim, together)
        scores = contract_cols(keys, queries) * scale
        scores = scores + jnp.concatenate([bias_ref[...]] * together, axis=1)
        weights = jnp.exp(scores - jnp.max(scores, axis=0, keepdims=True))
        weights = weights / jnp.sum(weights, axis=0, keepdims=True)
        weight_cot = contract_cols(values, cots)
        delta = jnp.sum(weights * weight_cot, axis=0, keepdims=True)
        score_cot = (weights * (weight_cot - delta)).astype(jnp.bfloat16)
        value_part = matmul(weights.astype(jnp.bfloat16), cots)
        key_part = matmul(score_cot, queries)
        if first:
            value_sum_ref[...] += value_part
            key_sum_ref[...] += key_part
        else:
            value_sum_ref[...] = value_part
            key_sum_ref[...] = key_part
        query_part = contract_rows(score_cot, keys) * scale
        for h in range(together):
            columns = slice((first + h) * head_dim, (first + h + 1) * head_dim)
            upstream = query_part[h * tokens : (h + 1) * tokens]
            turned = pltpu.roll(upstream, head_dim // 2, axis=1)
            upstream = upstream * cosine_ref[...] - turned * sine_ref[...]
            rows_cot, terms = norm_back(query_ref[:, columns], gain_ref[...], upstream)
            query_cot_ref[:, columns] = rows_cot.astype(jnp.bfloat16)
            gain_cot_ref[first + h : first + h + 1, :] = jnp.sum(terms, axis=0, keepdims=True)
    pair_cot_ref[:, :head_dim] = (key_sum_ref[...] * scale).astype(jnp.bfloat16)
    pair_cot_ref[:, head_dim:] = value_sum_ref[...].astype(jnp.bfloat16)


def attend(query_sum, pairs_all, gain, cosine, sine, query_pos, query_doc, key_pos, key_doc):
    tokens, q_width = query_sum.shape
    seq_len, pair_width = pairs_all.shape
    head_dim = gain.shape[0]
    key_heads = pair_width // (2 * head_dim)
    group = q_width // key_heads
    whole = lambda shape: pl.BlockSpec(shape, lambda g: (0, 0))
    flops = 4 * tokens * seq_len * q_width
    return pl.pallas_call(
        functools.partial(attend_kernel, head_dim, 2),
        grid=(key_heads,),
        in_specs=[
            pl.BlockSpec((tokens, group), lambda g: (0, g)),
            pl.BlockSpec((seq_len, 2 * head_dim), lambda g: (0, g)),
            whole((1, head_dim)),
            whole((tokens, head_dim)),
            whole((tokens, head_dim)),
            whole((tokens, 1)),
            whole((tokens, 1)),
            whole((1, seq_len)),
            whole((1, seq_len)),
        ],
        out_specs=[pl.BlockSpec((tokens, group), lambda g: (0, g))] * 2,
        out_shape=[jax.ShapeDtypeStruct((tokens, q_width), jnp.bfloat16)] * 2,
        scratch_shapes=[pltpu.VMEM((tokens, seq_len), jnp.float32)],
        compiler_params=pltpu.CompilerParams(vmem_limit_bytes=32 << 20),
        cost_estimate=pl.CostEstimate(
            flops=flops, bytes_accessed=8 * tokens * q_width, transcendentals=0
        ),
        name="attend",
    )(
        query_sum,
        pairs_all,
        gain[None, :],
        cosine,
        sine,
        query_pos[:, None],
        query_doc[:, None],
        key_pos[None, :],
        key_doc[None, :],
    )


def attend_back(
    query_sum,
    query_low,
    cots,
    pairs_all,
    gain,
    cosine,
    sine,
    query_pos,
    query_doc,
    key_pos,
    key_doc,
):
    tokens, q_width = query_sum.shape
    seq_len, pair_width = pairs_all.shape
    head_dim = gain.shape[0]
    key_heads = pair_width // (2 * head_dim)
    group = q_width // key_heads
    heads = group // head_dim
    whole = lambda shape: pl.BlockSpec(shape, lambda g: (0, 0))
    flops = 10 * tokens * seq_len * q_width
    return pl.pallas_call(
        functools.partial(attend_back_kernel, head_dim, 2),
        grid=(key_heads,),
        in_specs=[
            pl.BlockSpec((tokens, group), lambda g: (0, g)),
            pl.BlockSpec((tokens, group), lambda g: (0, g)),
            pl.BlockSpec((tokens, group), lambda g: (0, g)),
            pl.BlockSpec((seq_len, 2 * head_dim), lambda g: (0, g)),
            whole((1, head_dim)),
            whole((tokens, head_dim)),
            whole((tokens, head_dim)),
            whole((1, tokens)),
            whole((1, tokens)),
            whole((seq_len, 1)),
            whole((seq_len, 1)),
        ],
        out_specs=[
            pl.BlockSpec((tokens, group), lambda g: (0, g)),
            pl.BlockSpec((seq_len, 2 * head_dim), lambda g: (0, g)),
            pl.BlockSpec((heads, head_dim), lambda g: (g, 0)),
        ],
        out_shape=[
            jax.ShapeDtypeStruct((tokens, q_width), jnp.bfloat16),
            jax.ShapeDtypeStruct((seq_len, pair_width), jnp.bfloat16),
            jax.ShapeDtypeStruct((key_heads * heads, head_dim), jnp.float32),
        ],
        scratch_shapes=[
            pltpu.VMEM((seq_len, tokens), jnp.float32),
            pltpu.VMEM((seq_len, head_dim), jnp.float32),
            pltpu.VMEM((seq_len, head_dim), jnp.float32),
        ],
        compiler_params=pltpu.CompilerParams(vmem_limit_bytes=48 << 20),
        cost_estimate=pl.CostEstimate(
            flops=flops, bytes_accessed=12 * tokens * q_width, transcendentals=0
        ),
        name="attend_back",
    )(
        query_sum,
        query_low,
        cots,
        pairs_all,
        gain[None, :],
        cosine,
        sine,
        query_pos[None, :],
        query_doc[None, :],
        key_pos[:, None],
        key_doc[:, None],
    )


def sum_everywhere(vector):
    devices = lax.axis_size("ctx") * lax.axis_size("wt")
    spread = jnp.broadcast_to(vector[None, :], (devices, vector.shape[0]))
    return jnp.sum(
        lax.all_to_all(spread, ("ctx", "wt"), split_axis=0, concat_axis=0, tiled=True), axis=0
    )


def on_device(
    hidden_in,
    doc_lengths,
    routes,
    gain_attn,
    w_query,
    key_weight,
    value_weight,
    gain_query,
    gain_key,
    w_out,
    gain_moe,
    w_router,
    expert_gate,
    expert_up,
    expert_down,
    out_grad,
):
    tokens = hidden_in.shape[1]
    model_width = hidden_in.shape[2]
    ctx_size = lax.axis_size("ctx")
    wt_size = lax.axis_size("wt")
    devices = ctx_size * wt_size
    seq_len = tokens * ctx_size
    head_dim = gain_query.shape[0]
    kv_width = key_weight.shape[1]
    key_heads = kv_width // head_dim
    expert_count = w_router.shape[1]
    top_count = routes.shape[2]
    assert expert_gate.shape[0] == 1 and expert_count == devices
    capacity = tokens * top_count // wt_size
    ctx_index = lax.axis_index("ctx")
    wt_index = lax.axis_index("wt")
    both = ("ctx", "wt")
    by_stream = ("wt", "ctx")

    def gather(value, axes):
        return lax.all_gather(value, axes, axis=0, tiled=True)

    def exchange(value, axes):
        return lax.all_to_all(value, axes, split_axis=0, concat_axis=0, tiled=True)

    def scatter_sum(value, axes):
        return lax.psum_scatter(value, axes, scatter_dimension=0, tiled=True)

    doc_ends = jnp.cumsum(doc_lengths[0])
    all_positions = jnp.arange(seq_len, dtype=jnp.int32)
    doc_all = jnp.sum((doc_ends[None, :] <= all_positions[:, None]).astype(jnp.int32), axis=1)
    first_pos = ctx_index * tokens
    my_positions = first_pos + jnp.arange(tokens, dtype=jnp.int32)
    my_docs = lax.dynamic_slice_in_dim(doc_all, first_pos, tokens)
    cosine_table, sine_table = rotary_tables(my_positions, head_dim)
    cosine_rows = cosine_table[:, 0, :]
    first_half = jnp.arange(head_dim) < head_dim // 2
    sine_rows = jnp.where(first_half[None, :], -sine_table[:, 0, :], sine_table[:, 0, :])

    expert_ids = jnp.arange(expert_count, dtype=jnp.int32)
    hits = jnp.sum((routes[0][:, :, None] == expert_ids[None, None, :]).astype(jnp.int32), axis=1)
    local_rank = jnp.cumsum(hits, axis=0) - hits
    counts = lax.all_gather(jnp.sum(hits, axis=0), "ctx")
    earlier = jnp.arange(ctx_size, dtype=jnp.int32)[:, None] < ctx_index
    offsets = jnp.sum(jnp.where(earlier, counts, 0), axis=0)
    kept = (hits > 0) & (local_rank + offsets[None, :] < capacity)
    keep_float = kept.astype(jnp.float32)
    hits_float = hits.astype(jnp.float32)

    def to_owner_rows(table):
        return table.reshape(tokens, ctx_size, wt_size).transpose(2, 1, 0).reshape(devices, tokens)

    def from_owner_rows(table):
        return table.reshape(wt_size, ctx_size, tokens).transpose(2, 1, 0).reshape(tokens, devices)

    hit_mine = exchange(to_owner_rows(hits), by_stream).reshape(wt_size, seq_len)
    slot_mine = jnp.cumsum(hit_mine, axis=1) - hit_mine
    slot_mine = jnp.where((hit_mine > 0) & (slot_mine < capacity), slot_mine, -1)
    slot_ids = jnp.arange(capacity, dtype=jnp.int32)
    place = slot_mine[:, None, :] == slot_ids[None, :, None]
    place_low = place.astype(jnp.bfloat16)
    hit_plane = exchange(hits.T.reshape(ctx_size, wt_size, tokens), "ctx").transpose(1, 0, 2)
    hit_plane = hit_plane.reshape(wt_size, seq_len)[
        (wt_index - jnp.arange(wt_size)) % wt_size
    ]
    slot_plane = jnp.cumsum(hit_plane, axis=1) - hit_plane
    slot_plane = jnp.where((hit_plane > 0) & (slot_plane < capacity), slot_plane, -1)
    spread_low = (slot_plane[:, None, :] == slot_ids[None, :, None]).astype(jnp.bfloat16)

    resid_in = hidden_in[0].astype(jnp.float32)
    normed_in = norm_rows(resid_in, gain_attn).astype(jnp.bfloat16)
    router_pad = -expert_count % head_dim
    side_mine = jnp.concatenate(
        [key_weight, value_weight, jnp.pad(w_router, ((0, 0), (0, router_pad)))], axis=1
    )
    small_plane = ctx_size == 8
    if small_plane:
        side_weights, query_full, out_full = spread(
            [side_mine, w_query, w_out], (2, 4, 4), (False,) * 3, 1
        )
    else:
        side_weights = gather(side_mine, both)
        query_full = gather(w_query, both)
        out_full = gather(w_out, both)
    key_full = side_weights[:, :kv_width]
    value_full = side_weights[:, kv_width : 2 * kv_width]
    router_full = side_weights[:, 2 * kv_width : 2 * kv_width + expert_count]
    key_sum = matmul(normed_in, key_full).reshape(tokens, key_heads, head_dim)
    value_low = matmul(normed_in, value_full).astype(jnp.bfloat16)
    key_low = (
        rotate(norm_rows(key_sum, gain_key), cosine_table, sine_table)
        .reshape(tokens, kv_width)
        .astype(jnp.bfloat16)
    )

    def interleave(left, right):
        both_heads = jnp.stack(
            [side.reshape(-1, key_heads, head_dim) for side in (left, right)], axis=2
        )
        return both_heads.reshape(-1, 2 * kv_width)

    pairs_all = gather(interleave(key_low, value_low), "ctx")
    if small_plane:
        cot_all = gather(after(out_grad[0], pairs_all), by_stream)
    query_sum = lax.optimization_barrier(matmul(normed_in, query_full))
    mixed_low, query_low = attend(
        query_sum,
        pairs_all,
        gain_query,
        cosine_rows,
        sine_rows,
        my_positions,
        my_docs,
        all_positions,
        doc_all,
    )
    resid_mid = resid_in + matmul(mixed_low, out_full)
    normed_mid = norm_rows(resid_mid, gain_moe).astype(jnp.bfloat16)

    if small_plane:
        (mid_all,) = spread([normed_mid], (4,), (True,), 2)
    else:
        mid_all = gather(normed_mid, by_stream)
    mid_all = mid_all.reshape(wt_size, seq_len, model_width)
    logits = matmul(normed_mid, router_full)
    logit_exp = jnp.exp(logits - jnp.max(logits, axis=-1, keepdims=True))
    router_probs = logit_exp / jnp.sum(logit_exp, axis=-1, keepdims=True)
    chosen_total = jnp.sum(hits_float * router_probs, axis=1, keepdims=True)
    gate_kept = jnp.where(kept, router_probs / chosen_total, 0.0)
    gate_mine = exchange(to_owner_rows(gate_kept), by_stream).reshape(wt_size, seq_len)

    def column_blocks(value):
        width = value.shape[1] // ctx_size
        blocks = value.reshape(tokens, ctx_size, width).transpose(1, 0, 2)
        return exchange(blocks, "ctx").reshape(seq_len, width)

    def pick_rows(table):
        return (
            jnp.einsum("wkt,wtd->wkd", place_low, table, preferred_element_type=jnp.float32)
            .astype(jnp.bfloat16)
            .reshape(wt_size * capacity, model_width)
        )

    filled = pick_rows(mid_all)
    if not small_plane:
        cot_all = gather(after(out_grad[0], filled), by_stream)
    cot_all = cot_all.reshape(wt_size, seq_len, model_width)
    normed_in_all = gather(after(normed_in, filled), "ctx")
    mixed_columns = column_blocks(after(mixed_low, filled))
    gate_h = matmul(filled, expert_gate[0])
    up_h = matmul(filled, expert_up[0])
    sigma_h = jax.nn.sigmoid(gate_h)
    hidden_h = (gate_h * sigma_h * up_h).astype(jnp.bfloat16)
    result_rows = matmul(hidden_h, expert_down[0]).astype(jnp.bfloat16)
    cot_rows = pick_rows(cot_all)
    gate_rows = jnp.sum(jnp.where(place, gate_mine[:, None, :], 0.0), axis=2).reshape(-1)
    gate_cot_rows = jnp.sum(
        result_rows.astype(jnp.float32) * cot_rows.astype(jnp.float32), axis=1
    ).reshape(wt_size, capacity)
    gate_cot_mine = jnp.sum(jnp.where(place, gate_cot_rows[:, :, None], 0.0), axis=1)
    out_rows_cot = (gate_rows[:, None] * cot_rows.astype(jnp.float32)).astype(jnp.bfloat16)
    hidden_cot = contract_cols(out_rows_cot, expert_down[0])
    grad_down = contract_rows(hidden_h, out_rows_cot)
    gate_cot_h = (hidden_cot * up_h * sigma_h * (1.0 + gate_h * (1.0 - sigma_h))).astype(
        jnp.bfloat16
    )
    up_cot_h = (hidden_cot * gate_h * sigma_h).astype(jnp.bfloat16)
    grad_gate = contract_rows(filled, gate_cot_h)
    grad_up = contract_rows(filled, up_cot_h)
    in_rows_cot = (
        contract_cols(gate_cot_h, expert_gate[0]) + contract_cols(up_cot_h, expert_up[0])
    ).astype(jnp.bfloat16)

    def turn(blocks):
        arrived = []
        for step in range(wt_size):
            block = lax.dynamic_index_in_dim(
                blocks, lax.rem(wt_index + step, wt_size), keepdims=False
            )
            if step:
                pairs = [(w, (w + step) % wt_size) for w in range(wt_size)]
                block = lax.ppermute(block, "wt", pairs)
            arrived.append(block)
        return arrived

    def add_pairs(table, stream_rows):
        partial = contract_rows(
            table.reshape(wt_size * capacity, seq_len), jnp.concatenate(stream_rows, axis=0)
        ).astype(jnp.bfloat16)
        return scatter_sum(partial, "ctx").astype(jnp.float32)

    gate_cot = from_owner_rows(exchange(gate_cot_mine.reshape(devices, tokens), by_stream))
    mixed_rows = (gate_rows[:, None] * result_rows.astype(jnp.float32)).astype(jnp.bfloat16)
    in_rows_cot, normed_in_all, mixed_columns = lax.optimization_barrier(
        (in_rows_cot, normed_in_all, mixed_columns)
    )
    blocks_shape = (wt_size, capacity, model_width)
    stream_cots = turn(in_rows_cot.reshape(blocks_shape))
    returned_cot = add_pairs(spread_low, stream_cots)
    stream_mixed = turn(after(mixed_rows, stream_cots).reshape(blocks_shape))
    out_cot = out_grad[0].astype(jnp.float32)

    kept_cot = gate_cot * keep_float
    chosen_cot = kept_cot / chosen_total - jnp.sum(
        kept_cot * router_probs, axis=1, keepdims=True
    ) / (chosen_total * chosen_total)
    probs_cot = hits_float * chosen_cot
    logit_cot = (
        router_probs * (probs_cot - jnp.sum(router_probs * probs_cot, axis=1, keepdims=True))
    ).astype(jnp.bfloat16)
    mid_cot = returned_cot + contract_cols(logit_cot, router_full)
    mid_norm_cot, gain_moe_terms = norm_back(resid_mid, gain_moe, mid_cot)
    resid_cot = out_cot + mid_norm_cot
    attn_cot = resid_cot.astype(jnp.bfloat16)
    router_parts = exchange(contract_rows(normed_mid, logit_cot).reshape(devices, -1), both)
    grad_w_router = jnp.sum(router_parts, axis=0).reshape(w_router.shape)

    mixed_cot = contract_cols(attn_cot, out_full)
    attn_cot_all = gather(attn_cot, "ctx")
    grad_w_out = scatter_sum(
        contract_rows(mixed_columns, attn_cot_all).astype(jnp.bfloat16), "wt"
    ).astype(jnp.float32)

    query_cot_low, pair_cots, gain_query_terms = attend_back(
        query_sum,
        query_low,
        mixed_cot.astype(jnp.bfloat16),
        pairs_all,
        gain_query,
        cosine_rows,
        sine_rows,
        my_positions,
        my_docs,
        all_positions,
        doc_all,
    )
    mixed_mine = add_pairs(after(spread_low, query_cot_low), stream_mixed)
    hidden_out = after(resid_mid, query_cot_low) + mixed_mine
    pair_mine = scatter_sum(pair_cots, "ctx").reshape(tokens, key_heads, 2, head_dim)
    key_mine = pair_mine[:, :, 0].astype(jnp.float32)
    value_cot_low = pair_mine[:, :, 1].reshape(tokens, kv_width)
    key_pre, gain_key_terms = norm_back(
        key_sum,
        gain_key,
        rotate(key_mine, cosine_table, -sine_table),
    )
    key_cot_low = key_pre.reshape(tokens, kv_width).astype(jnp.bfloat16)
    pair_cot_low = jnp.concatenate([key_cot_low, value_cot_low], axis=1)

    def weight_grad(cots):
        width = cots.shape[1] // ctx_size
        block = contract_rows(normed_in_all, column_blocks(cots)).astype(jnp.bfloat16)
        block = block.reshape(ctx_size, wt_size, -1, width).transpose(1, 0, 2, 3)
        mine = scatter_sum(block.reshape(model_width, width), "wt")
        rows = exchange(mine.reshape(ctx_size, -1, width), "ctx")
        return rows.transpose(1, 0, 2).reshape(-1, width * ctx_size).astype(jnp.float32)

    grad_w_query = weight_grad(query_cot_low)
    grad_pair = weight_grad(pair_cot_low)
    grad_w_key = grad_pair[:, :kv_width]
    grad_w_value = grad_pair[:, kv_width:]
    in_cot = contract_cols(query_cot_low, query_full) + contract_cols(
        pair_cot_low, side_weights[:, : 2 * kv_width]
    )
    in_norm_cot, gain_attn_terms = norm_back(resid_in, gain_attn, in_cot)
    grad_in = resid_cot + in_norm_cot
    gains = sum_everywhere(
        jnp.concatenate(
            [
                jnp.sum(gain_attn_terms, axis=0),
                jnp.sum(gain_query_terms, axis=0),
                jnp.sum(gain_key_terms, axis=(0, 1)),
                jnp.sum(gain_moe_terms, axis=0),
            ]
        )
    )
    grad_gain_attn = gains[:model_width]
    grad_gain_query = gains[model_width : model_width + head_dim]
    grad_gain_key = gains[model_width + head_dim : model_width + 2 * head_dim]
    grad_gain_moe = gains[model_width + 2 * head_dim :]
    return (
        hidden_out[None],
        grad_in[None],
        grad_gain_attn,
        grad_w_query,
        grad_w_key,
        grad_w_value,
        grad_gain_query,
        grad_gain_key,
        grad_w_out,
        grad_gain_moe,
        grad_w_router,
        grad_gate[None],
        grad_up[None],
        grad_down[None],
    )


def solution(mesh):
    in_specs = (
        P("wt", "ctx", None),
        P("wt", None),
        P("wt", "ctx", None),
        P(),
        P(("ctx", "wt"), None),
        P(("ctx", "wt"), None),
        P(("ctx", "wt"), None),
        P(),
        P(),
        P(("ctx", "wt"), None),
        P(),
        P(("ctx", "wt"), None),
        P(("ctx", "wt"), None, None),
        P(("ctx", "wt"), None, None),
        P(("ctx", "wt"), None, None),
        P("wt", "ctx", None),
    )
    out_specs = (
        P("wt", "ctx", None),
        P("wt", "ctx", None),
        P(),
        P(("ctx", "wt"), None),
        P(("ctx", "wt"), None),
        P(("ctx", "wt"), None),
        P(),
        P(),
        P(("ctx", "wt"), None),
        P(),
        P(("ctx", "wt"), None),
        P(("ctx", "wt"), None, None),
        P(("ctx", "wt"), None, None),
        P(("ctx", "wt"), None, None),
    )

    return jax.shard_map(
        on_device, mesh=mesh, in_specs=in_specs, out_specs=out_specs, check_vma=False
    )
```

```python
import functools
import math

import jax
import jax.numpy as jnp
from jax import lax
from jax.experimental import pallas as pl
from jax.experimental.pallas import tpu as pltpu
from jax.sharding import PartitionSpec as P


EPS = 1e-06
THETA = 1000000.0
MASKED = -1e30
MESH = pl.DeviceIdType.MESH


def norm_rows(value_rows, gain_vec):
    return (
        value_rows
        * lax.rsqrt(jnp.mean(value_rows * value_rows, axis=-1, keepdims=True) + EPS)
        * gain_vec
    )


def norm_back(value_rows, gain_vec, upstream):
    factor = lax.rsqrt(jnp.mean(value_rows * value_rows, axis=-1, keepdims=True) + EPS)
    normalized_input = value_rows * factor
    weighted = upstream * gain_vec
    inner_mean = jnp.mean(weighted * normalized_input, axis=-1, keepdims=True)
    return (factor * (weighted - normalized_input * inner_mean), upstream * normalized_input)


def rotary_tables(positions, head_dim):
    half_dim = head_dim // 2
    frequency = jnp.exp(
        jnp.arange(half_dim, dtype=jnp.float32) * (-2.0 * math.log(THETA) / head_dim)
    )
    angles = positions.astype(jnp.float32)[:, None] * frequency[None, :]
    angles = jnp.concatenate([angles, angles], axis=1)
    return (jnp.cos(angles)[:, None, :], jnp.sin(angles)[:, None, :])


def rotate(value_rows, cosine_table, sine_table):
    half_dim = value_rows.shape[-1] // 2
    turned = jnp.concatenate([-value_rows[..., half_dim:], value_rows[..., :half_dim]], axis=-1)
    return value_rows * cosine_table + turned * sine_table


def matmul(left_side, right_side):
    return jnp.dot(left_side, right_side, preferred_element_type=jnp.float32)


def contract_rows(left_side, right_side):
    return lax.dot_general(
        left_side, right_side, (((0,), (0,)), ((), ())), preferred_element_type=jnp.float32
    )


def contract_cols(left_side, right_side):
    return lax.dot_general(
        left_side, right_side, (((1,), (1,)), ((), ())), preferred_element_type=jnp.float32
    )


def spread_kernel(splits, streams_first, *refs):
    count = len(splits)
    ins, outs, stages = refs[:count], refs[count : 2 * count], refs[2 * count : 3 * count]
    send_sems, recv_sems, load_sems, store_sems = refs[3 * count :]
    ctx = lax.axis_index("ctx")
    z = lax.axis_index("wt")
    depth = lax.axis_size("wt")
    flip_y = ctx + 4 - 8 * (ctx // 4)
    step_x = 2 - 4 * ((ctx // 2) % 2)
    step_c = 1 - 2 * (ctx % 2)
    flip_x = ctx + step_x
    flip_xy = flip_y + step_x

    barrier = pltpu.get_barrier_semaphore()
    line = [lax.rem(z + d, depth) for d in range(1, depth)]
    for peer in line:
        pl.semaphore_signal(barrier, inc=1, device_id=(ctx, peer), device_id_type=MESH)
    for peer in (flip_x, flip_y, ctx + step_c):
        pl.semaphore_signal(barrier, inc=1, device_id=(peer, z), device_id_type=MESH)
    loads = []
    for k in range(count):
        loads.append(pltpu.make_async_copy(ins[k], stages[k], load_sems.at[k]))
        loads[k].start()
    pl.semaphore_wait(barrier, depth + 2)

    pieces = []
    for part in range(max(splits)):
        for k in range(count):
            if part < splits[k]:
                pieces.append((k, part))

    def group(k, owner, rows):
        view = outs[k]
        return view.at[:, owner, rows] if streams_first[k] else view.at[owner, :, rows]

    def block(k, rows):
        view = outs[k]
        return view.at[z, ctx, rows] if streams_first[k] else view.at[ctx, z, rows]

    def rows_of(k, part):
        size = ins[k].shape[0] // splits[k]
        return pl.ds(part * size, size)

    def send(number, slot, source, target, device):
        copy = pltpu.make_async_remote_copy(
            src_ref=source,
            dst_ref=target,
            send_sem=send_sems.at[number, slot],
            recv_sem=recv_sems.at[number, slot],
            device_id=device,
            device_id_type=MESH,
        )
        copy.start()
        return copy

    along = []
    for number, (k, part) in enumerate(pieces):
        rows = rows_of(k, part)
        along.append(
            [
                send(number, d, ins[k].at[rows], block(k, rows), (ctx, peer))
                for d, peer in enumerate(line)
            ]
        )
    stores = []
    for k in range(count):
        loads[k].wait()
        whole = pl.ds(0, ins[k].shape[0])
        stores.append(pltpu.make_async_copy(stages[k], block(k, whole), store_sems.at[k]))
        stores[k].start()
    for k in range(count):
        stores[k].wait()

    first_slot = depth - 1
    crossed, turned, shared = {}, {}, {}

    def owners(number):
        if number % 2:
            return flip_x, flip_y
        return flip_y, flip_x

    def cross(number):
        k, part = pieces[number]
        rows = rows_of(k, part)
        near, far = owners(number)
        for copy in along[number]:
            copy.wait_recv()
        mine = group(k, ctx, rows)
        crossed[number] = send(number, first_slot, mine, mine, (near, z))
        turned[number] = [send(number, first_slot + 1, mine, mine, (far, z))]
        shared[number] = [send(number, first_slot + 3, mine, mine, (ctx + step_c, z))]

    def turn_corner(number):
        k, part = pieces[number]
        rows = rows_of(k, part)
        near, far = owners(number)
        crossed[number].wait_recv()
        theirs = group(k, near, rows)
        turned[number].append(send(number, first_slot + 2, theirs, theirs, (far, z)))
        shared[number].append(send(number, first_slot + 4, theirs, theirs, (ctx + step_c, z)))

    def share(number):
        k, part = pieces[number]
        rows = rows_of(k, part)
        _, far = owners(number)
        for slot, (copy, owner) in enumerate(zip(turned[number], (far, flip_xy))):
            copy.wait_recv()
            theirs = group(k, owner, rows)
            shared[number].append(
                send(number, first_slot + 5 + slot, theirs, theirs, (ctx + step_c, z))
            )

    total = len(pieces)
    for step in range(total + 2):
        if step < total:
            cross(step)
        if 0 <= step - 1 < total:
            turn_corner(step - 1)
        if 0 <= step - 2 < total:
            share(step - 2)
    for number in range(total):
        for copy in shared[number]:
            copy.wait_recv()
        for copy in along[number] + [crossed[number]] + turned[number] + shared[number]:
            copy.wait_send()


def spread(values, splits, streams_first, channel):
    ctx_size, wt_size = lax.axis_size("ctx"), lax.axis_size("wt")
    total = sum(splits)
    heads = [(wt_size, ctx_size) if first else (ctx_size, wt_size) for first in streams_first]
    size = sum(value.size * value.dtype.itemsize for value in values)
    results = pl.pallas_call(
        functools.partial(spread_kernel, splits, streams_first),
        out_shape=[
            jax.ShapeDtypeStruct(head + value.shape, value.dtype)
            for head, value in zip(heads, values)
        ],
        in_specs=[pl.BlockSpec(memory_space=pl.ANY)] * len(values),
        out_specs=[pl.BlockSpec(memory_space=pl.ANY)] * len(values),
        scratch_shapes=[pltpu.VMEM(value.shape, value.dtype) for value in values]
        + [
            pltpu.SemaphoreType.DMA((total, wt_size + 6)),
            pltpu.SemaphoreType.DMA((total, wt_size + 6)),
            pltpu.SemaphoreType.DMA((len(values),)),
            pltpu.SemaphoreType.DMA((len(values),)),
        ],
        compiler_params=pltpu.CompilerParams(collective_id=channel, has_side_effects=True),
        cost_estimate=pl.CostEstimate(
            flops=0, bytes_accessed=2 * ctx_size * wt_size * size, transcendentals=0
        ),
    )(*values)
    return [result.reshape(-1, result.shape[-1]) for result in results]


def after(value, earlier):
    return lax.optimization_barrier((value, earlier))[0]


def stack_heads(block, first, head_dim, count):
    return jnp.concatenate(
        [block[:, (first + h) * head_dim : (first + h + 1) * head_dim] for h in range(count)],
        axis=0,
    )


def attend_kernel(
    head_dim,
    together,
    query_ref,
    pairs_ref,
    gain_ref,
    cosine_ref,
    sine_ref,
    query_pos_ref,
    query_doc_ref,
    key_pos_ref,
    key_doc_ref,
    mixed_ref,
    query_low_ref,
    bias_ref,
):
    tokens = query_ref.shape[0]
    heads = query_ref.shape[1] // head_dim
    scale = head_dim ** (-0.5)

    @pl.when(pl.program_id(0) == 0)
    def _():
        allowed = (key_pos_ref[...] <= query_pos_ref[...]) & (
            key_doc_ref[...] == query_doc_ref[...]
        )
        bias_ref[...] = jnp.where(allowed, 0.0, MASKED)

    keys = pairs_ref[:, :head_dim]
    values = pairs_ref[:, head_dim:]
    for first in range(0, heads, together):
        for h in range(first, first + together):
            columns = slice(h * head_dim, (h + 1) * head_dim)
            rows = query_ref[:, columns]
            rows = norm_rows(rows, gain_ref[...])
            turned = pltpu.roll(rows, head_dim // 2, axis=1)
            rows = rows * cosine_ref[...] + turned * sine_ref[...]
            query_low_ref[:, columns] = rows.astype(jnp.bfloat16)
        queries = stack_heads(query_low_ref, first, head_dim, together)
        scores = contract_cols(queries, keys) * scale
        scores = scores + jnp.concatenate([bias_ref[...]] * together, axis=0)
        weights = jnp.exp(scores - jnp.max(scores, axis=1, keepdims=True))
        weights = weights / jnp.sum(weights, axis=1, keepdims=True)
        mixed = matmul(weights.astype(jnp.bfloat16), values)
        for h in range(together):
            columns = slice((first + h) * head_dim, (first + h + 1) * head_dim)
            mixed_ref[:, columns] = mixed[h * tokens : (h + 1) * tokens].astype(jnp.bfloat16)


def attend_back_kernel(
    head_dim,
    together,
    query_ref,
    query_low_ref,
    cot_ref,
    pairs_ref,
    gain_ref,
    cosine_ref,
    sine_ref,
    query_pos_ref,
    query_doc_ref,
    key_pos_ref,
    key_doc_ref,
    query_cot_ref,
    pair_cot_ref,
    gain_cot_ref,
    bias_ref,
    key_sum_ref,
    value_sum_ref,
):
    tokens = query_ref.shape[0]
    heads = query_ref.shape[1] // head_dim
    scale = head_dim ** (-0.5)

    @pl.when(pl.program_id(0) == 0)
    def _():
        allowed = (key_pos_ref[...] <= query_pos_ref[...]) & (
            key_doc_ref[...] == query_doc_ref[...]
        )
        bias_ref[...] = jnp.where(allowed, 0.0, MASKED)

    keys = pairs_ref[:, :head_dim]
    values = pairs_ref[:, head_dim:]
    for first in range(0, heads, together):
        queries = stack_heads(query_low_ref, first, head_dim, together)
        cots = stack_heads(cot_ref, first, head_dim, together)
        scores = contract_cols(keys, queries) * scale
        scores = scores + jnp.concatenate([bias_ref[...]] * together, axis=1)
        weights = jnp.exp(scores - jnp.max(scores, axis=0, keepdims=True))
        weights = weights / jnp.sum(weights, axis=0, keepdims=True)
        weight_cot = contract_cols(values, cots)
        delta = jnp.sum(weights * weight_cot, axis=0, keepdims=True)
        score_cot = (weights * (weight_cot - delta)).astype(jnp.bfloat16)
        value_part = matmul(weights.astype(jnp.bfloat16), cots)
        key_part = matmul(score_cot, queries)
        if first:
            value_sum_ref[...] += value_part
            key_sum_ref[...] += key_part
        else:
            value_sum_ref[...] = value_part
            key_sum_ref[...] = key_part
        query_part = contract_rows(score_cot, keys) * scale
        for h in range(together):
            columns = slice((first + h) * head_dim, (first + h + 1) * head_dim)
            upstream = query_part[h * tokens : (h + 1) * tokens]
            turned = pltpu.roll(upstream, head_dim // 2, axis=1)
            upstream = upstream * cosine_ref[...] - turned * sine_ref[...]
            rows_cot, terms = norm_back(query_ref[:, columns], gain_ref[...], upstream)
            query_cot_ref[:, columns] = rows_cot.astype(jnp.bfloat16)
            gain_cot_ref[first + h : first + h + 1, :] = jnp.sum(terms, axis=0, keepdims=True)
    pair_cot_ref[:, :head_dim] = (key_sum_ref[...] * scale).astype(jnp.bfloat16)
    pair_cot_ref[:, head_dim:] = value_sum_ref[...].astype(jnp.bfloat16)


def attend(query_sum, pairs_all, gain, cosine, sine, query_pos, query_doc, key_pos, key_doc):
    tokens, q_width = query_sum.shape
    seq_len, pair_width = pairs_all.shape
    head_dim = gain.shape[0]
    key_heads = pair_width // (2 * head_dim)
    group = q_width // key_heads
    whole = lambda shape: pl.BlockSpec(shape, lambda g: (0, 0))
    flops = 4 * tokens * seq_len * q_width
    return pl.pallas_call(
        functools.partial(attend_kernel, head_dim, 2),
        grid=(key_heads,),
        in_specs=[
            pl.BlockSpec((tokens, group), lambda g: (0, g)),
            pl.BlockSpec((seq_len, 2 * head_dim), lambda g: (0, g)),
            whole((1, head_dim)),
            whole((tokens, head_dim)),
            whole((tokens, head_dim)),
            whole((tokens, 1)),
            whole((tokens, 1)),
            whole((1, seq_len)),
            whole((1, seq_len)),
        ],
        out_specs=[pl.BlockSpec((tokens, group), lambda g: (0, g))] * 2,
        out_shape=[jax.ShapeDtypeStruct((tokens, q_width), jnp.bfloat16)] * 2,
        scratch_shapes=[pltpu.VMEM((tokens, seq_len), jnp.float32)],
        compiler_params=pltpu.CompilerParams(vmem_limit_bytes=32 << 20),
        cost_estimate=pl.CostEstimate(
            flops=flops, bytes_accessed=8 * tokens * q_width, transcendentals=0
        ),
        name="attend",
    )(
        query_sum,
        pairs_all,
        gain[None, :],
        cosine,
        sine,
        query_pos[:, None],
        query_doc[:, None],
        key_pos[None, :],
        key_doc[None, :],
    )


def attend_back(
    query_sum,
    query_low,
    cots,
    pairs_all,
    gain,
    cosine,
    sine,
    query_pos,
    query_doc,
    key_pos,
    key_doc,
):
    tokens, q_width = query_sum.shape
    seq_len, pair_width = pairs_all.shape
    head_dim = gain.shape[0]
    key_heads = pair_width // (2 * head_dim)
    group = q_width // key_heads
    heads = group // head_dim
    whole = lambda shape: pl.BlockSpec(shape, lambda g: (0, 0))
    flops = 10 * tokens * seq_len * q_width
    return pl.pallas_call(
        functools.partial(attend_back_kernel, head_dim, 2),
        grid=(key_heads,),
        in_specs=[
            pl.BlockSpec((tokens, group), lambda g: (0, g)),
            pl.BlockSpec((tokens, group), lambda g: (0, g)),
            pl.BlockSpec((tokens, group), lambda g: (0, g)),
            pl.BlockSpec((seq_len, 2 * head_dim), lambda g: (0, g)),
            whole((1, head_dim)),
            whole((tokens, head_dim)),
            whole((tokens, head_dim)),
            whole((1, tokens)),
            whole((1, tokens)),
            whole((seq_len, 1)),
            whole((seq_len, 1)),
        ],
        out_specs=[
            pl.BlockSpec((tokens, group), lambda g: (0, g)),
            pl.BlockSpec((seq_len, 2 * head_dim), lambda g: (0, g)),
            pl.BlockSpec((heads, head_dim), lambda g: (g, 0)),
        ],
        out_shape=[
            jax.ShapeDtypeStruct((tokens, q_width), jnp.bfloat16),
            jax.ShapeDtypeStruct((seq_len, pair_width), jnp.bfloat16),
            jax.ShapeDtypeStruct((key_heads * heads, head_dim), jnp.float32),
        ],
        scratch_shapes=[
            pltpu.VMEM((seq_len, tokens), jnp.float32),
            pltpu.VMEM((seq_len, head_dim), jnp.float32),
            pltpu.VMEM((seq_len, head_dim), jnp.float32),
        ],
        compiler_params=pltpu.CompilerParams(vmem_limit_bytes=48 << 20),
        cost_estimate=pl.CostEstimate(
            flops=flops, bytes_accessed=12 * tokens * q_width, transcendentals=0
        ),
        name="attend_back",
    )(
        query_sum,
        query_low,
        cots,
        pairs_all,
        gain[None, :],
        cosine,
        sine,
        query_pos[None, :],
        query_doc[None, :],
        key_pos[:, None],
        key_doc[:, None],
    )


def sum_everywhere(vector):
    devices = lax.axis_size("ctx") * lax.axis_size("wt")
    spread = jnp.broadcast_to(vector[None, :], (devices, vector.shape[0]))
    return jnp.sum(
        lax.all_to_all(spread, ("ctx", "wt"), split_axis=0, concat_axis=0, tiled=True), axis=0
    )


def on_device(
    hidden_in,
    doc_lengths,
    routes,
    gain_attn,
    w_query,
    key_weight,
    value_weight,
    gain_query,
    gain_key,
    w_out,
    gain_moe,
    w_router,
    expert_gate,
    expert_up,
    expert_down,
    out_grad,
):
    tokens = hidden_in.shape[1]
    model_width = hidden_in.shape[2]
    ctx_size = lax.axis_size("ctx")
    wt_size = lax.axis_size("wt")
    devices = ctx_size * wt_size
    seq_len = tokens * ctx_size
    head_dim = gain_query.shape[0]
    kv_width = key_weight.shape[1]
    key_heads = kv_width // head_dim
    expert_count = w_router.shape[1]
    top_count = routes.shape[2]
    assert expert_gate.shape[0] == 1 and expert_count == devices
    capacity = tokens * top_count // wt_size
    ctx_index = lax.axis_index("ctx")
    wt_index = lax.axis_index("wt")
    both = ("ctx", "wt")
    by_stream = ("wt", "ctx")

    def gather(value, axes):
        return lax.all_gather(value, axes, axis=0, tiled=True)

    def exchange(value, axes):
        return lax.all_to_all(value, axes, split_axis=0, concat_axis=0, tiled=True)

    def scatter_sum(value, axes):
        return lax.psum_scatter(value, axes, scatter_dimension=0, tiled=True)

    def turn(blocks):
        arrived = []
        for step in range(wt_size):
            block = lax.dynamic_index_in_dim(
                blocks, lax.rem(wt_index + step, wt_size), keepdims=False
            )
            if step:
                pairs = [(w, (w + step) % wt_size) for w in range(wt_size)]
                block = lax.ppermute(block, "wt", pairs)
            arrived.append(block)
        return arrived

    def line_sum(blocks):
        return sum(block.astype(jnp.float32) for block in turn(blocks))

    doc_ends = jnp.cumsum(doc_lengths[0])
    all_positions = jnp.arange(seq_len, dtype=jnp.int32)
    doc_all = jnp.sum((doc_ends[None, :] <= all_positions[:, None]).astype(jnp.int32), axis=1)
    first_pos = ctx_index * tokens
    my_positions = first_pos + jnp.arange(tokens, dtype=jnp.int32)
    my_docs = lax.dynamic_slice_in_dim(doc_all, first_pos, tokens)
    cosine_all, sine_all = rotary_tables(all_positions, head_dim)

    def mine_of(rows):
        return lax.dynamic_slice_in_dim(rows, first_pos, tokens)

    cosine_table, sine_table = mine_of(cosine_all), mine_of(sine_all)
    cosine_rows = cosine_table[:, 0, :]
    first_half = jnp.arange(head_dim) < head_dim // 2
    sine_rows = jnp.where(first_half[None, :], -sine_table[:, 0, :], sine_table[:, 0, :])

    expert_ids = jnp.arange(expert_count, dtype=jnp.int32)
    hits = jnp.sum((routes[0][:, :, None] == expert_ids[None, None, :]).astype(jnp.int32), axis=1)
    local_rank = jnp.cumsum(hits, axis=0) - hits
    assert expert_count <= tokens
    counts = jnp.pad(jnp.sum(hits, axis=0), (0, tokens - expert_count))
    plane_mine = jnp.concatenate(
        [
            hits.T.reshape(ctx_size, wt_size, tokens),
            jnp.broadcast_to(counts, (ctx_size, 1, tokens)),
        ],
        axis=1,
    )
    plane = exchange(plane_mine, "ctx")
    earlier = jnp.arange(ctx_size, dtype=jnp.int32)[:, None] < ctx_index
    offsets = jnp.sum(jnp.where(earlier, plane[:, wt_size, :expert_count], 0), axis=0)
    kept = (hits > 0) & (local_rank + offsets[None, :] < capacity)
    keep_float = kept.astype(jnp.float32)
    hits_float = hits.astype(jnp.float32)

    def to_owner_rows(table):
        return table.reshape(tokens, ctx_size, wt_size).transpose(2, 1, 0).reshape(devices, tokens)

    def from_owner_rows(table):
        return table.reshape(wt_size, ctx_size, tokens).transpose(2, 1, 0).reshape(tokens, devices)

    hit_mine = exchange(to_owner_rows(hits), by_stream).reshape(wt_size, seq_len)
    slot_mine = jnp.cumsum(hit_mine, axis=1) - hit_mine
    slot_mine = jnp.where((hit_mine > 0) & (slot_mine < capacity), slot_mine, -1)
    slot_ids = jnp.arange(capacity, dtype=jnp.int32)
    place = slot_mine[:, None, :] == slot_ids[None, :, None]
    place_low = place.astype(jnp.bfloat16)
    hit_plane = plane[:, :wt_size].transpose(1, 0, 2).reshape(wt_size, seq_len)
    hit_plane = hit_plane[(wt_index - jnp.arange(wt_size)) % wt_size]
    slot_plane = jnp.cumsum(hit_plane, axis=1) - hit_plane
    slot_plane = jnp.where((hit_plane > 0) & (slot_plane < capacity), slot_plane, -1)
    spread_low = (slot_plane[:, None, :] == slot_ids[None, :, None]).astype(jnp.bfloat16)

    resid_in = hidden_in[0].astype(jnp.float32)
    normed_in = norm_rows(resid_in, gain_attn).astype(jnp.bfloat16)
    router_pad = -expert_count % head_dim
    normed_in_all = gather(normed_in, "ctx")
    side_mine = jnp.concatenate(
        [key_weight, value_weight, jnp.pad(w_router, ((0, 0), (0, router_pad)))], axis=1
    )
    small_plane = ctx_size == 8
    if small_plane:
        side_weights, query_full, out_full = spread(
            [side_mine, w_query, w_out], (2, 4, 4), (False,) * 3, 1
        )
    else:
        side_weights = gather(side_mine, both)
        query_full = gather(w_query, both)
        out_full = gather(w_out, both)
    router_full = side_weights[:, 2 * kv_width : 2 * kv_width + expert_count]
    pair_sums = lax.optimization_barrier(
        matmul(normed_in_all, side_weights[:, : 2 * kv_width])
    )
    key_sums = pair_sums[:, :kv_width].reshape(seq_len, key_heads, head_dim)
    key_low = rotate(norm_rows(key_sums, gain_key), cosine_all, sine_all).astype(jnp.bfloat16)
    value_low = pair_sums[:, kv_width:].astype(jnp.bfloat16)
    pairs_all = jnp.concatenate(
        [key_low, value_low.reshape(seq_len, key_heads, head_dim)], axis=2
    ).reshape(seq_len, 2 * kv_width)
    key_sum = mine_of(key_sums)
    if small_plane:
        cot_all = gather(after(out_grad[0], query_full), by_stream)
    query_sum = lax.optimization_barrier(matmul(normed_in, query_full))
    mixed_low, query_low = attend(
        query_sum,
        pairs_all,
        gain_query,
        cosine_rows,
        sine_rows,
        my_positions,
        my_docs,
        all_positions,
        doc_all,
    )
    resid_mid = resid_in + matmul(mixed_low, out_full)
    normed_mid = norm_rows(resid_mid, gain_moe).astype(jnp.bfloat16)

    if small_plane:
        (mid_all,) = spread([normed_mid], (4,), (True,), 2)
    else:
        mid_all = gather(normed_mid, by_stream)
    mid_all = mid_all.reshape(wt_size, seq_len, model_width)
    logits = matmul(normed_mid, router_full)
    logit_exp = jnp.exp(logits - jnp.max(logits, axis=-1, keepdims=True))
    router_probs = logit_exp / jnp.sum(logit_exp, axis=-1, keepdims=True)
    chosen_total = jnp.sum(hits_float * router_probs, axis=1, keepdims=True)
    gate_kept = jnp.where(kept, router_probs / chosen_total, 0.0)
    gate_mine = exchange(to_owner_rows(gate_kept), by_stream).reshape(wt_size, seq_len)

    def column_blocks(value):
        width = value.shape[1] // ctx_size
        blocks = value.reshape(tokens, ctx_size, width).transpose(1, 0, 2)
        return exchange(blocks, "ctx").reshape(seq_len, width)

    def pick_rows(table):
        return (
            jnp.einsum("wkt,wtd->wkd", place_low, table, preferred_element_type=jnp.float32)
            .astype(jnp.bfloat16)
            .reshape(wt_size * capacity, model_width)
        )

    filled = pick_rows(mid_all)
    if not small_plane:
        cot_all = gather(after(out_grad[0], filled), by_stream)
    cot_all = cot_all.reshape(wt_size, seq_len, model_width)
    mixed_columns = column_blocks(after(mixed_low, filled))
    gate_h = matmul(filled, expert_gate[0])
    up_h = matmul(filled, expert_up[0])
    sigma_h = jax.nn.sigmoid(gate_h)
    hidden_h = (gate_h * sigma_h * up_h).astype(jnp.bfloat16)
    result_rows = matmul(hidden_h, expert_down[0]).astype(jnp.bfloat16)
    cot_rows = pick_rows(cot_all)
    gate_rows = jnp.sum(jnp.where(place, gate_mine[:, None, :], 0.0), axis=2).reshape(-1)
    gate_cot_rows = jnp.sum(
        result_rows.astype(jnp.float32) * cot_rows.astype(jnp.float32), axis=1
    ).reshape(wt_size, capacity)
    gate_cot_mine = jnp.sum(jnp.where(place, gate_cot_rows[:, :, None], 0.0), axis=1)
    out_rows_cot = (gate_rows[:, None] * cot_rows.astype(jnp.float32)).astype(jnp.bfloat16)
    hidden_cot = contract_cols(out_rows_cot, expert_down[0])
    grad_down = contract_rows(hidden_h, out_rows_cot)
    gate_cot_h = (hidden_cot * up_h * sigma_h * (1.0 + gate_h * (1.0 - sigma_h))).astype(
        jnp.bfloat16
    )
    up_cot_h = (hidden_cot * gate_h * sigma_h).astype(jnp.bfloat16)
    grad_gate = contract_rows(filled, gate_cot_h)
    grad_up = contract_rows(filled, up_cot_h)
    in_rows_cot = (
        contract_cols(gate_cot_h, expert_gate[0]) + contract_cols(up_cot_h, expert_up[0])
    ).astype(jnp.bfloat16)

    def add_pairs(table, stream_rows):
        partial = contract_rows(
            table.reshape(wt_size * capacity, seq_len), jnp.concatenate(stream_rows, axis=0)
        ).astype(jnp.bfloat16)
        return scatter_sum(partial, "ctx").astype(jnp.float32)

    mixed_rows = (gate_rows[:, None] * result_rows.astype(jnp.float32)).astype(jnp.bfloat16)
    in_rows_cot, mixed_columns, spread_low = lax.optimization_barrier(
        (in_rows_cot, mixed_columns, spread_low)
    )
    gate_cot = from_owner_rows(exchange(
        after(gate_cot_mine, in_rows_cot).reshape(devices, tokens), by_stream
    ))
    blocks_shape = (wt_size, capacity, model_width)
    stream_cots = turn(in_rows_cot.reshape(blocks_shape))
    returned_cot = add_pairs(spread_low, stream_cots)
    stream_mixed = turn(after(mixed_rows, stream_cots).reshape(blocks_shape))
    out_cot = out_grad[0].astype(jnp.float32)

    kept_cot = gate_cot * keep_float
    chosen_cot = kept_cot / chosen_total - jnp.sum(
        kept_cot * router_probs, axis=1, keepdims=True
    ) / (chosen_total * chosen_total)
    probs_cot = hits_float * chosen_cot
    logit_cot = (
        router_probs * (probs_cot - jnp.sum(router_probs * probs_cot, axis=1, keepdims=True))
    ).astype(jnp.bfloat16)
    mid_cot = returned_cot + contract_cols(logit_cot, router_full)
    mid_norm_cot, gain_moe_terms = norm_back(resid_mid, gain_moe, mid_cot)
    resid_cot = out_cot + mid_norm_cot
    attn_cot = resid_cot.astype(jnp.bfloat16)
    router_parts = exchange(contract_rows(normed_mid, logit_cot).reshape(devices, -1), both)
    grad_w_router = jnp.sum(router_parts, axis=0).reshape(w_router.shape)

    mixed_cot = contract_cols(attn_cot, out_full)
    attn_cot_all = gather(attn_cot, "ctx")
    out_block = contract_rows(mixed_columns, attn_cot_all).astype(jnp.bfloat16)
    grad_w_out = line_sum(out_block.reshape(wt_size, -1, model_width))

    query_cot_low, pair_cots, gain_query_terms = attend_back(
        query_sum,
        query_low,
        mixed_cot.astype(jnp.bfloat16),
        pairs_all,
        gain_query,
        cosine_rows,
        sine_rows,
        my_positions,
        my_docs,
        all_positions,
        doc_all,
    )
    mixed_mine = add_pairs(after(spread_low, query_cot_low), stream_mixed)
    hidden_out = after(resid_mid, query_cot_low) + mixed_mine
    pair_mine = scatter_sum(pair_cots, "ctx").reshape(tokens, key_heads, 2, head_dim)
    key_mine = pair_mine[:, :, 0].astype(jnp.float32)
    value_cot_low = pair_mine[:, :, 1].reshape(tokens, kv_width)
    key_pre, gain_key_terms = norm_back(
        key_sum,
        gain_key,
        rotate(key_mine, cosine_table, -sine_table),
    )
    key_cot_low = key_pre.reshape(tokens, kv_width).astype(jnp.bfloat16)
    pair_cot_low = jnp.concatenate([key_cot_low, value_cot_low], axis=1)

    def weight_grad(cots):
        width = cots.shape[1] // ctx_size
        block = contract_rows(normed_in_all, column_blocks(cots)).astype(jnp.bfloat16)
        block = block.reshape(ctx_size, wt_size, -1, width).transpose(1, 0, 2, 3)
        mine = line_sum(block).astype(jnp.bfloat16)
        rows = exchange(mine, "ctx")
        return rows.transpose(1, 0, 2).reshape(-1, width * ctx_size).astype(jnp.float32)

    grad_w_query = weight_grad(query_cot_low)
    grad_pair = weight_grad(pair_cot_low)
    grad_w_key = grad_pair[:, :kv_width]
    grad_w_value = grad_pair[:, kv_width:]
    in_cot = contract_cols(query_cot_low, query_full) + contract_cols(
        pair_cot_low, side_weights[:, : 2 * kv_width]
    )
    in_norm_cot, gain_attn_terms = norm_back(resid_in, gain_attn, in_cot)
    grad_in = resid_cot + in_norm_cot
    gains = sum_everywhere(
        jnp.concatenate(
            [
                jnp.sum(gain_attn_terms, axis=0),
                jnp.sum(gain_query_terms, axis=0),
                jnp.sum(gain_key_terms, axis=(0, 1)),
                jnp.sum(gain_moe_terms, axis=0),
            ]
        )
    )
    grad_gain_attn = gains[:model_width]
    grad_gain_query = gains[model_width : model_width + head_dim]
    grad_gain_key = gains[model_width + head_dim : model_width + 2 * head_dim]
    grad_gain_moe = gains[model_width + 2 * head_dim :]
    return (
        hidden_out[None],
        grad_in[None],
        grad_gain_attn,
        grad_w_query,
        grad_w_key,
        grad_w_value,
        grad_gain_query,
        grad_gain_key,
        grad_w_out,
        grad_gain_moe,
        grad_w_router,
        grad_gate[None],
        grad_up[None],
        grad_down[None],
    )


def solution(mesh):
    in_specs = (
        P("wt", "ctx", None),
        P("wt", None),
        P("wt", "ctx", None),
        P(),
        P(("ctx", "wt"), None),
        P(("ctx", "wt"), None),
        P(("ctx", "wt"), None),
        P(),
        P(),
        P(("ctx", "wt"), None),
        P(),
        P(("ctx", "wt"), None),
        P(("ctx", "wt"), None, None),
        P(("ctx", "wt"), None, None),
        P(("ctx", "wt"), None, None),
        P("wt", "ctx", None),
    )
    out_specs = (
        P("wt", "ctx", None),
        P("wt", "ctx", None),
        P(),
        P(("ctx", "wt"), None),
        P(("ctx", "wt"), None),
        P(("ctx", "wt"), None),
        P(),
        P(),
        P(("ctx", "wt"), None),
        P(),
        P(("ctx", "wt"), None),
        P(("ctx", "wt"), None, None),
        P(("ctx", "wt"), None, None),
        P(("ctx", "wt"), None, None),
    )

    return jax.shard_map(
        on_device, mesh=mesh, in_specs=in_specs, out_specs=out_specs, check_vma=False
    )
```

```python
import functools
import math

import jax
import jax.numpy as jnp
from jax import lax
from jax.experimental import pallas as pl
from jax.experimental.pallas import tpu as pltpu
from jax.sharding import PartitionSpec as P


EPS = 1e-06
THETA = 1000000.0
MASKED = -1e30
MESH = pl.DeviceIdType.MESH


def norm_rows(value_rows, gain_vec):
    return (
        value_rows
        * lax.rsqrt(jnp.mean(value_rows * value_rows, axis=-1, keepdims=True) + EPS)
        * gain_vec
    )


def norm_back(value_rows, gain_vec, upstream):
    factor = lax.rsqrt(jnp.mean(value_rows * value_rows, axis=-1, keepdims=True) + EPS)
    normalized_input = value_rows * factor
    weighted = upstream * gain_vec
    inner_mean = jnp.mean(weighted * normalized_input, axis=-1, keepdims=True)
    return (factor * (weighted - normalized_input * inner_mean), upstream * normalized_input)


def rotary_tables(positions, head_dim):
    half_dim = head_dim // 2
    frequency = jnp.exp(
        jnp.arange(half_dim, dtype=jnp.float32) * (-2.0 * math.log(THETA) / head_dim)
    )
    angles = positions.astype(jnp.float32)[:, None] * frequency[None, :]
    angles = jnp.concatenate([angles, angles], axis=1)
    return (jnp.cos(angles)[:, None, :], jnp.sin(angles)[:, None, :])


def rotate(value_rows, cosine_table, sine_table):
    half_dim = value_rows.shape[-1] // 2
    turned = jnp.concatenate([-value_rows[..., half_dim:], value_rows[..., :half_dim]], axis=-1)
    return value_rows * cosine_table + turned * sine_table


def matmul(left_side, right_side):
    return jnp.dot(left_side, right_side, preferred_element_type=jnp.float32)


def contract_rows(left_side, right_side):
    return lax.dot_general(
        left_side, right_side, (((0,), (0,)), ((), ())), preferred_element_type=jnp.float32
    )


def contract_cols(left_side, right_side):
    return lax.dot_general(
        left_side, right_side, (((1,), (1,)), ((), ())), preferred_element_type=jnp.float32
    )


def spread_kernel(splits, streams_first, *refs):
    count = len(splits)
    ins, outs, stages = refs[:count], refs[count : 2 * count], refs[2 * count : 3 * count]
    send_sems, recv_sems, load_sems, store_sems = refs[3 * count :]
    ctx = lax.axis_index("ctx")
    z = lax.axis_index("wt")
    depth = lax.axis_size("wt")
    flip_y = ctx + 4 - 8 * (ctx // 4)
    step_x = 2 - 4 * ((ctx // 2) % 2)
    step_c = 1 - 2 * (ctx % 2)
    flip_x = ctx + step_x
    flip_xy = flip_y + step_x

    barrier = pltpu.get_barrier_semaphore()
    line = [lax.rem(z + d, depth) for d in range(1, depth)]
    for peer in line:
        pl.semaphore_signal(barrier, inc=1, device_id=(ctx, peer), device_id_type=MESH)
    for peer in (flip_x, flip_y, ctx + step_c):
        pl.semaphore_signal(barrier, inc=1, device_id=(peer, z), device_id_type=MESH)
    loads = []
    for k in range(count):
        loads.append(pltpu.make_async_copy(ins[k], stages[k], load_sems.at[k]))
        loads[k].start()
    pl.semaphore_wait(barrier, depth + 2)

    pieces = []
    for part in range(max(splits)):
        for k in range(count):
            if part < splits[k]:
                pieces.append((k, part))

    def group(k, owner, rows):
        view = outs[k]
        return view.at[:, owner, rows] if streams_first[k] else view.at[owner, :, rows]

    def block(k, rows):
        view = outs[k]
        return view.at[z, ctx, rows] if streams_first[k] else view.at[ctx, z, rows]

    def rows_of(k, part):
        size = ins[k].shape[0] // splits[k]
        return pl.ds(part * size, size)

    def send(number, slot, source, target, device):
        copy = pltpu.make_async_remote_copy(
            src_ref=source,
            dst_ref=target,
            send_sem=send_sems.at[number, slot],
            recv_sem=recv_sems.at[number, slot],
            device_id=device,
            device_id_type=MESH,
        )
        copy.start()
        return copy

    along = []
    for number, (k, part) in enumerate(pieces):
        rows = rows_of(k, part)
        along.append(
            [
                send(number, d, ins[k].at[rows], block(k, rows), (ctx, peer))
                for d, peer in enumerate(line)
            ]
        )
    stores = []
    for k in range(count):
        loads[k].wait()
        whole = pl.ds(0, ins[k].shape[0])
        stores.append(pltpu.make_async_copy(stages[k], block(k, whole), store_sems.at[k]))
        stores[k].start()
    for k in range(count):
        stores[k].wait()

    first_slot = depth - 1
    crossed, turned, shared = {}, {}, {}

    def owners(number):
        if number % 2:
            return flip_x, flip_y
        return flip_y, flip_x

    def cross(number):
        k, part = pieces[number]
        rows = rows_of(k, part)
        near, far = owners(number)
        for copy in along[number]:
            copy.wait_recv()
        mine = group(k, ctx, rows)
        crossed[number] = send(number, first_slot, mine, mine, (near, z))
        turned[number] = [send(number, first_slot + 1, mine, mine, (far, z))]
        shared[number] = [send(number, first_slot + 3, mine, mine, (ctx + step_c, z))]

    def turn_corner(number):
        k, part = pieces[number]
        rows = rows_of(k, part)
        near, far = owners(number)
        crossed[number].wait_recv()
        theirs = group(k, near, rows)
        turned[number].append(send(number, first_slot + 2, theirs, theirs, (far, z)))
        shared[number].append(send(number, first_slot + 4, theirs, theirs, (ctx + step_c, z)))

    def share(number):
        k, part = pieces[number]
        rows = rows_of(k, part)
        _, far = owners(number)
        for slot, (copy, owner) in enumerate(zip(turned[number], (far, flip_xy))):
            copy.wait_recv()
            theirs = group(k, owner, rows)
            shared[number].append(
                send(number, first_slot + 5 + slot, theirs, theirs, (ctx + step_c, z))
            )

    total = len(pieces)
    for step in range(total + 2):
        if step < total:
            cross(step)
        if 0 <= step - 1 < total:
            turn_corner(step - 1)
        if 0 <= step - 2 < total:
            share(step - 2)
    for number in range(total):
        for copy in shared[number]:
            copy.wait_recv()
        for copy in along[number] + [crossed[number]] + turned[number] + shared[number]:
            copy.wait_send()


def spread(values, splits, streams_first, channel):
    ctx_size, wt_size = lax.axis_size("ctx"), lax.axis_size("wt")
    total = sum(splits)
    heads = [(wt_size, ctx_size) if first else (ctx_size, wt_size) for first in streams_first]
    size = sum(value.size * value.dtype.itemsize for value in values)
    results = pl.pallas_call(
        functools.partial(spread_kernel, splits, streams_first),
        out_shape=[
            jax.ShapeDtypeStruct(head + value.shape, value.dtype)
            for head, value in zip(heads, values)
        ],
        in_specs=[pl.BlockSpec(memory_space=pl.ANY)] * len(values),
        out_specs=[pl.BlockSpec(memory_space=pl.ANY)] * len(values),
        scratch_shapes=[pltpu.VMEM(value.shape, value.dtype) for value in values]
        + [
            pltpu.SemaphoreType.DMA((total, wt_size + 6)),
            pltpu.SemaphoreType.DMA((total, wt_size + 6)),
            pltpu.SemaphoreType.DMA((len(values),)),
            pltpu.SemaphoreType.DMA((len(values),)),
        ],
        compiler_params=pltpu.CompilerParams(collective_id=channel, has_side_effects=True),
        cost_estimate=pl.CostEstimate(
            flops=0, bytes_accessed=2 * ctx_size * wt_size * size, transcendentals=0
        ),
    )(*values)
    return [result.reshape(-1, result.shape[-1]) for result in results]


def after(value, earlier):
    return lax.optimization_barrier((value, earlier))[0]


def stack_heads(block, first, head_dim, count):
    return jnp.concatenate(
        [block[:, (first + h) * head_dim : (first + h + 1) * head_dim] for h in range(count)],
        axis=0,
    )


def rotated(sums, gain_ref, cosine_ref, sine_ref):
    rows = norm_rows(sums, gain_ref[...])
    turned = pltpu.roll(rows, rows.shape[1] // 2, axis=1)
    return (rows * cosine_ref[...] + turned * sine_ref[...]).astype(jnp.bfloat16)


def attend_kernel(
    head_dim,
    together,
    query_ref,
    key_ref,
    value_ref,
    gain_ref,
    cosine_ref,
    sine_ref,
    key_gain_ref,
    key_cosine_ref,
    key_sine_ref,
    query_pos_ref,
    query_doc_ref,
    key_pos_ref,
    key_doc_ref,
    mixed_ref,
    query_low_ref,
    bias_ref,
):
    tokens = query_ref.shape[0]
    heads = query_ref.shape[1] // head_dim
    scale = head_dim ** (-0.5)

    @pl.when(pl.program_id(0) == 0)
    def _():
        allowed = (key_pos_ref[...] <= query_pos_ref[...]) & (
            key_doc_ref[...] == query_doc_ref[...]
        )
        bias_ref[...] = jnp.where(allowed, 0.0, MASKED)

    keys = rotated(key_ref[...], key_gain_ref, key_cosine_ref, key_sine_ref)
    values = value_ref[...].astype(jnp.bfloat16)
    for first in range(0, heads, together):
        for h in range(first, first + together):
            columns = slice(h * head_dim, (h + 1) * head_dim)
            query_low_ref[:, columns] = rotated(
                query_ref[:, columns], gain_ref, cosine_ref, sine_ref
            )
        queries = stack_heads(query_low_ref, first, head_dim, together)
        scores = contract_cols(queries, keys) * scale
        scores = scores + jnp.concatenate([bias_ref[...]] * together, axis=0)
        weights = jnp.exp(scores - jnp.max(scores, axis=1, keepdims=True))
        weights = weights / jnp.sum(weights, axis=1, keepdims=True)
        mixed = matmul(weights.astype(jnp.bfloat16), values)
        for h in range(together):
            columns = slice((first + h) * head_dim, (first + h + 1) * head_dim)
            mixed_ref[:, columns] = mixed[h * tokens : (h + 1) * tokens].astype(jnp.bfloat16)


def attend_back_kernel(
    head_dim,
    together,
    query_ref,
    query_low_ref,
    cot_ref,
    key_ref,
    value_ref,
    gain_ref,
    cosine_ref,
    sine_ref,
    key_gain_ref,
    key_cosine_ref,
    key_sine_ref,
    query_pos_ref,
    query_doc_ref,
    key_pos_ref,
    key_doc_ref,
    query_cot_ref,
    pair_cot_ref,
    gain_cot_ref,
    bias_ref,
    key_sum_ref,
    value_sum_ref,
):
    tokens = query_ref.shape[0]
    heads = query_ref.shape[1] // head_dim
    scale = head_dim ** (-0.5)

    @pl.when(pl.program_id(0) == 0)
    def _():
        allowed = (key_pos_ref[...] <= query_pos_ref[...]) & (
            key_doc_ref[...] == query_doc_ref[...]
        )
        bias_ref[...] = jnp.where(allowed, 0.0, MASKED)

    keys = rotated(key_ref[...], key_gain_ref, key_cosine_ref, key_sine_ref)
    values = value_ref[...].astype(jnp.bfloat16)
    for first in range(0, heads, together):
        queries = stack_heads(query_low_ref, first, head_dim, together)
        cots = stack_heads(cot_ref, first, head_dim, together)
        scores = contract_cols(keys, queries) * scale
        scores = scores + jnp.concatenate([bias_ref[...]] * together, axis=1)
        weights = jnp.exp(scores - jnp.max(scores, axis=0, keepdims=True))
        weights = weights / jnp.sum(weights, axis=0, keepdims=True)
        weight_cot = contract_cols(values, cots)
        delta = jnp.sum(weights * weight_cot, axis=0, keepdims=True)
        score_cot = (weights * (weight_cot - delta)).astype(jnp.bfloat16)
        value_part = matmul(weights.astype(jnp.bfloat16), cots)
        key_part = matmul(score_cot, queries)
        if first:
            value_sum_ref[...] += value_part
            key_sum_ref[...] += key_part
        else:
            value_sum_ref[...] = value_part
            key_sum_ref[...] = key_part
        query_part = contract_rows(score_cot, keys) * scale
        for h in range(together):
            columns = slice((first + h) * head_dim, (first + h + 1) * head_dim)
            upstream = query_part[h * tokens : (h + 1) * tokens]
            turned = pltpu.roll(upstream, head_dim // 2, axis=1)
            upstream = upstream * cosine_ref[...] - turned * sine_ref[...]
            rows_cot, terms = norm_back(query_ref[:, columns], gain_ref[...], upstream)
            query_cot_ref[:, columns] = rows_cot.astype(jnp.bfloat16)
            gain_cot_ref[first + h : first + h + 1, :] = jnp.sum(terms, axis=0, keepdims=True)
    pair_cot_ref[:, :head_dim] = (key_sum_ref[...] * scale).astype(jnp.bfloat16)
    pair_cot_ref[:, head_dim:] = value_sum_ref[...].astype(jnp.bfloat16)


def attend(query_sum, pair_sums, gains, tables, query_rows, key_rows):
    tokens, q_width = query_sum.shape
    seq_len, pair_width = pair_sums.shape
    head_dim = gains[0].shape[0]
    key_heads = pair_width // (2 * head_dim)
    group = q_width // key_heads
    whole = lambda shape: pl.BlockSpec(shape, lambda g: (0, 0))
    flops = 4 * tokens * seq_len * q_width
    return pl.pallas_call(
        functools.partial(attend_kernel, head_dim, 2),
        grid=(key_heads,),
        in_specs=[
            pl.BlockSpec((tokens, group), lambda g: (0, g)),
            pl.BlockSpec((seq_len, head_dim), lambda g: (0, g)),
            pl.BlockSpec((seq_len, head_dim), lambda g: (0, key_heads + g)),
            whole((1, head_dim)),
            whole((tokens, head_dim)),
            whole((tokens, head_dim)),
            whole((1, head_dim)),
            whole((seq_len, head_dim)),
            whole((seq_len, head_dim)),
            whole((tokens, 1)),
            whole((tokens, 1)),
            whole((1, seq_len)),
            whole((1, seq_len)),
        ],
        out_specs=[pl.BlockSpec((tokens, group), lambda g: (0, g))] * 2,
        out_shape=[jax.ShapeDtypeStruct((tokens, q_width), jnp.bfloat16)] * 2,
        scratch_shapes=[pltpu.VMEM((tokens, seq_len), jnp.float32)],
        compiler_params=pltpu.CompilerParams(vmem_limit_bytes=48 << 20),
        cost_estimate=pl.CostEstimate(
            flops=flops, bytes_accessed=8 * tokens * q_width, transcendentals=0
        ),
        name="attend",
    )(
        query_sum,
        pair_sums,
        pair_sums,
        gains[0][None, :],
        *tables[:2],
        gains[1][None, :],
        *tables[2:],
        *(row[:, None] for row in query_rows),
        *(row[None, :] for row in key_rows),
    )


def attend_back(query_sum, query_low, cots, pair_sums, gains, tables, query_rows, key_rows):
    tokens, q_width = query_sum.shape
    seq_len, pair_width = pair_sums.shape
    head_dim = gains[0].shape[0]
    key_heads = pair_width // (2 * head_dim)
    group = q_width // key_heads
    heads = group // head_dim
    whole = lambda shape: pl.BlockSpec(shape, lambda g: (0, 0))
    flops = 10 * tokens * seq_len * q_width
    return pl.pallas_call(
        functools.partial(attend_back_kernel, head_dim, 2),
        grid=(key_heads,),
        in_specs=[
            pl.BlockSpec((tokens, group), lambda g: (0, g)),
            pl.BlockSpec((tokens, group), lambda g: (0, g)),
            pl.BlockSpec((tokens, group), lambda g: (0, g)),
            pl.BlockSpec((seq_len, head_dim), lambda g: (0, g)),
            pl.BlockSpec((seq_len, head_dim), lambda g: (0, key_heads + g)),
            whole((1, head_dim)),
            whole((tokens, head_dim)),
            whole((tokens, head_dim)),
            whole((1, head_dim)),
            whole((seq_len, head_dim)),
            whole((seq_len, head_dim)),
            whole((1, tokens)),
            whole((1, tokens)),
            whole((seq_len, 1)),
            whole((seq_len, 1)),
        ],
        out_specs=[
            pl.BlockSpec((tokens, group), lambda g: (0, g)),
            pl.BlockSpec((seq_len, 2 * head_dim), lambda g: (0, g)),
            pl.BlockSpec((heads, head_dim), lambda g: (g, 0)),
        ],
        out_shape=[
            jax.ShapeDtypeStruct((tokens, q_width), jnp.bfloat16),
            jax.ShapeDtypeStruct((seq_len, pair_width), jnp.bfloat16),
            jax.ShapeDtypeStruct((key_heads * heads, head_dim), jnp.float32),
        ],
        scratch_shapes=[
            pltpu.VMEM((seq_len, tokens), jnp.float32),
            pltpu.VMEM((seq_len, head_dim), jnp.float32),
            pltpu.VMEM((seq_len, head_dim), jnp.float32),
        ],
        compiler_params=pltpu.CompilerParams(vmem_limit_bytes=56 << 20),
        cost_estimate=pl.CostEstimate(
            flops=flops, bytes_accessed=12 * tokens * q_width, transcendentals=0
        ),
        name="attend_back",
    )(
        query_sum,
        query_low,
        cots,
        pair_sums,
        pair_sums,
        gains[0][None, :],
        *tables[:2],
        gains[1][None, :],
        *tables[2:],
        *(row[None, :] for row in query_rows),
        *(row[:, None] for row in key_rows),
    )


def sum_everywhere(vector):
    devices = lax.axis_size("ctx") * lax.axis_size("wt")
    spread = jnp.broadcast_to(vector[None, :], (devices, vector.shape[0]))
    return jnp.sum(
        lax.all_to_all(spread, ("ctx", "wt"), split_axis=0, concat_axis=0, tiled=True), axis=0
    )


def on_device(
    hidden_in,
    doc_lengths,
    routes,
    gain_attn,
    w_query,
    key_weight,
    value_weight,
    gain_query,
    gain_key,
    w_out,
    gain_moe,
    w_router,
    expert_gate,
    expert_up,
    expert_down,
    out_grad,
):
    tokens = hidden_in.shape[1]
    model_width = hidden_in.shape[2]
    ctx_size = lax.axis_size("ctx")
    wt_size = lax.axis_size("wt")
    devices = ctx_size * wt_size
    seq_len = tokens * ctx_size
    head_dim = gain_query.shape[0]
    kv_width = key_weight.shape[1]
    key_heads = kv_width // head_dim
    expert_count = w_router.shape[1]
    top_count = routes.shape[2]
    assert expert_gate.shape[0] == 1 and expert_count == devices
    capacity = tokens * top_count // wt_size
    ctx_index = lax.axis_index("ctx")
    wt_index = lax.axis_index("wt")
    both = ("ctx", "wt")
    by_stream = ("wt", "ctx")

    def gather(value, axes):
        return lax.all_gather(value, axes, axis=0, tiled=True)

    def exchange(value, axes):
        return lax.all_to_all(value, axes, split_axis=0, concat_axis=0, tiled=True)

    def scatter_sum(value, axes):
        return lax.psum_scatter(value, axes, scatter_dimension=0, tiled=True)

    def turn(blocks):
        arrived = []
        for step in range(wt_size):
            block = lax.dynamic_index_in_dim(
                blocks, lax.rem(wt_index + step, wt_size), keepdims=False
            )
            if step:
                pairs = [(w, (w + step) % wt_size) for w in range(wt_size)]
                block = lax.ppermute(block, "wt", pairs)
            arrived.append(block)
        return arrived

    def add_up(blocks):
        return sum(block.astype(jnp.float32) for block in blocks)

    doc_ends = jnp.cumsum(doc_lengths[0])
    all_positions = jnp.arange(seq_len, dtype=jnp.int32)
    doc_all = jnp.sum((doc_ends[None, :] <= all_positions[:, None]).astype(jnp.int32), axis=1)
    first_pos = ctx_index * tokens
    my_positions = first_pos + jnp.arange(tokens, dtype=jnp.int32)
    my_docs = lax.dynamic_slice_in_dim(doc_all, first_pos, tokens)
    cosine_all, sine_all = rotary_tables(all_positions, head_dim)

    def mine_of(rows):
        return lax.dynamic_slice_in_dim(rows, first_pos, tokens)

    cosine_table, sine_table = mine_of(cosine_all), mine_of(sine_all)
    first_half = jnp.arange(head_dim) < head_dim // 2
    turned_all = jnp.where(first_half[None, :], -sine_all[:, 0, :], sine_all[:, 0, :])
    tables = (mine_of(cosine_all[:, 0, :]), mine_of(turned_all), cosine_all[:, 0, :], turned_all)

    expert_ids = jnp.arange(expert_count, dtype=jnp.int32)
    hits = jnp.sum((routes[0][:, :, None] == expert_ids[None, None, :]).astype(jnp.int32), axis=1)
    local_rank = jnp.cumsum(hits, axis=0) - hits
    assert expert_count <= tokens
    counts = jnp.pad(jnp.sum(hits, axis=0), (0, tokens - expert_count))
    plane_mine = jnp.concatenate(
        [
            hits.T.reshape(ctx_size, wt_size, tokens),
            jnp.broadcast_to(counts, (ctx_size, 1, tokens)),
        ],
        axis=1,
    )
    plane = exchange(plane_mine, "ctx")
    earlier = jnp.arange(ctx_size, dtype=jnp.int32)[:, None] < ctx_index
    offsets = jnp.sum(jnp.where(earlier, plane[:, wt_size, :expert_count], 0), axis=0)
    kept = (hits > 0) & (local_rank + offsets[None, :] < capacity)
    keep_float = kept.astype(jnp.float32)
    hits_float = hits.astype(jnp.float32)

    def to_owner_rows(table):
        return table.reshape(tokens, ctx_size, wt_size).transpose(2, 1, 0).reshape(devices, tokens)

    def from_owner_rows(table):
        return table.reshape(wt_size, ctx_size, tokens).transpose(2, 1, 0).reshape(tokens, devices)

    hit_mine = exchange(to_owner_rows(hits), by_stream).reshape(wt_size, seq_len)
    slot_mine = jnp.cumsum(hit_mine, axis=1) - hit_mine
    slot_mine = jnp.where((hit_mine > 0) & (slot_mine < capacity), slot_mine, -1)
    slot_ids = jnp.arange(capacity, dtype=jnp.int32)
    place = slot_mine[:, None, :] == slot_ids[None, :, None]
    place_low = place.astype(jnp.bfloat16)
    hit_plane = plane[:, :wt_size].transpose(1, 0, 2).reshape(wt_size, seq_len)
    hit_plane = hit_plane[(wt_index - jnp.arange(wt_size)) % wt_size]
    slot_plane = jnp.cumsum(hit_plane, axis=1) - hit_plane
    slot_plane = jnp.where((hit_plane > 0) & (slot_plane < capacity), slot_plane, -1)
    spread_low = (slot_plane[:, None, :] == slot_ids[None, :, None]).astype(jnp.bfloat16)

    resid_in = hidden_in[0].astype(jnp.float32)
    normed_in = norm_rows(resid_in, gain_attn).astype(jnp.bfloat16)
    router_pad = -expert_count % head_dim
    normed_in_all = gather(normed_in, "ctx")
    side_mine = jnp.concatenate(
        [key_weight, value_weight, jnp.pad(w_router, ((0, 0), (0, router_pad)))], axis=1
    )
    small_plane = ctx_size == 8
    if small_plane:
        side_weights, query_full, out_full = spread(
            [side_mine, w_query, w_out], (2, 4, 4), (False,) * 3, 1
        )
    else:
        side_weights = gather(side_mine, both)
        query_full = gather(w_query, both)
        out_full = gather(w_out, both)
    router_full = side_weights[:, 2 * kv_width : 2 * kv_width + expert_count]
    pair_sums = lax.optimization_barrier(
        matmul(normed_in_all, side_weights[:, : 2 * kv_width])
    )
    key_sum = mine_of(pair_sums)[:, :kv_width].reshape(tokens, key_heads, head_dim)
    if small_plane:
        cot_all = gather(after(out_grad[0], query_full), by_stream)
    query_sum = lax.optimization_barrier(matmul(normed_in, query_full))
    gains = (gain_query, gain_key)
    query_rows, key_rows = (my_positions, my_docs), (all_positions, doc_all)
    mixed_low, query_low = attend(query_sum, pair_sums, gains, tables, query_rows, key_rows)
    resid_mid = resid_in + matmul(mixed_low, out_full)
    normed_mid = norm_rows(resid_mid, gain_moe).astype(jnp.bfloat16)

    if small_plane:
        (mid_all,) = spread([normed_mid], (4,), (True,), 2)
    else:
        mid_all = gather(normed_mid, by_stream)
    mid_all = mid_all.reshape(wt_size, seq_len, model_width)
    logits = matmul(normed_mid, router_full)
    logit_exp = jnp.exp(logits - jnp.max(logits, axis=-1, keepdims=True))
    router_probs = logit_exp / jnp.sum(logit_exp, axis=-1, keepdims=True)
    chosen_total = jnp.sum(hits_float * router_probs, axis=1, keepdims=True)
    gate_kept = jnp.where(kept, router_probs / chosen_total, 0.0)
    gate_mine = exchange(to_owner_rows(gate_kept), by_stream).reshape(wt_size, seq_len)

    def column_blocks(value):
        width = value.shape[1] // ctx_size
        blocks = value.reshape(tokens, ctx_size, width).transpose(1, 0, 2)
        return exchange(blocks, "ctx").reshape(seq_len, width)

    def pick_rows(table):
        return (
            jnp.einsum("wkt,wtd->wkd", place_low, table, preferred_element_type=jnp.float32)
            .astype(jnp.bfloat16)
            .reshape(wt_size * capacity, model_width)
        )

    filled = pick_rows(mid_all)
    if not small_plane:
        cot_all = gather(after(out_grad[0], filled), by_stream)
    cot_all = cot_all.reshape(wt_size, seq_len, model_width)
    mixed_columns = column_blocks(after(mixed_low, filled))
    gate_h = matmul(filled, expert_gate[0])
    up_h = matmul(filled, expert_up[0])
    sigma_h = jax.nn.sigmoid(gate_h)
    hidden_h = (gate_h * sigma_h * up_h).astype(jnp.bfloat16)
    result_rows = matmul(hidden_h, expert_down[0]).astype(jnp.bfloat16)
    cot_rows = pick_rows(cot_all)
    gate_rows = jnp.sum(jnp.where(place, gate_mine[:, None, :], 0.0), axis=2).reshape(-1)
    gate_cot_rows = jnp.sum(
        result_rows.astype(jnp.float32) * cot_rows.astype(jnp.float32), axis=1
    ).reshape(wt_size, capacity)
    gate_cot_mine = jnp.sum(jnp.where(place, gate_cot_rows[:, :, None], 0.0), axis=1)
    out_rows_cot = (gate_rows[:, None] * cot_rows.astype(jnp.float32)).astype(jnp.bfloat16)
    hidden_cot = contract_cols(out_rows_cot, expert_down[0])
    gate_cot_h = (hidden_cot * up_h * sigma_h * (1.0 + gate_h * (1.0 - sigma_h))).astype(
        jnp.bfloat16
    )
    up_cot_h = (hidden_cot * gate_h * sigma_h).astype(jnp.bfloat16)
    in_rows_cot = (
        contract_cols(gate_cot_h, expert_gate[0]) + contract_cols(up_cot_h, expert_up[0])
    ).astype(jnp.bfloat16)

    def add_pairs(table, stream_rows):
        return contract_rows(
            table.reshape(wt_size * capacity, seq_len), jnp.concatenate(stream_rows, axis=0)
        ).astype(jnp.bfloat16)

    mixed_rows = (gate_rows[:, None] * result_rows.astype(jnp.float32)).astype(jnp.bfloat16)
    in_rows_cot, mixed_columns, spread_low = lax.optimization_barrier(
        (in_rows_cot, mixed_columns, spread_low)
    )
    gate_cot = from_owner_rows(exchange(
        after(gate_cot_mine, in_rows_cot).reshape(devices, tokens), by_stream
    ))
    blocks_shape = (wt_size, capacity, model_width)
    stream_cots = turn(in_rows_cot.reshape(blocks_shape))
    returned_cot = scatter_sum(add_pairs(spread_low, stream_cots), "ctx")
    returned_cot = returned_cot.astype(jnp.float32)
    stream_mixed = turn(after(mixed_rows, stream_cots).reshape(blocks_shape))
    out_cot = out_grad[0].astype(jnp.float32)

    kept_cot = gate_cot * keep_float
    chosen_cot = kept_cot / chosen_total - jnp.sum(
        kept_cot * router_probs, axis=1, keepdims=True
    ) / (chosen_total * chosen_total)
    probs_cot = hits_float * chosen_cot
    logit_cot = (
        router_probs * (probs_cot - jnp.sum(router_probs * probs_cot, axis=1, keepdims=True))
    ).astype(jnp.bfloat16)
    mid_cot = returned_cot + contract_cols(logit_cot, router_full)
    mid_norm_cot, gain_moe_terms = norm_back(resid_mid, gain_moe, mid_cot)
    resid_cot = out_cot + mid_norm_cot
    attn_cot = resid_cot.astype(jnp.bfloat16)

    mixed_cot = contract_cols(attn_cot, out_full)
    attn_cot_all = gather(attn_cot, "ctx")
    query_cot_low, pair_cots, gain_query_terms = attend_back(
        query_sum,
        query_low,
        mixed_cot.astype(jnp.bfloat16),
        pair_sums,
        gains,
        tables,
        query_rows,
        key_rows,
    )
    query_columns = column_blocks(query_cot_low)
    filled, hidden_h = after((filled, hidden_h), query_cot_low)
    normed_mid = after(normed_mid, query_columns)
    grad_gate = contract_rows(filled, gate_cot_h)
    grad_up = contract_rows(filled, up_cot_h)
    grad_down = contract_rows(hidden_h, out_rows_cot)
    router_parts = exchange(contract_rows(normed_mid, logit_cot).reshape(devices, -1), both)
    grad_w_router = jnp.sum(router_parts, axis=0).reshape(w_router.shape)
    mixed_partial = add_pairs(after(spread_low, query_cot_low), stream_mixed)
    mixed_mine = scatter_sum(mixed_partial, "ctx").astype(jnp.float32)
    hidden_out = after(resid_mid, query_cot_low) + mixed_mine
    out_block = contract_rows(after(mixed_columns, query_cot_low), attn_cot_all)
    out_parts = turn(out_block.astype(jnp.bfloat16).reshape(wt_size, -1, model_width))
    pair_mine = scatter_sum(pair_cots, "ctx").reshape(tokens, key_heads, 2, head_dim)
    key_mine = pair_mine[:, :, 0].astype(jnp.float32)
    value_cot_low = pair_mine[:, :, 1].reshape(tokens, kv_width)
    key_pre, gain_key_terms = norm_back(
        key_sum,
        gain_key,
        rotate(key_mine, cosine_table, -sine_table),
    )
    key_cot_low = key_pre.reshape(tokens, kv_width).astype(jnp.bfloat16)
    pair_cot_low = jnp.concatenate([key_cot_low, value_cot_low], axis=1)

    def weight_parts(columns):
        width = columns.shape[1]
        block = contract_rows(normed_in_all, columns).astype(jnp.bfloat16)
        block = block.reshape(ctx_size, wt_size, -1, width).transpose(1, 0, 2, 3)
        return turn(block), block

    def weight_rows(parts):
        rows = exchange(add_up(parts).astype(jnp.bfloat16), "ctx")
        return rows.transpose(1, 0, 2).reshape(rows.shape[1], -1).astype(jnp.float32)

    query_parts, query_block = weight_parts(after(query_columns, (out_block, mixed_partial)))
    pair_parts, pair_block = weight_parts(column_blocks(after(pair_cot_low, query_block)))
    in_cot = contract_cols(after(query_cot_low, query_block), query_full) + contract_cols(
        pair_cot_low, side_weights[:, : 2 * kv_width]
    )
    query_parts = after(query_parts, (pair_block, in_cot))
    grad_w_query = weight_rows(query_parts)
    grad_w_out = add_up(after(out_parts, query_parts))
    grad_pair = weight_rows(after(pair_parts, query_parts))
    grad_w_key = grad_pair[:, :kv_width]
    grad_w_value = grad_pair[:, kv_width:]
    in_norm_cot, gain_attn_terms = norm_back(resid_in, gain_attn, in_cot)
    grad_in = resid_cot + in_norm_cot
    gain_sums = sum_everywhere(
        jnp.concatenate(
            [
                jnp.sum(gain_attn_terms, axis=0),
                jnp.sum(gain_query_terms, axis=0),
                jnp.sum(gain_key_terms, axis=(0, 1)),
                jnp.sum(gain_moe_terms, axis=0),
            ]
        )
    )
    grad_gain_attn = gain_sums[:model_width]
    grad_gain_query = gain_sums[model_width : model_width + head_dim]
    grad_gain_key = gain_sums[model_width + head_dim : model_width + 2 * head_dim]
    grad_gain_moe = gain_sums[model_width + 2 * head_dim :]
    return (
        hidden_out[None],
        grad_in[None],
        grad_gain_attn,
        grad_w_query,
        grad_w_key,
        grad_w_value,
        grad_gain_query,
        grad_gain_key,
        grad_w_out,
        grad_gain_moe,
        grad_w_router,
        grad_gate[None],
        grad_up[None],
        grad_down[None],
    )


def solution(mesh):
    in_specs = (
        P("wt", "ctx", None),
        P("wt", None),
        P("wt", "ctx", None),
        P(),
        P(("ctx", "wt"), None),
        P(("ctx", "wt"), None),
        P(("ctx", "wt"), None),
        P(),
        P(),
        P(("ctx", "wt"), None),
        P(),
        P(("ctx", "wt"), None),
        P(("ctx", "wt"), None, None),
        P(("ctx", "wt"), None, None),
        P(("ctx", "wt"), None, None),
        P("wt", "ctx", None),
    )
    out_specs = (
        P("wt", "ctx", None),
        P("wt", "ctx", None),
        P(),
        P(("ctx", "wt"), None),
        P(("ctx", "wt"), None),
        P(("ctx", "wt"), None),
        P(),
        P(),
        P(("ctx", "wt"), None),
        P(),
        P(("ctx", "wt"), None),
        P(("ctx", "wt"), None, None),
        P(("ctx", "wt"), None, None),
        P(("ctx", "wt"), None, None),
    )

    return jax.shard_map(
        on_device, mesh=mesh, in_specs=in_specs, out_specs=out_specs, check_vma=False
    )
```

```python
import functools
import math

import jax
import jax.numpy as jnp
from jax import lax
from jax.experimental import pallas as pl
from jax.experimental.pallas import tpu as pltpu
from jax.sharding import PartitionSpec as P


EPS = 1e-06
THETA = 1000000.0
MASKED = -1e30
MESH = pl.DeviceIdType.MESH


def norm_rows(value_rows, gain_vec):
    return (
        value_rows
        * lax.rsqrt(jnp.mean(value_rows * value_rows, axis=-1, keepdims=True) + EPS)
        * gain_vec
    )


def norm_back(value_rows, gain_vec, upstream):
    factor = lax.rsqrt(jnp.mean(value_rows * value_rows, axis=-1, keepdims=True) + EPS)
    normalized_input = value_rows * factor
    weighted = upstream * gain_vec
    inner_mean = jnp.mean(weighted * normalized_input, axis=-1, keepdims=True)
    return (factor * (weighted - normalized_input * inner_mean), upstream * normalized_input)


def rotary_tables(positions, head_dim):
    half_dim = head_dim // 2
    frequency = jnp.exp(
        jnp.arange(half_dim, dtype=jnp.float32) * (-2.0 * math.log(THETA) / head_dim)
    )
    angles = positions.astype(jnp.float32)[:, None] * frequency[None, :]
    angles = jnp.concatenate([angles, angles], axis=1)
    return (jnp.cos(angles)[:, None, :], jnp.sin(angles)[:, None, :])


def rotate(value_rows, cosine_table, sine_table):
    half_dim = value_rows.shape[-1] // 2
    turned = jnp.concatenate([-value_rows[..., half_dim:], value_rows[..., :half_dim]], axis=-1)
    return value_rows * cosine_table + turned * sine_table


def matmul(left_side, right_side):
    return jnp.dot(left_side, right_side, preferred_element_type=jnp.float32)


def contract_rows(left_side, right_side):
    return lax.dot_general(
        left_side, right_side, (((0,), (0,)), ((), ())), preferred_element_type=jnp.float32
    )


def contract_cols(left_side, right_side):
    return lax.dot_general(
        left_side, right_side, (((1,), (1,)), ((), ())), preferred_element_type=jnp.float32
    )


def spread_kernel(splits, streams_first, *refs):
    count = len(splits)
    ins, outs, stages = refs[:count], refs[count : 2 * count], refs[2 * count : 3 * count]
    send_sems, recv_sems, load_sems, store_sems = refs[3 * count :]
    ctx = lax.axis_index("ctx")
    z = lax.axis_index("wt")
    depth = lax.axis_size("wt")
    flip_y = ctx + 4 - 8 * (ctx // 4)
    step_x = 2 - 4 * ((ctx // 2) % 2)
    step_c = 1 - 2 * (ctx % 2)
    flip_x = ctx + step_x
    flip_xy = flip_y + step_x

    barrier = pltpu.get_barrier_semaphore()
    line = [lax.rem(z + d, depth) for d in range(1, depth)]
    for peer in line:
        pl.semaphore_signal(barrier, inc=1, device_id=(ctx, peer), device_id_type=MESH)
    for peer in (flip_x, flip_y, ctx + step_c):
        pl.semaphore_signal(barrier, inc=1, device_id=(peer, z), device_id_type=MESH)
    loads = []
    for k in range(count):
        loads.append(pltpu.make_async_copy(ins[k], stages[k], load_sems.at[k]))
        loads[k].start()
    pl.semaphore_wait(barrier, depth + 2)

    pieces = []
    for part in range(max(splits)):
        for k in range(count):
            if part < splits[k]:
                pieces.append((k, part))

    def group(k, owner, rows):
        view = outs[k]
        return view.at[:, owner, rows] if streams_first[k] else view.at[owner, :, rows]

    def block(k, rows):
        view = outs[k]
        return view.at[z, ctx, rows] if streams_first[k] else view.at[ctx, z, rows]

    def rows_of(k, part):
        size = ins[k].shape[0] // splits[k]
        return pl.ds(part * size, size)

    def send(number, slot, source, target, device):
        copy = pltpu.make_async_remote_copy(
            src_ref=source,
            dst_ref=target,
            send_sem=send_sems.at[number, slot],
            recv_sem=recv_sems.at[number, slot],
            device_id=device,
            device_id_type=MESH,
        )
        copy.start()
        return copy

    along = []
    for number, (k, part) in enumerate(pieces):
        rows = rows_of(k, part)
        along.append(
            [
                send(number, d, ins[k].at[rows], block(k, rows), (ctx, peer))
                for d, peer in enumerate(line)
            ]
        )
    stores = []
    for k in range(count):
        loads[k].wait()
        whole = pl.ds(0, ins[k].shape[0])
        stores.append(pltpu.make_async_copy(stages[k], block(k, whole), store_sems.at[k]))
        stores[k].start()
    for k in range(count):
        stores[k].wait()

    first_slot = depth - 1
    crossed, turned, shared = {}, {}, {}

    def owners(number):
        if number % 2:
            return flip_x, flip_y
        return flip_y, flip_x

    def cross(number):
        k, part = pieces[number]
        rows = rows_of(k, part)
        near, far = owners(number)
        for copy in along[number]:
            copy.wait_recv()
        mine = group(k, ctx, rows)
        crossed[number] = send(number, first_slot, mine, mine, (near, z))
        turned[number] = [send(number, first_slot + 1, mine, mine, (far, z))]
        shared[number] = [send(number, first_slot + 3, mine, mine, (ctx + step_c, z))]

    def turn_corner(number):
        k, part = pieces[number]
        rows = rows_of(k, part)
        near, far = owners(number)
        crossed[number].wait_recv()
        theirs = group(k, near, rows)
        turned[number].append(send(number, first_slot + 2, theirs, theirs, (far, z)))
        shared[number].append(send(number, first_slot + 4, theirs, theirs, (ctx + step_c, z)))

    def share(number):
        k, part = pieces[number]
        rows = rows_of(k, part)
        _, far = owners(number)
        for slot, (copy, owner) in enumerate(zip(turned[number], (far, flip_xy))):
            copy.wait_recv()
            theirs = group(k, owner, rows)
            shared[number].append(
                send(number, first_slot + 5 + slot, theirs, theirs, (ctx + step_c, z))
            )

    total = len(pieces)
    for step in range(total + 2):
        if step < total:
            cross(step)
        if 0 <= step - 1 < total:
            turn_corner(step - 1)
        if 0 <= step - 2 < total:
            share(step - 2)
    for number in range(total):
        for copy in shared[number]:
            copy.wait_recv()
        for copy in along[number] + [crossed[number]] + turned[number] + shared[number]:
            copy.wait_send()


def spread(values, splits, streams_first, channel):
    ctx_size, wt_size = lax.axis_size("ctx"), lax.axis_size("wt")
    total = sum(splits)
    heads = [(wt_size, ctx_size) if first else (ctx_size, wt_size) for first in streams_first]
    size = sum(value.size * value.dtype.itemsize for value in values)
    results = pl.pallas_call(
        functools.partial(spread_kernel, splits, streams_first),
        out_shape=[
            jax.ShapeDtypeStruct(head + value.shape, value.dtype)
            for head, value in zip(heads, values)
        ],
        in_specs=[pl.BlockSpec(memory_space=pl.ANY)] * len(values),
        out_specs=[pl.BlockSpec(memory_space=pl.ANY)] * len(values),
        scratch_shapes=[pltpu.VMEM(value.shape, value.dtype) for value in values]
        + [
            pltpu.SemaphoreType.DMA((total, wt_size + 6)),
            pltpu.SemaphoreType.DMA((total, wt_size + 6)),
            pltpu.SemaphoreType.DMA((len(values),)),
            pltpu.SemaphoreType.DMA((len(values),)),
        ],
        compiler_params=pltpu.CompilerParams(collective_id=channel, has_side_effects=True),
        cost_estimate=pl.CostEstimate(
            flops=0, bytes_accessed=2 * ctx_size * wt_size * size, transcendentals=0
        ),
    )(*values)
    return [result.reshape(-1, result.shape[-1]) for result in results]


def after(value, earlier):
    return lax.optimization_barrier((value, earlier))[0]


def stack_heads(block, first, head_dim, count):
    return jnp.concatenate(
        [block[:, (first + h) * head_dim : (first + h + 1) * head_dim] for h in range(count)],
        axis=0,
    )


def rotated(sums, gain_ref, cosine_ref, sine_ref):
    rows = norm_rows(sums, gain_ref[...])
    turned = pltpu.roll(rows, rows.shape[1] // 2, axis=1)
    return (rows * cosine_ref[...] + turned * sine_ref[...]).astype(jnp.bfloat16)


def attend_kernel(
    head_dim,
    together,
    query_ref,
    key_ref,
    value_ref,
    gain_ref,
    cosine_ref,
    sine_ref,
    key_gain_ref,
    key_cosine_ref,
    key_sine_ref,
    query_pos_ref,
    query_doc_ref,
    key_pos_ref,
    key_doc_ref,
    mixed_ref,
    query_low_ref,
    bias_ref,
):
    tokens = query_ref.shape[0]
    heads = query_ref.shape[1] // head_dim
    scale = head_dim ** (-0.5)

    @pl.when(pl.program_id(0) == 0)
    def _():
        allowed = (key_pos_ref[...] <= query_pos_ref[...]) & (
            key_doc_ref[...] == query_doc_ref[...]
        )
        bias_ref[...] = jnp.where(allowed, 0.0, MASKED)

    keys = rotated(key_ref[...], key_gain_ref, key_cosine_ref, key_sine_ref)
    values = value_ref[...].astype(jnp.bfloat16)
    for first in range(0, heads, together):
        for h in range(first, first + together):
            columns = slice(h * head_dim, (h + 1) * head_dim)
            query_low_ref[:, columns] = rotated(
                query_ref[:, columns], gain_ref, cosine_ref, sine_ref
            )
        queries = stack_heads(query_low_ref, first, head_dim, together)
        scores = contract_cols(queries, keys) * scale
        scores = scores + jnp.concatenate([bias_ref[...]] * together, axis=0)
        weights = jnp.exp(scores - jnp.max(scores, axis=1, keepdims=True))
        weights = weights / jnp.sum(weights, axis=1, keepdims=True)
        mixed = matmul(weights.astype(jnp.bfloat16), values)
        for h in range(together):
            columns = slice((first + h) * head_dim, (first + h + 1) * head_dim)
            mixed_ref[:, columns] = mixed[h * tokens : (h + 1) * tokens].astype(jnp.bfloat16)


def attend_back_kernel(
    head_dim,
    together,
    query_ref,
    query_low_ref,
    cot_ref,
    key_ref,
    value_ref,
    gain_ref,
    cosine_ref,
    sine_ref,
    key_gain_ref,
    key_cosine_ref,
    key_sine_ref,
    query_pos_ref,
    query_doc_ref,
    key_pos_ref,
    key_doc_ref,
    query_cot_ref,
    pair_cot_ref,
    gain_cot_ref,
    bias_ref,
    key_sum_ref,
    value_sum_ref,
):
    tokens = query_ref.shape[0]
    heads = query_ref.shape[1] // head_dim
    scale = head_dim ** (-0.5)

    @pl.when(pl.program_id(0) == 0)
    def _():
        allowed = (key_pos_ref[...] <= query_pos_ref[...]) & (
            key_doc_ref[...] == query_doc_ref[...]
        )
        bias_ref[...] = jnp.where(allowed, 0.0, MASKED)

    keys = rotated(key_ref[...], key_gain_ref, key_cosine_ref, key_sine_ref)
    values = value_ref[...].astype(jnp.bfloat16)
    for first in range(0, heads, together):
        queries = stack_heads(query_low_ref, first, head_dim, together)
        cots = stack_heads(cot_ref, first, head_dim, together)
        scores = contract_cols(keys, queries) * scale
        scores = scores + jnp.concatenate([bias_ref[...]] * together, axis=1)
        weights = jnp.exp(scores - jnp.max(scores, axis=0, keepdims=True))
        weights = weights / jnp.sum(weights, axis=0, keepdims=True)
        weight_cot = contract_cols(values, cots)
        delta = jnp.sum(weights * weight_cot, axis=0, keepdims=True)
        score_cot = (weights * (weight_cot - delta)).astype(jnp.bfloat16)
        value_part = matmul(weights.astype(jnp.bfloat16), cots)
        key_part = matmul(score_cot, queries)
        if first:
            value_sum_ref[...] += value_part
            key_sum_ref[...] += key_part
        else:
            value_sum_ref[...] = value_part
            key_sum_ref[...] = key_part
        query_part = contract_rows(score_cot, keys) * scale
        for h in range(together):
            columns = slice((first + h) * head_dim, (first + h + 1) * head_dim)
            upstream = query_part[h * tokens : (h + 1) * tokens]
            turned = pltpu.roll(upstream, head_dim // 2, axis=1)
            upstream = upstream * cosine_ref[...] - turned * sine_ref[...]
            rows_cot, terms = norm_back(query_ref[:, columns], gain_ref[...], upstream)
            query_cot_ref[:, columns] = rows_cot.astype(jnp.bfloat16)
            gain_cot_ref[first + h : first + h + 1, :] = jnp.sum(terms, axis=0, keepdims=True)
    pair_cot_ref[:, :head_dim] = (key_sum_ref[...] * scale).astype(jnp.bfloat16)
    pair_cot_ref[:, head_dim:] = value_sum_ref[...].astype(jnp.bfloat16)


def attend(query_sum, pair_sums, gains, tables, query_rows, key_rows):
    tokens, q_width = query_sum.shape
    seq_len, pair_width = pair_sums.shape
    head_dim = gains[0].shape[0]
    key_heads = pair_width // (2 * head_dim)
    group = q_width // key_heads
    whole = lambda shape: pl.BlockSpec(shape, lambda g: (0, 0))
    flops = 4 * tokens * seq_len * q_width
    return pl.pallas_call(
        functools.partial(attend_kernel, head_dim, 2),
        grid=(key_heads,),
        in_specs=[
            pl.BlockSpec((tokens, group), lambda g: (0, g)),
            pl.BlockSpec((seq_len, head_dim), lambda g: (0, g)),
            pl.BlockSpec((seq_len, head_dim), lambda g: (0, key_heads + g)),
            whole((1, head_dim)),
            whole((tokens, head_dim)),
            whole((tokens, head_dim)),
            whole((1, head_dim)),
            whole((seq_len, head_dim)),
            whole((seq_len, head_dim)),
            whole((tokens, 1)),
            whole((tokens, 1)),
            whole((1, seq_len)),
            whole((1, seq_len)),
        ],
        out_specs=[pl.BlockSpec((tokens, group), lambda g: (0, g))] * 2,
        out_shape=[jax.ShapeDtypeStruct((tokens, q_width), jnp.bfloat16)] * 2,
        scratch_shapes=[pltpu.VMEM((tokens, seq_len), jnp.float32)],
        compiler_params=pltpu.CompilerParams(vmem_limit_bytes=48 << 20),
        cost_estimate=pl.CostEstimate(
            flops=flops, bytes_accessed=8 * tokens * q_width, transcendentals=0
        ),
        name="attend",
    )(
        query_sum,
        pair_sums,
        pair_sums,
        gains[0][None, :],
        *tables[:2],
        gains[1][None, :],
        *tables[2:],
        *(row[:, None] for row in query_rows),
        *(row[None, :] for row in key_rows),
    )


def attend_back(query_sum, query_low, cots, pair_sums, gains, tables, query_rows, key_rows):
    tokens, q_width = query_sum.shape
    seq_len, pair_width = pair_sums.shape
    head_dim = gains[0].shape[0]
    key_heads = pair_width // (2 * head_dim)
    group = q_width // key_heads
    heads = group // head_dim
    whole = lambda shape: pl.BlockSpec(shape, lambda g: (0, 0))
    flops = 10 * tokens * seq_len * q_width
    return pl.pallas_call(
        functools.partial(attend_back_kernel, head_dim, 2),
        grid=(key_heads,),
        in_specs=[
            pl.BlockSpec((tokens, group), lambda g: (0, g)),
            pl.BlockSpec((tokens, group), lambda g: (0, g)),
            pl.BlockSpec((tokens, group), lambda g: (0, g)),
            pl.BlockSpec((seq_len, head_dim), lambda g: (0, g)),
            pl.BlockSpec((seq_len, head_dim), lambda g: (0, key_heads + g)),
            whole((1, head_dim)),
            whole((tokens, head_dim)),
            whole((tokens, head_dim)),
            whole((1, head_dim)),
            whole((seq_len, head_dim)),
            whole((seq_len, head_dim)),
            whole((1, tokens)),
            whole((1, tokens)),
            whole((seq_len, 1)),
            whole((seq_len, 1)),
        ],
        out_specs=[
            pl.BlockSpec((tokens, group), lambda g: (0, g)),
            pl.BlockSpec((seq_len, 2 * head_dim), lambda g: (0, g)),
            pl.BlockSpec((heads, head_dim), lambda g: (g, 0)),
        ],
        out_shape=[
            jax.ShapeDtypeStruct((tokens, q_width), jnp.bfloat16),
            jax.ShapeDtypeStruct((seq_len, pair_width), jnp.bfloat16),
            jax.ShapeDtypeStruct((key_heads * heads, head_dim), jnp.float32),
        ],
        scratch_shapes=[
            pltpu.VMEM((seq_len, tokens), jnp.float32),
            pltpu.VMEM((seq_len, head_dim), jnp.float32),
            pltpu.VMEM((seq_len, head_dim), jnp.float32),
        ],
        compiler_params=pltpu.CompilerParams(vmem_limit_bytes=56 << 20),
        cost_estimate=pl.CostEstimate(
            flops=flops, bytes_accessed=12 * tokens * q_width, transcendentals=0
        ),
        name="attend_back",
    )(
        query_sum,
        query_low,
        cots,
        pair_sums,
        pair_sums,
        gains[0][None, :],
        *tables[:2],
        gains[1][None, :],
        *tables[2:],
        *(row[None, :] for row in query_rows),
        *(row[:, None] for row in key_rows),
    )


def sum_everywhere(vector):
    devices = lax.axis_size("ctx") * lax.axis_size("wt")
    spread = jnp.broadcast_to(vector[None, :], (devices, vector.shape[0]))
    return jnp.sum(
        lax.all_to_all(spread, ("ctx", "wt"), split_axis=0, concat_axis=0, tiled=True), axis=0
    )


def on_device(
    hidden_in,
    doc_lengths,
    routes,
    gain_attn,
    w_query,
    key_weight,
    value_weight,
    gain_query,
    gain_key,
    w_out,
    gain_moe,
    w_router,
    expert_gate,
    expert_up,
    expert_down,
    out_grad,
):
    tokens = hidden_in.shape[1]
    model_width = hidden_in.shape[2]
    ctx_size = lax.axis_size("ctx")
    wt_size = lax.axis_size("wt")
    devices = ctx_size * wt_size
    seq_len = tokens * ctx_size
    head_dim = gain_query.shape[0]
    kv_width = key_weight.shape[1]
    key_heads = kv_width // head_dim
    expert_count = w_router.shape[1]
    top_count = routes.shape[2]
    assert expert_gate.shape[0] == 1 and expert_count == devices
    capacity = tokens * top_count // wt_size
    ctx_index = lax.axis_index("ctx")
    wt_index = lax.axis_index("wt")
    both = ("ctx", "wt")
    by_stream = ("wt", "ctx")

    def gather(value, axes):
        return lax.all_gather(value, axes, axis=0, tiled=True)

    def exchange(value, axes):
        return lax.all_to_all(value, axes, split_axis=0, concat_axis=0, tiled=True)

    def scatter_sum(value, axes):
        return lax.psum_scatter(value, axes, scatter_dimension=0, tiled=True)

    def cut(blocks):
        return [
            lax.dynamic_index_in_dim(blocks, lax.rem(wt_index + step, wt_size), keepdims=False)
            for step in range(wt_size)
        ]

    def pass_on(cuts):
        arrived = cuts[:1]
        for step in range(1, wt_size):
            pairs = [(w, (w + step) % wt_size) for w in range(wt_size)]
            arrived.append(lax.ppermute(cuts[step], "wt", pairs))
        return arrived

    def turn(blocks):
        return pass_on(cut(blocks))

    def add_up(blocks):
        return sum(block.astype(jnp.float32) for block in blocks)

    doc_ends = jnp.cumsum(doc_lengths[0])
    all_positions = jnp.arange(seq_len, dtype=jnp.int32)
    doc_all = jnp.sum((doc_ends[None, :] <= all_positions[:, None]).astype(jnp.int32), axis=1)
    first_pos = ctx_index * tokens
    my_positions = first_pos + jnp.arange(tokens, dtype=jnp.int32)
    my_docs = lax.dynamic_slice_in_dim(doc_all, first_pos, tokens)
    cosine_all, sine_all = rotary_tables(all_positions, head_dim)

    def mine_of(rows):
        return lax.dynamic_slice_in_dim(rows, first_pos, tokens)

    cosine_table, sine_table = mine_of(cosine_all), mine_of(sine_all)
    first_half = jnp.arange(head_dim) < head_dim // 2
    turned_all = jnp.where(first_half[None, :], -sine_all[:, 0, :], sine_all[:, 0, :])
    tables = (mine_of(cosine_all[:, 0, :]), mine_of(turned_all), cosine_all[:, 0, :], turned_all)

    expert_ids = jnp.arange(expert_count, dtype=jnp.int32)
    hits = jnp.sum((routes[0][:, :, None] == expert_ids[None, None, :]).astype(jnp.int32), axis=1)
    local_rank = jnp.cumsum(hits, axis=0) - hits
    assert expert_count <= tokens
    counts = jnp.pad(jnp.sum(hits, axis=0), (0, tokens - expert_count))
    plane_mine = jnp.concatenate(
        [
            hits.T.reshape(ctx_size, wt_size, tokens),
            jnp.broadcast_to(counts, (ctx_size, 1, tokens)),
        ],
        axis=1,
    )
    plane = exchange(plane_mine, "ctx")
    earlier = jnp.arange(ctx_size, dtype=jnp.int32)[:, None] < ctx_index
    offsets = jnp.sum(jnp.where(earlier, plane[:, wt_size, :expert_count], 0), axis=0)
    kept = (hits > 0) & (local_rank + offsets[None, :] < capacity)
    rank_lines = exchange(
        jnp.where(kept, local_rank, -1).T.reshape(ctx_size, wt_size, tokens).transpose(1, 0, 2),
        "wt",
    )
    keep_float = kept.astype(jnp.float32)
    hits_float = hits.astype(jnp.float32)

    def to_owner_rows(table):
        return table.reshape(tokens, ctx_size, wt_size).transpose(2, 1, 0).reshape(devices, tokens)

    def from_owner_rows(table):
        return table.reshape(wt_size, ctx_size, tokens).transpose(2, 1, 0).reshape(tokens, devices)

    hit_mine = exchange(to_owner_rows(hits), by_stream).reshape(wt_size, seq_len)
    slot_mine = jnp.cumsum(hit_mine, axis=1) - hit_mine
    slot_mine = jnp.where((hit_mine > 0) & (slot_mine < capacity), slot_mine, -1)
    send_slots = 2 * tokens * top_count // expert_count
    send_ids = jnp.arange(send_slots, dtype=jnp.int32)
    block_hits = jnp.sum(hit_mine.reshape(wt_size, ctx_size, tokens), axis=2)
    block_first = jnp.cumsum(block_hits, axis=1) - block_hits
    slot_ids = jnp.arange(capacity, dtype=jnp.int32)
    place = slot_mine[:, None, :] == slot_ids[None, :, None]
    place_low = after(place.astype(jnp.bfloat16), rank_lines)
    hit_plane = plane[:, :wt_size].transpose(1, 0, 2).reshape(wt_size, seq_len)
    hit_plane = hit_plane[(wt_index - jnp.arange(wt_size)) % wt_size]
    slot_plane = jnp.cumsum(hit_plane, axis=1) - hit_plane
    slot_plane = jnp.where((hit_plane > 0) & (slot_plane < capacity), slot_plane, -1)
    spread_low = (slot_plane[:, None, :] == slot_ids[None, :, None]).astype(jnp.bfloat16)

    resid_in = hidden_in[0].astype(jnp.float32)
    normed_in = norm_rows(resid_in, gain_attn).astype(jnp.bfloat16)
    router_pad = -expert_count % head_dim
    normed_in_all = gather(normed_in, "ctx")
    side_mine = jnp.concatenate(
        [key_weight, value_weight, jnp.pad(w_router, ((0, 0), (0, router_pad)))], axis=1
    )
    small_plane = ctx_size == 8
    if small_plane:
        side_weights, query_full, out_full = spread(
            [side_mine, w_query, w_out], (2, 4, 4), (False,) * 3, 1
        )
    else:
        side_weights = gather(side_mine, both)
        query_full = gather(w_query, both)
        out_full = gather(w_out, both)
    router_full = side_weights[:, 2 * kv_width : 2 * kv_width + expert_count]
    pair_sums = lax.optimization_barrier(
        matmul(normed_in_all, side_weights[:, : 2 * kv_width])
    )
    key_sum = mine_of(pair_sums)[:, :kv_width].reshape(tokens, key_heads, head_dim)
    if small_plane:
        cot_all = gather(after(out_grad[0], query_full), by_stream)
    query_sum = lax.optimization_barrier(matmul(normed_in, query_full))
    gains = (gain_query, gain_key)
    query_rows, key_rows = (my_positions, my_docs), (all_positions, doc_all)
    mixed_low, query_low = attend(query_sum, pair_sums, gains, tables, query_rows, key_rows)
    resid_mid = resid_in + matmul(mixed_low, out_full)
    normed_mid = norm_rows(resid_mid, gain_moe).astype(jnp.bfloat16)

    if small_plane:
        (mid_all,) = spread([normed_mid], (4,), (True,), 2)
    else:
        mid_all = gather(normed_mid, by_stream)
    mid_all = mid_all.reshape(wt_size, seq_len, model_width)
    logits = matmul(normed_mid, router_full)
    logit_exp = jnp.exp(logits - jnp.max(logits, axis=-1, keepdims=True))
    router_probs = logit_exp / jnp.sum(logit_exp, axis=-1, keepdims=True)
    chosen_total = jnp.sum(hits_float * router_probs, axis=1, keepdims=True)
    gate_kept = jnp.where(kept, router_probs / chosen_total, 0.0)
    gate_mine = exchange(to_owner_rows(gate_kept), by_stream).reshape(wt_size, seq_len)

    def column_blocks(value):
        width = value.shape[1] // ctx_size
        blocks = value.reshape(tokens, ctx_size, width).transpose(1, 0, 2)
        return exchange(blocks, "ctx").reshape(seq_len, width)

    def pick_rows(table):
        return (
            jnp.einsum("wkt,wtd->wkd", place_low, table, preferred_element_type=jnp.float32)
            .astype(jnp.bfloat16)
            .reshape(wt_size * capacity, model_width)
        )

    filled = pick_rows(mid_all)
    if not small_plane:
        cot_all = gather(after(out_grad[0], filled), by_stream)
    cot_all = cot_all.reshape(wt_size, seq_len, model_width)
    mixed_columns = column_blocks(after(mixed_low, filled))
    gate_h = matmul(filled, expert_gate[0])
    up_h = matmul(filled, expert_up[0])
    sigma_h = jax.nn.sigmoid(gate_h)
    hidden_h = (gate_h * sigma_h * up_h).astype(jnp.bfloat16)
    result_rows = matmul(hidden_h, expert_down[0]).astype(jnp.bfloat16)
    cot_rows = pick_rows(cot_all)
    gate_rows = jnp.sum(jnp.where(place, gate_mine[:, None, :], 0.0), axis=2).reshape(-1)
    gate_cot_rows = jnp.sum(
        result_rows.astype(jnp.float32) * cot_rows.astype(jnp.float32), axis=1
    ).reshape(wt_size, capacity)
    gate_cot_mine = jnp.sum(jnp.where(place, gate_cot_rows[:, :, None], 0.0), axis=1)
    out_rows_cot = (gate_rows[:, None] * cot_rows.astype(jnp.float32)).astype(jnp.bfloat16)
    hidden_cot = contract_cols(out_rows_cot, expert_down[0])
    gate_cot_h = (hidden_cot * up_h * sigma_h * (1.0 + gate_h * (1.0 - sigma_h))).astype(
        jnp.bfloat16
    )
    up_cot_h = (hidden_cot * gate_h * sigma_h).astype(jnp.bfloat16)
    in_rows_cot = (
        contract_cols(gate_cot_h, expert_gate[0]) + contract_cols(up_cot_h, expert_up[0])
    ).astype(jnp.bfloat16)

    def add_pairs(table, stream_rows):
        return contract_rows(
            table.reshape(wt_size * capacity, seq_len), jnp.concatenate(stream_rows, axis=0)
        ).astype(jnp.bfloat16)

    mixed_rows = (gate_rows[:, None] * result_rows.astype(jnp.float32)).astype(jnp.bfloat16)
    gate_cot = exchange(after(gate_cot_mine, mixed_columns).reshape(devices, tokens), by_stream)
    in_rows_cot, gate_cot, mixed_columns = lax.optimization_barrier(
        (in_rows_cot, gate_cot, mixed_columns)
    )
    gate_cot = from_owner_rows(gate_cot)
    blocks_shape = (wt_size, capacity, -1)

    half = model_width // 2
    stream_cots = turn(in_rows_cot[:, :half].reshape(blocks_shape))
    send_slot = jnp.where(
        send_ids[None, None, :] < block_hits[:, :, None],
        block_first[:, :, None] + send_ids[None, None, :],
        -1,
    ).reshape(wt_size, ctx_size * send_slots)
    send_low = (send_slot[:, :, None] == slot_ids[None, None, :]).astype(jnp.bfloat16)
    plane_sent = (
        jnp.einsum(
            "wjk,wkd->wjd",
            send_low,
            in_rows_cot[:, half:].reshape(blocks_shape),
            preferred_element_type=jnp.float32,
        )
        .astype(jnp.bfloat16)
        .reshape(wt_size, ctx_size, send_slots, half)
        .transpose(1, 0, 2, 3)
    )
    plane_cots = exchange(plane_sent, "ctx")
    first_part = scatter_sum(add_pairs(spread_low, stream_cots), "ctx")
    line_low = (rank_lines[:, :, :, None] == send_ids).astype(jnp.bfloat16)
    line_sent = jnp.einsum(
        "sctj,csjd->std", line_low, plane_cots, preferred_element_type=jnp.float32
    ).astype(jnp.bfloat16)
    line_cots = turn(line_sent)
    mixed_rows = after(mixed_rows, line_sent).reshape(blocks_shape)
    mixed_cuts = cut(mixed_rows)
    stream_mixed = pass_on(mixed_cuts)
    returned_cot = after(
        jnp.concatenate([first_part.astype(jnp.float32), add_up(line_cots)], axis=1), mixed_cuts
    )
    out_cot = out_grad[0].astype(jnp.float32)

    kept_cot = gate_cot * keep_float
    chosen_cot = kept_cot / chosen_total - jnp.sum(
        kept_cot * router_probs, axis=1, keepdims=True
    ) / (chosen_total * chosen_total)
    probs_cot = hits_float * chosen_cot
    logit_cot = (
        router_probs * (probs_cot - jnp.sum(router_probs * probs_cot, axis=1, keepdims=True))
    ).astype(jnp.bfloat16)
    mid_cot = returned_cot + contract_cols(logit_cot, router_full)
    mid_norm_cot, gain_moe_terms = norm_back(resid_mid, gain_moe, mid_cot)
    resid_cot = out_cot + mid_norm_cot
    attn_cot = resid_cot.astype(jnp.bfloat16)

    mixed_cot = contract_cols(attn_cot, out_full)
    attn_cot_all = gather(attn_cot, "ctx")
    query_cot_low, pair_cots, gain_query_terms = attend_back(
        query_sum,
        query_low,
        mixed_cot.astype(jnp.bfloat16),
        pair_sums,
        gains,
        tables,
        query_rows,
        key_rows,
    )
    query_columns = column_blocks(query_cot_low)
    filled, hidden_h = after((filled, hidden_h), query_cot_low)
    normed_mid = after(normed_mid, query_columns)
    grad_gate = contract_rows(filled, gate_cot_h)
    grad_up = contract_rows(filled, up_cot_h)
    grad_down = contract_rows(hidden_h, out_rows_cot)
    router_parts = exchange(contract_rows(normed_mid, logit_cot).reshape(devices, -1), both)
    grad_w_router = jnp.sum(router_parts, axis=0).reshape(w_router.shape)
    mixed_partial = add_pairs(after(spread_low, query_cot_low), stream_mixed)
    mixed_mine = scatter_sum(mixed_partial, "ctx").astype(jnp.float32)
    hidden_out = after(resid_mid, query_cot_low) + mixed_mine
    out_block = contract_rows(after(mixed_columns, query_cot_low), attn_cot_all)
    out_parts = turn(out_block.astype(jnp.bfloat16).reshape(wt_size, -1, model_width))
    pair_mine = scatter_sum(pair_cots, "ctx").reshape(tokens, key_heads, 2, head_dim)
    key_mine = pair_mine[:, :, 0].astype(jnp.float32)
    value_cot_low = pair_mine[:, :, 1].reshape(tokens, kv_width)
    key_pre, gain_key_terms = norm_back(
        key_sum,
        gain_key,
        rotate(key_mine, cosine_table, -sine_table),
    )
    key_cot_low = key_pre.reshape(tokens, kv_width).astype(jnp.bfloat16)
    pair_cot_low = jnp.concatenate([key_cot_low, value_cot_low], axis=1)

    def weight_parts(columns):
        width = columns.shape[1]
        block = contract_rows(normed_in_all, columns).astype(jnp.bfloat16)
        block = block.reshape(ctx_size, wt_size, -1, width).transpose(1, 0, 2, 3)
        return turn(block), block

    def weight_rows(parts):
        rows = exchange(add_up(parts).astype(jnp.bfloat16), "ctx")
        return rows.transpose(1, 0, 2).reshape(rows.shape[1], -1).astype(jnp.float32)

    query_parts, query_block = weight_parts(after(query_columns, (out_block, mixed_partial)))
    pair_parts, pair_block = weight_parts(column_blocks(after(pair_cot_low, query_block)))
    in_cot = contract_cols(after(query_cot_low, query_block), query_full) + contract_cols(
        pair_cot_low, side_weights[:, : 2 * kv_width]
    )
    query_parts = after(query_parts, (pair_block, in_cot))
    grad_w_query = weight_rows(query_parts)
    grad_w_out = add_up(after(out_parts, query_parts))
    grad_pair = weight_rows(after(pair_parts, query_parts))
    grad_w_key = grad_pair[:, :kv_width]
    grad_w_value = grad_pair[:, kv_width:]
    in_norm_cot, gain_attn_terms = norm_back(resid_in, gain_attn, in_cot)
    grad_in = resid_cot + in_norm_cot
    gain_sums = sum_everywhere(
        jnp.concatenate(
            [
                jnp.sum(gain_attn_terms, axis=0),
                jnp.sum(gain_query_terms, axis=0),
                jnp.sum(gain_key_terms, axis=(0, 1)),
                jnp.sum(gain_moe_terms, axis=0),
            ]
        )
    )
    grad_gain_attn = gain_sums[:model_width]
    grad_gain_query = gain_sums[model_width : model_width + head_dim]
    grad_gain_key = gain_sums[model_width + head_dim : model_width + 2 * head_dim]
    grad_gain_moe = gain_sums[model_width + 2 * head_dim :]
    return (
        hidden_out[None],
        grad_in[None],
        grad_gain_attn,
        grad_w_query,
        grad_w_key,
        grad_w_value,
        grad_gain_query,
        grad_gain_key,
        grad_w_out,
        grad_gain_moe,
        grad_w_router,
        grad_gate[None],
        grad_up[None],
        grad_down[None],
    )


def solution(mesh):
    in_specs = (
        P("wt", "ctx", None),
        P("wt", None),
        P("wt", "ctx", None),
        P(),
        P(("ctx", "wt"), None),
        P(("ctx", "wt"), None),
        P(("ctx", "wt"), None),
        P(),
        P(),
        P(("ctx", "wt"), None),
        P(),
        P(("ctx", "wt"), None),
        P(("ctx", "wt"), None, None),
        P(("ctx", "wt"), None, None),
        P(("ctx", "wt"), None, None),
        P("wt", "ctx", None),
    )
    out_specs = (
        P("wt", "ctx", None),
        P("wt", "ctx", None),
        P(),
        P(("ctx", "wt"), None),
        P(("ctx", "wt"), None),
        P(("ctx", "wt"), None),
        P(),
        P(),
        P(("ctx", "wt"), None),
        P(),
        P(("ctx", "wt"), None),
        P(("ctx", "wt"), None, None),
        P(("ctx", "wt"), None, None),
        P(("ctx", "wt"), None, None),
    )

    return jax.shard_map(
        on_device, mesh=mesh, in_specs=in_specs, out_specs=out_specs, check_vma=False
    )
```

```python
import functools
import math

import jax
import jax.numpy as jnp
from jax import lax
from jax.experimental import pallas as pl
from jax.experimental.pallas import tpu as pltpu
from jax.sharding import PartitionSpec as P


EPS = 1e-06
THETA = 1000000.0
MASKED = -1e30
MESH = pl.DeviceIdType.MESH


def norm_rows(value_rows, gain_vec):
    return (
        value_rows
        * lax.rsqrt(jnp.mean(value_rows * value_rows, axis=-1, keepdims=True) + EPS)
        * gain_vec
    )


def norm_back(value_rows, gain_vec, upstream):
    factor = lax.rsqrt(jnp.mean(value_rows * value_rows, axis=-1, keepdims=True) + EPS)
    normalized_input = value_rows * factor
    weighted = upstream * gain_vec
    inner_mean = jnp.mean(weighted * normalized_input, axis=-1, keepdims=True)
    return (factor * (weighted - normalized_input * inner_mean), upstream * normalized_input)


def rotary_tables(positions, head_dim):
    half_dim = head_dim // 2
    frequency = jnp.exp(
        jnp.arange(half_dim, dtype=jnp.float32) * (-2.0 * math.log(THETA) / head_dim)
    )
    angles = positions.astype(jnp.float32)[:, None] * frequency[None, :]
    angles = jnp.concatenate([angles, angles], axis=1)
    return (jnp.cos(angles)[:, None, :], jnp.sin(angles)[:, None, :])


def rotate(value_rows, cosine_table, sine_table):
    half_dim = value_rows.shape[-1] // 2
    turned = jnp.concatenate([-value_rows[..., half_dim:], value_rows[..., :half_dim]], axis=-1)
    return value_rows * cosine_table + turned * sine_table


def matmul(left_side, right_side):
    return jnp.dot(left_side, right_side, preferred_element_type=jnp.float32)


def contract_rows(left_side, right_side):
    return lax.dot_general(
        left_side, right_side, (((0,), (0,)), ((), ())), preferred_element_type=jnp.float32
    )


def contract_cols(left_side, right_side):
    return lax.dot_general(
        left_side, right_side, (((1,), (1,)), ((), ())), preferred_element_type=jnp.float32
    )


def spread_kernel(splits, streams_first, *refs):
    count = len(splits)
    ins, outs, stages = refs[:count], refs[count : 2 * count], refs[2 * count : 3 * count]
    send_sems, recv_sems, load_sems, store_sems = refs[3 * count :]
    ctx = lax.axis_index("ctx")
    z = lax.axis_index("wt")
    depth = lax.axis_size("wt")
    flip_y = ctx + 4 - 8 * (ctx // 4)
    step_x = 2 - 4 * ((ctx // 2) % 2)
    step_c = 1 - 2 * (ctx % 2)
    flip_x = ctx + step_x
    flip_xy = flip_y + step_x

    barrier = pltpu.get_barrier_semaphore()
    line = [lax.rem(z + d, depth) for d in range(1, depth)]
    for peer in line:
        pl.semaphore_signal(barrier, inc=1, device_id=(ctx, peer), device_id_type=MESH)
    for peer in (flip_x, flip_y, ctx + step_c):
        pl.semaphore_signal(barrier, inc=1, device_id=(peer, z), device_id_type=MESH)
    loads = []
    for k in range(count):
        loads.append(pltpu.make_async_copy(ins[k], stages[k], load_sems.at[k]))
        loads[k].start()
    pl.semaphore_wait(barrier, depth + 2)

    pieces = []
    for part in range(max(splits)):
        for k in range(count):
            if part < splits[k]:
                pieces.append((k, part))

    def group(k, owner, rows):
        view = outs[k]
        return view.at[:, owner, rows] if streams_first[k] else view.at[owner, :, rows]

    def block(k, rows):
        view = outs[k]
        return view.at[z, ctx, rows] if streams_first[k] else view.at[ctx, z, rows]

    def rows_of(k, part):
        size = ins[k].shape[0] // splits[k]
        return pl.ds(part * size, size)

    def send(number, slot, source, target, device):
        copy = pltpu.make_async_remote_copy(
            src_ref=source,
            dst_ref=target,
            send_sem=send_sems.at[number, slot],
            recv_sem=recv_sems.at[number, slot],
            device_id=device,
            device_id_type=MESH,
        )
        copy.start()
        return copy

    along = []
    for number, (k, part) in enumerate(pieces):
        rows = rows_of(k, part)
        along.append(
            [
                send(number, d, ins[k].at[rows], block(k, rows), (ctx, peer))
                for d, peer in enumerate(line)
            ]
        )
    stores = []
    for k in range(count):
        loads[k].wait()
        whole = pl.ds(0, ins[k].shape[0])
        stores.append(pltpu.make_async_copy(stages[k], block(k, whole), store_sems.at[k]))
        stores[k].start()
    for k in range(count):
        stores[k].wait()

    first_slot = depth - 1
    crossed, turned, shared = {}, {}, {}

    def owners(number):
        if number % 2:
            return flip_x, flip_y
        return flip_y, flip_x

    def cross(number):
        k, part = pieces[number]
        rows = rows_of(k, part)
        near, far = owners(number)
        for copy in along[number]:
            copy.wait_recv()
        mine = group(k, ctx, rows)
        crossed[number] = send(number, first_slot, mine, mine, (near, z))
        turned[number] = [send(number, first_slot + 1, mine, mine, (far, z))]
        shared[number] = [send(number, first_slot + 3, mine, mine, (ctx + step_c, z))]

    def turn_corner(number):
        k, part = pieces[number]
        rows = rows_of(k, part)
        near, far = owners(number)
        crossed[number].wait_recv()
        theirs = group(k, near, rows)
        turned[number].append(send(number, first_slot + 2, theirs, theirs, (far, z)))
        shared[number].append(send(number, first_slot + 4, theirs, theirs, (ctx + step_c, z)))

    def share(number):
        k, part = pieces[number]
        rows = rows_of(k, part)
        _, far = owners(number)
        for slot, (copy, owner) in enumerate(zip(turned[number], (far, flip_xy))):
            copy.wait_recv()
            theirs = group(k, owner, rows)
            shared[number].append(
                send(number, first_slot + 5 + slot, theirs, theirs, (ctx + step_c, z))
            )

    total = len(pieces)
    for step in range(total + 2):
        if step < total:
            cross(step)
        if 0 <= step - 1 < total:
            turn_corner(step - 1)
        if 0 <= step - 2 < total:
            share(step - 2)
    for number in range(total):
        for copy in shared[number]:
            copy.wait_recv()
        for copy in along[number] + [crossed[number]] + turned[number] + shared[number]:
            copy.wait_send()


def spread(values, splits, streams_first, channel):
    ctx_size, wt_size = lax.axis_size("ctx"), lax.axis_size("wt")
    total = sum(splits)
    heads = [(wt_size, ctx_size) if first else (ctx_size, wt_size) for first in streams_first]
    size = sum(value.size * value.dtype.itemsize for value in values)
    results = pl.pallas_call(
        functools.partial(spread_kernel, splits, streams_first),
        out_shape=[
            jax.ShapeDtypeStruct(head + value.shape, value.dtype)
            for head, value in zip(heads, values)
        ],
        in_specs=[pl.BlockSpec(memory_space=pl.ANY)] * len(values),
        out_specs=[pl.BlockSpec(memory_space=pl.ANY)] * len(values),
        scratch_shapes=[pltpu.VMEM(value.shape, value.dtype) for value in values]
        + [
            pltpu.SemaphoreType.DMA((total, wt_size + 6)),
            pltpu.SemaphoreType.DMA((total, wt_size + 6)),
            pltpu.SemaphoreType.DMA((len(values),)),
            pltpu.SemaphoreType.DMA((len(values),)),
        ],
        compiler_params=pltpu.CompilerParams(collective_id=channel, has_side_effects=True),
        cost_estimate=pl.CostEstimate(
            flops=0, bytes_accessed=2 * ctx_size * wt_size * size, transcendentals=0
        ),
    )(*values)
    return [result.reshape(-1, result.shape[-1]) for result in results]


def after(value, earlier):
    return lax.optimization_barrier((value, earlier))[0]


def stack_heads(block, first, head_dim, count):
    return jnp.concatenate(
        [block[:, (first + h) * head_dim : (first + h + 1) * head_dim] for h in range(count)],
        axis=0,
    )


def rotated(sums, gain_ref, cosine_ref, sine_ref):
    rows = norm_rows(sums, gain_ref[...])
    turned = pltpu.roll(rows, rows.shape[1] // 2, axis=1)
    return (rows * cosine_ref[...] + turned * sine_ref[...]).astype(jnp.bfloat16)


def attend_kernel(
    head_dim,
    together,
    query_ref,
    key_ref,
    value_ref,
    gain_ref,
    cosine_ref,
    sine_ref,
    key_gain_ref,
    key_cosine_ref,
    key_sine_ref,
    query_pos_ref,
    query_doc_ref,
    key_pos_ref,
    key_doc_ref,
    mixed_ref,
    query_low_ref,
    bias_ref,
):
    tokens = query_ref.shape[0]
    heads = query_ref.shape[1] // head_dim
    scale = head_dim ** (-0.5)

    @pl.when(pl.program_id(0) == 0)
    def _():
        allowed = (key_pos_ref[...] <= query_pos_ref[...]) & (
            key_doc_ref[...] == query_doc_ref[...]
        )
        bias_ref[...] = jnp.where(allowed, 0.0, MASKED)

    keys = rotated(key_ref[...], key_gain_ref, key_cosine_ref, key_sine_ref)
    values = value_ref[...].astype(jnp.bfloat16)
    for first in range(0, heads, together):
        for h in range(first, first + together):
            columns = slice(h * head_dim, (h + 1) * head_dim)
            query_low_ref[:, columns] = rotated(
                query_ref[:, columns], gain_ref, cosine_ref, sine_ref
            )
        queries = stack_heads(query_low_ref, first, head_dim, together)
        scores = contract_cols(queries, keys) * scale
        scores = scores + jnp.concatenate([bias_ref[...]] * together, axis=0)
        weights = jnp.exp(scores - jnp.max(scores, axis=1, keepdims=True))
        weights = weights / jnp.sum(weights, axis=1, keepdims=True)
        mixed = matmul(weights.astype(jnp.bfloat16), values)
        for h in range(together):
            columns = slice((first + h) * head_dim, (first + h + 1) * head_dim)
            mixed_ref[:, columns] = mixed[h * tokens : (h + 1) * tokens].astype(jnp.bfloat16)


def attend_back_kernel(
    head_dim,
    together,
    query_ref,
    query_low_ref,
    cot_ref,
    key_ref,
    value_ref,
    gain_ref,
    cosine_ref,
    sine_ref,
    key_gain_ref,
    key_cosine_ref,
    key_sine_ref,
    query_pos_ref,
    query_doc_ref,
    key_pos_ref,
    key_doc_ref,
    query_cot_ref,
    pair_cot_ref,
    gain_cot_ref,
    bias_ref,
    key_sum_ref,
    value_sum_ref,
):
    tokens = query_ref.shape[0]
    heads = query_ref.shape[1] // head_dim
    scale = head_dim ** (-0.5)

    @pl.when(pl.program_id(0) == 0)
    def _():
        allowed = (key_pos_ref[...] <= query_pos_ref[...]) & (
            key_doc_ref[...] == query_doc_ref[...]
        )
        bias_ref[...] = jnp.where(allowed, 0.0, MASKED)

    keys = rotated(key_ref[...], key_gain_ref, key_cosine_ref, key_sine_ref)
    values = value_ref[...].astype(jnp.bfloat16)
    for first in range(0, heads, together):
        queries = stack_heads(query_low_ref, first, head_dim, together)
        cots = stack_heads(cot_ref, first, head_dim, together)
        scores = contract_cols(keys, queries) * scale
        scores = scores + jnp.concatenate([bias_ref[...]] * together, axis=1)
        weights = jnp.exp(scores - jnp.max(scores, axis=0, keepdims=True))
        weights = weights / jnp.sum(weights, axis=0, keepdims=True)
        weight_cot = contract_cols(values, cots)
        delta = jnp.sum(weights * weight_cot, axis=0, keepdims=True)
        score_cot = (weights * (weight_cot - delta)).astype(jnp.bfloat16)
        value_part = matmul(weights.astype(jnp.bfloat16), cots)
        key_part = matmul(score_cot, queries)
        if first:
            value_sum_ref[...] += value_part
            key_sum_ref[...] += key_part
        else:
            value_sum_ref[...] = value_part
            key_sum_ref[...] = key_part
        query_part = contract_rows(score_cot, keys) * scale
        for h in range(together):
            columns = slice((first + h) * head_dim, (first + h + 1) * head_dim)
            upstream = query_part[h * tokens : (h + 1) * tokens]
            turned = pltpu.roll(upstream, head_dim // 2, axis=1)
            upstream = upstream * cosine_ref[...] - turned * sine_ref[...]
            rows_cot, terms = norm_back(query_ref[:, columns], gain_ref[...], upstream)
            query_cot_ref[:, columns] = rows_cot.astype(jnp.bfloat16)
            gain_cot_ref[first + h : first + h + 1, :] = jnp.sum(terms, axis=0, keepdims=True)
    pair_cot_ref[:, :head_dim] = (key_sum_ref[...] * scale).astype(jnp.bfloat16)
    pair_cot_ref[:, head_dim:] = value_sum_ref[...].astype(jnp.bfloat16)


def attend(query_sum, pair_sums, gains, tables, query_rows, key_rows):
    tokens, q_width = query_sum.shape
    seq_len, pair_width = pair_sums.shape
    head_dim = gains[0].shape[0]
    key_heads = pair_width // (2 * head_dim)
    group = q_width // key_heads
    whole = lambda shape: pl.BlockSpec(shape, lambda g: (0, 0))
    flops = 4 * tokens * seq_len * q_width
    return pl.pallas_call(
        functools.partial(attend_kernel, head_dim, 2),
        grid=(key_heads,),
        in_specs=[
            pl.BlockSpec((tokens, group), lambda g: (0, g)),
            pl.BlockSpec((seq_len, head_dim), lambda g: (0, g)),
            pl.BlockSpec((seq_len, head_dim), lambda g: (0, key_heads + g)),
            whole((1, head_dim)),
            whole((tokens, head_dim)),
            whole((tokens, head_dim)),
            whole((1, head_dim)),
            whole((seq_len, head_dim)),
            whole((seq_len, head_dim)),
            whole((tokens, 1)),
            whole((tokens, 1)),
            whole((1, seq_len)),
            whole((1, seq_len)),
        ],
        out_specs=[pl.BlockSpec((tokens, group), lambda g: (0, g))] * 2,
        out_shape=[jax.ShapeDtypeStruct((tokens, q_width), jnp.bfloat16)] * 2,
        scratch_shapes=[pltpu.VMEM((tokens, seq_len), jnp.float32)],
        compiler_params=pltpu.CompilerParams(vmem_limit_bytes=48 << 20),
        cost_estimate=pl.CostEstimate(
            flops=flops, bytes_accessed=8 * tokens * q_width, transcendentals=0
        ),
        name="attend",
    )(
        query_sum,
        pair_sums,
        pair_sums,
        gains[0][None, :],
        *tables[:2],
        gains[1][None, :],
        *tables[2:],
        *(row[:, None] for row in query_rows),
        *(row[None, :] for row in key_rows),
    )


def attend_back(query_sum, query_low, cots, pair_sums, gains, tables, query_rows, key_rows):
    tokens, q_width = query_sum.shape
    seq_len, pair_width = pair_sums.shape
    head_dim = gains[0].shape[0]
    key_heads = pair_width // (2 * head_dim)
    group = q_width // key_heads
    heads = group // head_dim
    whole = lambda shape: pl.BlockSpec(shape, lambda g: (0, 0))
    flops = 10 * tokens * seq_len * q_width
    return pl.pallas_call(
        functools.partial(attend_back_kernel, head_dim, 2),
        grid=(key_heads,),
        in_specs=[
            pl.BlockSpec((tokens, group), lambda g: (0, g)),
            pl.BlockSpec((tokens, group), lambda g: (0, g)),
            pl.BlockSpec((tokens, group), lambda g: (0, g)),
            pl.BlockSpec((seq_len, head_dim), lambda g: (0, g)),
            pl.BlockSpec((seq_len, head_dim), lambda g: (0, key_heads + g)),
            whole((1, head_dim)),
            whole((tokens, head_dim)),
            whole((tokens, head_dim)),
            whole((1, head_dim)),
            whole((seq_len, head_dim)),
            whole((seq_len, head_dim)),
            whole((1, tokens)),
            whole((1, tokens)),
            whole((seq_len, 1)),
            whole((seq_len, 1)),
        ],
        out_specs=[
            pl.BlockSpec((tokens, group), lambda g: (0, g)),
            pl.BlockSpec((seq_len, 2 * head_dim), lambda g: (0, g)),
            pl.BlockSpec((heads, head_dim), lambda g: (g, 0)),
        ],
        out_shape=[
            jax.ShapeDtypeStruct((tokens, q_width), jnp.bfloat16),
            jax.ShapeDtypeStruct((seq_len, pair_width), jnp.bfloat16),
            jax.ShapeDtypeStruct((key_heads * heads, head_dim), jnp.float32),
        ],
        scratch_shapes=[
            pltpu.VMEM((seq_len, tokens), jnp.float32),
            pltpu.VMEM((seq_len, head_dim), jnp.float32),
            pltpu.VMEM((seq_len, head_dim), jnp.float32),
        ],
        compiler_params=pltpu.CompilerParams(vmem_limit_bytes=56 << 20),
        cost_estimate=pl.CostEstimate(
            flops=flops, bytes_accessed=12 * tokens * q_width, transcendentals=0
        ),
        name="attend_back",
    )(
        query_sum,
        query_low,
        cots,
        pair_sums,
        pair_sums,
        gains[0][None, :],
        *tables[:2],
        gains[1][None, :],
        *tables[2:],
        *(row[None, :] for row in query_rows),
        *(row[:, None] for row in key_rows),
    )


def sum_everywhere(vector):
    devices = lax.axis_size("ctx") * lax.axis_size("wt")
    spread = jnp.broadcast_to(vector[None, :], (devices, vector.shape[0]))
    return jnp.sum(
        lax.all_to_all(spread, ("ctx", "wt"), split_axis=0, concat_axis=0, tiled=True), axis=0
    )


def on_device(
    hidden_in,
    doc_lengths,
    routes,
    gain_attn,
    w_query,
    key_weight,
    value_weight,
    gain_query,
    gain_key,
    w_out,
    gain_moe,
    w_router,
    expert_gate,
    expert_up,
    expert_down,
    out_grad,
):
    tokens = hidden_in.shape[1]
    model_width = hidden_in.shape[2]
    ctx_size = lax.axis_size("ctx")
    wt_size = lax.axis_size("wt")
    devices = ctx_size * wt_size
    seq_len = tokens * ctx_size
    head_dim = gain_query.shape[0]
    q_width = w_query.shape[1]
    kv_width = key_weight.shape[1]
    key_heads = kv_width // head_dim
    expert_count = w_router.shape[1]
    top_count = routes.shape[2]
    assert expert_gate.shape[0] == 1 and expert_count == devices
    capacity = tokens * top_count // wt_size
    ctx_index = lax.axis_index("ctx")
    wt_index = lax.axis_index("wt")
    both = ("ctx", "wt")
    by_stream = ("wt", "ctx")

    def gather(value, axes):
        return lax.all_gather(value, axes, axis=0, tiled=True)

    def exchange(value, axes):
        return lax.all_to_all(value, axes, split_axis=0, concat_axis=0, tiled=True)

    def scatter_sum(value, axes):
        return lax.psum_scatter(value, axes, scatter_dimension=0, tiled=True)

    def cut(blocks):
        return [
            lax.dynamic_index_in_dim(blocks, lax.rem(wt_index + step, wt_size), keepdims=False)
            for step in range(wt_size)
        ]

    def pass_on(cuts):
        arrived = cuts[:1]
        for step in range(1, wt_size):
            pairs = [(w, (w + step) % wt_size) for w in range(wt_size)]
            arrived.append(lax.ppermute(cuts[step], "wt", pairs))
        return arrived

    def turn(blocks):
        return pass_on(cut(blocks))

    def add_up(blocks):
        return sum(block.astype(jnp.float32) for block in blocks)

    doc_ends = jnp.cumsum(doc_lengths[0])
    all_positions = jnp.arange(seq_len, dtype=jnp.int32)
    doc_all = jnp.sum((doc_ends[None, :] <= all_positions[:, None]).astype(jnp.int32), axis=1)
    first_pos = ctx_index * tokens
    my_positions = first_pos + jnp.arange(tokens, dtype=jnp.int32)
    my_docs = lax.dynamic_slice_in_dim(doc_all, first_pos, tokens)
    cosine_all, sine_all = rotary_tables(all_positions, head_dim)

    def mine_of(rows):
        return lax.dynamic_slice_in_dim(rows, first_pos, tokens)

    cosine_table, sine_table = mine_of(cosine_all), mine_of(sine_all)
    first_half = jnp.arange(head_dim) < head_dim // 2
    turned_all = jnp.where(first_half[None, :], -sine_all[:, 0, :], sine_all[:, 0, :])
    tables = (mine_of(cosine_all[:, 0, :]), mine_of(turned_all), cosine_all[:, 0, :], turned_all)

    expert_ids = jnp.arange(expert_count, dtype=jnp.int32)
    hits = jnp.sum((routes[0][:, :, None] == expert_ids[None, None, :]).astype(jnp.int32), axis=1)
    local_rank = jnp.cumsum(hits, axis=0) - hits
    assert expert_count <= tokens
    counts = jnp.pad(jnp.sum(hits, axis=0), (0, tokens - expert_count))
    plane_mine = jnp.concatenate(
        [
            hits.T.reshape(ctx_size, wt_size, tokens),
            jnp.broadcast_to(counts, (ctx_size, 1, tokens)),
        ],
        axis=1,
    )
    plane = exchange(plane_mine, "ctx")
    earlier = jnp.arange(ctx_size, dtype=jnp.int32)[:, None] < ctx_index
    offsets = jnp.sum(jnp.where(earlier, plane[:, wt_size, :expert_count], 0), axis=0)
    kept = (hits > 0) & (local_rank + offsets[None, :] < capacity)
    rank_lines = exchange(
        jnp.where(kept, local_rank, -1).T.reshape(ctx_size, wt_size, tokens).transpose(1, 0, 2),
        "wt",
    )
    keep_float = kept.astype(jnp.float32)
    hits_float = hits.astype(jnp.float32)

    def to_owner_rows(table):
        return table.reshape(tokens, ctx_size, wt_size).transpose(2, 1, 0).reshape(devices, tokens)

    def from_owner_rows(table):
        return table.reshape(wt_size, ctx_size, tokens).transpose(2, 1, 0).reshape(tokens, devices)

    hit_mine = exchange(to_owner_rows(hits), by_stream).reshape(wt_size, seq_len)
    slot_mine = jnp.cumsum(hit_mine, axis=1) - hit_mine
    slot_mine = jnp.where((hit_mine > 0) & (slot_mine < capacity), slot_mine, -1)
    send_slots = 2 * tokens * top_count // expert_count
    send_ids = jnp.arange(send_slots, dtype=jnp.int32)
    block_hits = jnp.sum(hit_mine.reshape(wt_size, ctx_size, tokens), axis=2)
    block_first = jnp.cumsum(block_hits, axis=1) - block_hits
    slot_ids = jnp.arange(capacity, dtype=jnp.int32)
    place = slot_mine[:, None, :] == slot_ids[None, :, None]
    place_low = after(place.astype(jnp.bfloat16), rank_lines)
    hit_plane = plane[:, :wt_size].transpose(1, 0, 2).reshape(wt_size, seq_len)
    hit_plane = hit_plane[(wt_index - jnp.arange(wt_size)) % wt_size]
    slot_plane = jnp.cumsum(hit_plane, axis=1) - hit_plane
    slot_plane = jnp.where((hit_plane > 0) & (slot_plane < capacity), slot_plane, -1)
    spread_low = (slot_plane[:, None, :] == slot_ids[None, :, None]).astype(jnp.bfloat16)

    resid_in = hidden_in[0].astype(jnp.float32)
    normed_in = norm_rows(resid_in, gain_attn).astype(jnp.bfloat16)
    router_pad = -expert_count % head_dim
    normed_in_all = gather(normed_in, "ctx")
    side_mine = jnp.concatenate(
        [key_weight, value_weight, jnp.pad(w_router, ((0, 0), (0, router_pad)))], axis=1
    )
    small_plane = ctx_size == 8
    if small_plane:
        side_weights, query_full, out_full = spread(
            [side_mine, w_query, w_out], (2, 4, 4), (False,) * 3, 1
        )
    else:
        side_weights = gather(side_mine, both)
        query_full = gather(w_query, both)
        out_full = gather(w_out, both)
    router_full = side_weights[:, 2 * kv_width : 2 * kv_width + expert_count]
    pair_sums = lax.optimization_barrier(
        matmul(normed_in_all, side_weights[:, : 2 * kv_width])
    )
    key_sum = mine_of(pair_sums)[:, :kv_width].reshape(tokens, key_heads, head_dim)
    if small_plane:
        cot_all = gather(after(out_grad[0], query_full), by_stream)
    query_sum = lax.optimization_barrier(matmul(normed_in, query_full))
    gains = (gain_query, gain_key)
    query_rows, key_rows = (my_positions, my_docs), (all_positions, doc_all)
    mixed_low, query_low = attend(query_sum, pair_sums, gains, tables, query_rows, key_rows)
    resid_mid = resid_in + matmul(mixed_low, out_full)
    normed_mid = norm_rows(resid_mid, gain_moe).astype(jnp.bfloat16)

    if small_plane:
        (mid_all,) = spread([normed_mid], (4,), (True,), 2)
    else:
        mid_all = gather(normed_mid, by_stream)
    mid_all = mid_all.reshape(wt_size, seq_len, model_width)
    logits = matmul(normed_mid, router_full)
    logit_exp = jnp.exp(logits - jnp.max(logits, axis=-1, keepdims=True))
    router_probs = logit_exp / jnp.sum(logit_exp, axis=-1, keepdims=True)
    chosen_total = jnp.sum(hits_float * router_probs, axis=1, keepdims=True)
    gate_kept = jnp.where(kept, router_probs / chosen_total, 0.0)
    gate_mine = exchange(to_owner_rows(gate_kept), by_stream).reshape(wt_size, seq_len)

    def column_blocks(value):
        width = value.shape[1] // ctx_size
        blocks = value.reshape(tokens, ctx_size, width).transpose(1, 0, 2)
        return exchange(blocks, "ctx").reshape(seq_len, width)

    def pick_rows(table):
        return (
            jnp.einsum("wkt,wtd->wkd", place_low, table, preferred_element_type=jnp.float32)
            .astype(jnp.bfloat16)
            .reshape(wt_size * capacity, model_width)
        )

    filled = pick_rows(mid_all)
    if not small_plane:
        cot_all = gather(after(out_grad[0], filled), by_stream)
    cot_all = cot_all.reshape(wt_size, seq_len, model_width)
    mixed_columns = column_blocks(mixed_low)
    gate_h = matmul(filled, expert_gate[0])
    up_h = matmul(filled, expert_up[0])
    sigma_h = jax.nn.sigmoid(gate_h)
    hidden_h = (gate_h * sigma_h * up_h).astype(jnp.bfloat16)
    result_rows = lax.optimization_barrier(
        matmul(hidden_h, expert_down[0]).astype(jnp.bfloat16)
    )
    cot_rows = pick_rows(cot_all)
    gate_rows = jnp.sum(jnp.where(place, gate_mine[:, None, :], 0.0), axis=2).reshape(-1)
    mixed_rows = (gate_rows[:, None] * result_rows.astype(jnp.float32)).astype(jnp.bfloat16)
    blocks_shape = (wt_size, capacity, -1)
    half = model_width // 2
    stream_mixed = turn(mixed_rows[:, :half].reshape(blocks_shape))
    gate_cot_rows = jnp.sum(
        result_rows.astype(jnp.float32) * cot_rows.astype(jnp.float32), axis=1
    ).reshape(wt_size, capacity)
    gate_cot_mine = jnp.sum(jnp.where(place, gate_cot_rows[:, :, None], 0.0), axis=1)
    out_rows_cot = (gate_rows[:, None] * cot_rows.astype(jnp.float32)).astype(jnp.bfloat16)
    hidden_cot = contract_cols(out_rows_cot, expert_down[0])
    gate_cot_h = (hidden_cot * up_h * sigma_h * (1.0 + gate_h * (1.0 - sigma_h))).astype(
        jnp.bfloat16
    )
    up_cot_h = (hidden_cot * gate_h * sigma_h).astype(jnp.bfloat16)
    gate_part = contract_cols(gate_cot_h, expert_gate[0])
    in_rows_cot = (
        gate_part + contract_cols(up_cot_h, expert_up[0])
    ).astype(jnp.bfloat16)

    def add_pairs(table, stream_rows):
        return contract_rows(
            table.reshape(wt_size * capacity, seq_len), jnp.concatenate(stream_rows, axis=0)
        ).astype(jnp.bfloat16)

    in_rows_cot, mixed_columns = lax.optimization_barrier((in_rows_cot, mixed_columns))

    stream_cots = turn(in_rows_cot[:, :half].reshape(blocks_shape))
    send_slot = jnp.where(
        send_ids[None, None, :] < block_hits[:, :, None],
        block_first[:, :, None] + send_ids[None, None, :],
        -1,
    ).reshape(wt_size, ctx_size * send_slots)
    send_low = (send_slot[:, :, None] == slot_ids[None, None, :]).astype(jnp.bfloat16)
    plane_sent = (
        jnp.einsum(
            "wjk,wkd->wjd",
            send_low,
            in_rows_cot[:, half:].reshape(blocks_shape),
            preferred_element_type=jnp.float32,
        )
        .astype(jnp.bfloat16)
        .reshape(wt_size, ctx_size, send_slots, half)
        .transpose(1, 0, 2, 3)
    )
    plane_cots = exchange(plane_sent, "ctx")
    first_part = scatter_sum(add_pairs(spread_low, stream_cots), "ctx")
    gate_cot = from_owner_rows(
        exchange(after(gate_cot_mine, plane_cots).reshape(devices, tokens), by_stream)
    )
    line_low = (rank_lines[:, :, :, None] == send_ids).astype(jnp.bfloat16)
    line_sent = jnp.einsum(
        "sctj,csjd->std", line_low, plane_cots, preferred_element_type=jnp.float32
    ).astype(jnp.bfloat16)
    line_cots = turn(line_sent)
    mixed_cuts = cut(after(mixed_rows[:, half:], line_sent).reshape(blocks_shape))
    stream_mixed_late = pass_on(mixed_cuts)
    returned_cot = after(
        jnp.concatenate([first_part.astype(jnp.float32), add_up(line_cots)], axis=1), mixed_cuts
    )
    out_cot = out_grad[0].astype(jnp.float32)

    kept_cot = gate_cot * keep_float
    chosen_cot = kept_cot / chosen_total - jnp.sum(
        kept_cot * router_probs, axis=1, keepdims=True
    ) / (chosen_total * chosen_total)
    probs_cot = hits_float * chosen_cot
    logit_cot = (
        router_probs * (probs_cot - jnp.sum(router_probs * probs_cot, axis=1, keepdims=True))
    ).astype(jnp.bfloat16)
    mid_cot = returned_cot + contract_cols(logit_cot, router_full)
    mid_norm_cot, gain_moe_terms = norm_back(resid_mid, gain_moe, mid_cot)
    resid_cot = out_cot + mid_norm_cot
    attn_cot = resid_cot.astype(jnp.bfloat16)

    mixed_cot = contract_cols(attn_cot, out_full)
    attn_cot_all = gather(attn_cot, "ctx")
    query_cot_low, pair_cots, gain_query_terms = attend_back(
        query_sum,
        query_low,
        mixed_cot.astype(jnp.bfloat16),
        pair_sums,
        gains,
        tables,
        query_rows,
        key_rows,
    )
    query_columns = column_blocks(query_cot_low)
    filled, hidden_h = after((filled, hidden_h), query_cot_low)
    normed_mid = after(normed_mid, query_columns)
    grad_gate = contract_rows(filled, gate_cot_h)
    grad_up = contract_rows(filled, up_cot_h)
    grad_down = contract_rows(hidden_h, out_rows_cot)
    grad_w_router = scatter_sum(contract_rows(normed_mid, logit_cot), both)
    spread_late = after(spread_low, query_cot_low)
    mixed_partial = jnp.concatenate(
        [add_pairs(spread_late, part) for part in (stream_mixed, stream_mixed_late)], axis=1
    )
    mixed_mine = scatter_sum(mixed_partial, "ctx").astype(jnp.float32)
    out_block = contract_rows(after(mixed_columns, query_cot_low), attn_cot_all)
    out_parts = turn(out_block.astype(jnp.bfloat16).reshape(wt_size, -1, model_width))
    pair_mine = scatter_sum(pair_cots, "ctx").reshape(tokens, key_heads, 2, head_dim)
    key_mine = pair_mine[:, :, 0].astype(jnp.float32)
    value_cot_low = pair_mine[:, :, 1].reshape(tokens, kv_width)
    key_pre, gain_key_terms = norm_back(
        key_sum,
        gain_key,
        rotate(key_mine, cosine_table, -sine_table),
    )
    key_cot_low = key_pre.reshape(tokens, kv_width).astype(jnp.bfloat16)
    pair_cot_low = jnp.concatenate([key_cot_low, value_cot_low], axis=1)

    def weight_parts(columns):
        width = columns.shape[1]
        block = contract_rows(normed_in_all, columns).astype(jnp.bfloat16)
        block = block.reshape(ctx_size, wt_size, -1, width).transpose(1, 0, 2, 3)
        return turn(block), block

    query_parts, query_block = weight_parts(after(query_columns, (out_block, mixed_partial)))
    pair_parts, pair_block = weight_parts(column_blocks(after(pair_cot_low, query_block)))
    in_cot = contract_cols(after(query_cot_low, query_block), query_full) + contract_cols(
        pair_cot_low, side_weights[:, : 2 * kv_width]
    )
    in_norm_cot, gain_attn_terms = norm_back(resid_in, gain_attn, in_cot)
    grad_in = resid_cot + in_norm_cot
    gain_sums = sum_everywhere(
        jnp.concatenate(
            [
                jnp.sum(gain_attn_terms, axis=0),
                jnp.sum(gain_query_terms, axis=0),
                jnp.sum(gain_key_terms, axis=(0, 1)),
                jnp.sum(gain_moe_terms, axis=0),
            ]
        )
    )
    query_parts = after(query_parts, (pair_block, gain_sums))
    grad_w_out = add_up(after(out_parts, query_parts))
    rows_mine = jnp.concatenate(
        [add_up(query_parts), add_up(after(pair_parts, query_parts))], axis=2
    ).astype(jnp.bfloat16)
    hidden_out = after(resid_mid, rows_mine) + mixed_mine
    grad_w_router = after(grad_w_router, rows_mine)
    rows = exchange(rows_mine, "ctx").transpose(1, 0, 2).astype(jnp.float32)
    query_columns = q_width // ctx_size
    grad_w_query = rows[:, :, :query_columns].reshape(-1, q_width)
    grad_pair = rows[:, :, query_columns:].reshape(-1, 2 * kv_width)
    grad_w_key = grad_pair[:, :kv_width]
    grad_w_value = grad_pair[:, kv_width:]
    grad_gain_attn = gain_sums[:model_width]
    grad_gain_query = gain_sums[model_width : model_width + head_dim]
    grad_gain_key = gain_sums[model_width + head_dim : model_width + 2 * head_dim]
    grad_gain_moe = gain_sums[model_width + 2 * head_dim :]
    return (
        hidden_out[None],
        grad_in[None],
        grad_gain_attn,
        grad_w_query,
        grad_w_key,
        grad_w_value,
        grad_gain_query,
        grad_gain_key,
        grad_w_out,
        grad_gain_moe,
        grad_w_router,
        grad_gate[None],
        grad_up[None],
        grad_down[None],
    )


def solution(mesh):
    in_specs = (
        P("wt", "ctx", None),
        P("wt", None),
        P("wt", "ctx", None),
        P(),
        P(("ctx", "wt"), None),
        P(("ctx", "wt"), None),
        P(("ctx", "wt"), None),
        P(),
        P(),
        P(("ctx", "wt"), None),
        P(),
        P(("ctx", "wt"), None),
        P(("ctx", "wt"), None, None),
        P(("ctx", "wt"), None, None),
        P(("ctx", "wt"), None, None),
        P("wt", "ctx", None),
    )
    out_specs = (
        P("wt", "ctx", None),
        P("wt", "ctx", None),
        P(),
        P(("ctx", "wt"), None),
        P(("ctx", "wt"), None),
        P(("ctx", "wt"), None),
        P(),
        P(),
        P(("ctx", "wt"), None),
        P(),
        P(("ctx", "wt"), None),
        P(("ctx", "wt"), None, None),
        P(("ctx", "wt"), None, None),
        P(("ctx", "wt"), None, None),
    )

    return jax.shard_map(
        on_device, mesh=mesh, in_specs=in_specs, out_specs=out_specs, check_vma=False
    )
```

```python
import functools
import math

import jax
import jax.numpy as jnp
from jax import lax
from jax.experimental import pallas as pl
from jax.experimental.pallas import tpu as pltpu
from jax.sharding import PartitionSpec as P


EPS = 1e-06
THETA = 1000000.0
MASKED = -1e30
MESH = pl.DeviceIdType.MESH


def norm_rows(value_rows, gain_vec):
    return (
        value_rows
        * lax.rsqrt(jnp.mean(value_rows * value_rows, axis=-1, keepdims=True) + EPS)
        * gain_vec
    )


def norm_back(value_rows, gain_vec, upstream):
    factor = lax.rsqrt(jnp.mean(value_rows * value_rows, axis=-1, keepdims=True) + EPS)
    normalized_input = value_rows * factor
    weighted = upstream * gain_vec
    inner_mean = jnp.mean(weighted * normalized_input, axis=-1, keepdims=True)
    return (factor * (weighted - normalized_input * inner_mean), upstream * normalized_input)


def rotary_tables(positions, head_dim):
    half_dim = head_dim // 2
    frequency = jnp.exp(
        jnp.arange(half_dim, dtype=jnp.float32) * (-2.0 * math.log(THETA) / head_dim)
    )
    angles = positions.astype(jnp.float32)[:, None] * frequency[None, :]
    angles = jnp.concatenate([angles, angles], axis=1)
    return (jnp.cos(angles)[:, None, :], jnp.sin(angles)[:, None, :])


def rotate(value_rows, cosine_table, sine_table):
    half_dim = value_rows.shape[-1] // 2
    turned = jnp.concatenate([-value_rows[..., half_dim:], value_rows[..., :half_dim]], axis=-1)
    return value_rows * cosine_table + turned * sine_table


def matmul(left_side, right_side):
    return jnp.dot(left_side, right_side, preferred_element_type=jnp.float32)


def contract_rows(left_side, right_side):
    return lax.dot_general(
        left_side, right_side, (((0,), (0,)), ((), ())), preferred_element_type=jnp.float32
    )


def contract_cols(left_side, right_side):
    return lax.dot_general(
        left_side, right_side, (((1,), (1,)), ((), ())), preferred_element_type=jnp.float32
    )


def spread_kernel(splits, streams_first, *refs):
    count = len(splits)
    ins, outs, stages = refs[:count], refs[count : 2 * count], refs[2 * count : 3 * count]
    send_sems, recv_sems, load_sems, store_sems = refs[3 * count :]
    ctx = lax.axis_index("ctx")
    z = lax.axis_index("wt")
    depth = lax.axis_size("wt")
    flip_y = ctx + 4 - 8 * (ctx // 4)
    step_x = 2 - 4 * ((ctx // 2) % 2)
    step_c = 1 - 2 * (ctx % 2)
    flip_x = ctx + step_x
    flip_xy = flip_y + step_x

    barrier = pltpu.get_barrier_semaphore()
    line = [lax.rem(z + d, depth) for d in range(1, depth)]
    for peer in line:
        pl.semaphore_signal(barrier, inc=1, device_id=(ctx, peer), device_id_type=MESH)
    for peer in (flip_x, flip_y, ctx + step_c):
        pl.semaphore_signal(barrier, inc=1, device_id=(peer, z), device_id_type=MESH)
    loads = []
    for k in range(count):
        loads.append(pltpu.make_async_copy(ins[k], stages[k], load_sems.at[k]))
        loads[k].start()
    pl.semaphore_wait(barrier, depth + 2)

    pieces = []
    for part in range(max(splits)):
        for k in range(count):
            if part < splits[k]:
                pieces.append((k, part))

    def group(k, owner, rows):
        view = outs[k]
        return view.at[:, owner, rows] if streams_first[k] else view.at[owner, :, rows]

    def block(k, rows):
        view = outs[k]
        return view.at[z, ctx, rows] if streams_first[k] else view.at[ctx, z, rows]

    def rows_of(k, part):
        size = ins[k].shape[0] // splits[k]
        return pl.ds(part * size, size)

    def send(number, slot, source, target, device):
        copy = pltpu.make_async_remote_copy(
            src_ref=source,
            dst_ref=target,
            send_sem=send_sems.at[number, slot],
            recv_sem=recv_sems.at[number, slot],
            device_id=device,
            device_id_type=MESH,
        )
        copy.start()
        return copy

    along = []
    for number, (k, part) in enumerate(pieces):
        rows = rows_of(k, part)
        along.append(
            [
                send(number, d, ins[k].at[rows], block(k, rows), (ctx, peer))
                for d, peer in enumerate(line)
            ]
        )
    stores = []
    for k in range(count):
        loads[k].wait()
        whole = pl.ds(0, ins[k].shape[0])
        stores.append(pltpu.make_async_copy(stages[k], block(k, whole), store_sems.at[k]))
        stores[k].start()
    for k in range(count):
        stores[k].wait()

    first_slot = depth - 1
    crossed, turned, shared = {}, {}, {}

    def owners(number):
        if number % 2:
            return flip_x, flip_y
        return flip_y, flip_x

    def cross(number):
        k, part = pieces[number]
        rows = rows_of(k, part)
        near, far = owners(number)
        for copy in along[number]:
            copy.wait_recv()
        mine = group(k, ctx, rows)
        crossed[number] = send(number, first_slot, mine, mine, (near, z))
        turned[number] = [send(number, first_slot + 1, mine, mine, (far, z))]
        shared[number] = [send(number, first_slot + 3, mine, mine, (ctx + step_c, z))]

    def turn_corner(number):
        k, part = pieces[number]
        rows = rows_of(k, part)
        near, far = owners(number)
        crossed[number].wait_recv()
        theirs = group(k, near, rows)
        turned[number].append(send(number, first_slot + 2, theirs, theirs, (far, z)))
        shared[number].append(send(number, first_slot + 4, theirs, theirs, (ctx + step_c, z)))

    def share(number):
        k, part = pieces[number]
        rows = rows_of(k, part)
        _, far = owners(number)
        for slot, (copy, owner) in enumerate(zip(turned[number], (far, flip_xy))):
            copy.wait_recv()
            theirs = group(k, owner, rows)
            shared[number].append(
                send(number, first_slot + 5 + slot, theirs, theirs, (ctx + step_c, z))
            )

    total = len(pieces)
    for step in range(total + 2):
        if step < total:
            cross(step)
        if 0 <= step - 1 < total:
            turn_corner(step - 1)
        if 0 <= step - 2 < total:
            share(step - 2)
    for number in range(total):
        for copy in shared[number]:
            copy.wait_recv()
        for copy in along[number] + [crossed[number]] + turned[number] + shared[number]:
            copy.wait_send()


def spread(values, splits, streams_first, channel):
    ctx_size, wt_size = lax.axis_size("ctx"), lax.axis_size("wt")
    total = sum(splits)
    heads = [(wt_size, ctx_size) if first else (ctx_size, wt_size) for first in streams_first]
    size = sum(value.size * value.dtype.itemsize for value in values)
    results = pl.pallas_call(
        functools.partial(spread_kernel, splits, streams_first),
        out_shape=[
            jax.ShapeDtypeStruct(head + value.shape, value.dtype)
            for head, value in zip(heads, values)
        ],
        in_specs=[pl.BlockSpec(memory_space=pl.ANY)] * len(values),
        out_specs=[pl.BlockSpec(memory_space=pl.ANY)] * len(values),
        scratch_shapes=[pltpu.VMEM(value.shape, value.dtype) for value in values]
        + [
            pltpu.SemaphoreType.DMA((total, wt_size + 6)),
            pltpu.SemaphoreType.DMA((total, wt_size + 6)),
            pltpu.SemaphoreType.DMA((len(values),)),
            pltpu.SemaphoreType.DMA((len(values),)),
        ],
        compiler_params=pltpu.CompilerParams(collective_id=channel, has_side_effects=True),
        cost_estimate=pl.CostEstimate(
            flops=0, bytes_accessed=2 * ctx_size * wt_size * size, transcendentals=0
        ),
    )(*values)
    return [result.reshape(-1, result.shape[-1]) for result in results]


def after(value, earlier):
    return lax.optimization_barrier((value, earlier))[0]


def stack_heads(block, first, head_dim, count):
    return jnp.concatenate(
        [block[:, (first + h) * head_dim : (first + h + 1) * head_dim] for h in range(count)],
        axis=0,
    )


def rotated(sums, gain_ref, cosine_ref, sine_ref):
    rows = norm_rows(sums, gain_ref[...])
    turned = pltpu.roll(rows, rows.shape[1] // 2, axis=1)
    return (rows * cosine_ref[...] + turned * sine_ref[...]).astype(jnp.bfloat16)


def attend_kernel(
    head_dim,
    together,
    query_ref,
    key_ref,
    value_ref,
    gain_ref,
    cosine_ref,
    sine_ref,
    key_gain_ref,
    key_cosine_ref,
    key_sine_ref,
    query_pos_ref,
    query_doc_ref,
    key_pos_ref,
    key_doc_ref,
    mixed_ref,
    query_low_ref,
    bias_ref,
):
    tokens = query_ref.shape[0]
    heads = query_ref.shape[1] // head_dim
    scale = head_dim ** (-0.5)

    @pl.when(pl.program_id(0) == 0)
    def _():
        allowed = (key_pos_ref[...] <= query_pos_ref[...]) & (
            key_doc_ref[...] == query_doc_ref[...]
        )
        bias_ref[...] = jnp.where(allowed, 0.0, MASKED)

    keys = rotated(key_ref[...], key_gain_ref, key_cosine_ref, key_sine_ref)
    values = value_ref[...].astype(jnp.bfloat16)
    for first in range(0, heads, together):
        for h in range(first, first + together):
            columns = slice(h * head_dim, (h + 1) * head_dim)
            query_low_ref[:, columns] = rotated(
                query_ref[:, columns], gain_ref, cosine_ref, sine_ref
            )
        queries = stack_heads(query_low_ref, first, head_dim, together)
        scores = contract_cols(queries, keys) * scale
        scores = scores + jnp.concatenate([bias_ref[...]] * together, axis=0)
        weights = jnp.exp(scores - jnp.max(scores, axis=1, keepdims=True))
        weights = weights / jnp.sum(weights, axis=1, keepdims=True)
        mixed = matmul(weights.astype(jnp.bfloat16), values)
        for h in range(together):
            columns = slice((first + h) * head_dim, (first + h + 1) * head_dim)
            mixed_ref[:, columns] = mixed[h * tokens : (h + 1) * tokens].astype(jnp.bfloat16)


def attend_back_kernel(
    head_dim,
    together,
    query_ref,
    query_low_ref,
    cot_ref,
    key_ref,
    value_ref,
    gain_ref,
    cosine_ref,
    sine_ref,
    key_gain_ref,
    key_cosine_ref,
    key_sine_ref,
    query_pos_ref,
    query_doc_ref,
    key_pos_ref,
    key_doc_ref,
    query_cot_ref,
    pair_cot_ref,
    gain_cot_ref,
    bias_ref,
    key_sum_ref,
    value_sum_ref,
):
    tokens = query_ref.shape[0]
    heads = query_ref.shape[1] // head_dim
    scale = head_dim ** (-0.5)

    @pl.when(pl.program_id(0) == 0)
    def _():
        allowed = (key_pos_ref[...] <= query_pos_ref[...]) & (
            key_doc_ref[...] == query_doc_ref[...]
        )
        bias_ref[...] = jnp.where(allowed, 0.0, MASKED)

    keys = rotated(key_ref[...], key_gain_ref, key_cosine_ref, key_sine_ref)
    values = value_ref[...].astype(jnp.bfloat16)
    for first in range(0, heads, together):
        queries = stack_heads(query_low_ref, first, head_dim, together)
        cots = stack_heads(cot_ref, first, head_dim, together)
        scores = contract_cols(keys, queries) * scale
        scores = scores + jnp.concatenate([bias_ref[...]] * together, axis=1)
        weights = jnp.exp(scores - jnp.max(scores, axis=0, keepdims=True))
        weights = weights / jnp.sum(weights, axis=0, keepdims=True)
        weight_cot = contract_cols(values, cots)
        delta = jnp.sum(weights * weight_cot, axis=0, keepdims=True)
        score_cot = (weights * (weight_cot - delta)).astype(jnp.bfloat16)
        value_part = matmul(weights.astype(jnp.bfloat16), cots)
        key_part = matmul(score_cot, queries)
        if first:
            value_sum_ref[...] += value_part
            key_sum_ref[...] += key_part
        else:
            value_sum_ref[...] = value_part
            key_sum_ref[...] = key_part
        query_part = contract_rows(score_cot, keys) * scale
        for h in range(together):
            columns = slice((first + h) * head_dim, (first + h + 1) * head_dim)
            upstream = query_part[h * tokens : (h + 1) * tokens]
            turned = pltpu.roll(upstream, head_dim // 2, axis=1)
            upstream = upstream * cosine_ref[...] - turned * sine_ref[...]
            rows_cot, terms = norm_back(query_ref[:, columns], gain_ref[...], upstream)
            query_cot_ref[:, columns] = rows_cot.astype(jnp.bfloat16)
            gain_cot_ref[first + h : first + h + 1, :] = jnp.sum(terms, axis=0, keepdims=True)
    pair_cot_ref[:, :head_dim] = (key_sum_ref[...] * scale).astype(jnp.bfloat16)
    pair_cot_ref[:, head_dim:] = value_sum_ref[...].astype(jnp.bfloat16)


def attend(query_sum, pair_sums, gains, tables, query_rows, key_rows):
    tokens, q_width = query_sum.shape
    seq_len, pair_width = pair_sums.shape
    head_dim = gains[0].shape[0]
    key_heads = pair_width // (2 * head_dim)
    group = q_width // key_heads
    whole = lambda shape: pl.BlockSpec(shape, lambda g: (0, 0))
    flops = 4 * tokens * seq_len * q_width
    return pl.pallas_call(
        functools.partial(attend_kernel, head_dim, 2),
        grid=(key_heads,),
        in_specs=[
            pl.BlockSpec((tokens, group), lambda g: (0, g)),
            pl.BlockSpec((seq_len, head_dim), lambda g: (0, g)),
            pl.BlockSpec((seq_len, head_dim), lambda g: (0, key_heads + g)),
            whole((1, head_dim)),
            whole((tokens, head_dim)),
            whole((tokens, head_dim)),
            whole((1, head_dim)),
            whole((seq_len, head_dim)),
            whole((seq_len, head_dim)),
            whole((tokens, 1)),
            whole((tokens, 1)),
            whole((1, seq_len)),
            whole((1, seq_len)),
        ],
        out_specs=[pl.BlockSpec((tokens, group), lambda g: (0, g))] * 2,
        out_shape=[jax.ShapeDtypeStruct((tokens, q_width), jnp.bfloat16)] * 2,
        scratch_shapes=[pltpu.VMEM((tokens, seq_len), jnp.float32)],
        compiler_params=pltpu.CompilerParams(vmem_limit_bytes=48 << 20),
        cost_estimate=pl.CostEstimate(
            flops=flops, bytes_accessed=8 * tokens * q_width, transcendentals=0
        ),
        name="attend",
    )(
        query_sum,
        pair_sums,
        pair_sums,
        gains[0][None, :],
        *tables[:2],
        gains[1][None, :],
        *tables[2:],
        *(row[:, None] for row in query_rows),
        *(row[None, :] for row in key_rows),
    )


def attend_back(query_sum, query_low, cots, pair_sums, gains, tables, query_rows, key_rows):
    tokens, q_width = query_sum.shape
    seq_len, pair_width = pair_sums.shape
    head_dim = gains[0].shape[0]
    key_heads = pair_width // (2 * head_dim)
    group = q_width // key_heads
    heads = group // head_dim
    whole = lambda shape: pl.BlockSpec(shape, lambda g: (0, 0))
    flops = 10 * tokens * seq_len * q_width
    return pl.pallas_call(
        functools.partial(attend_back_kernel, head_dim, 2),
        grid=(key_heads,),
        in_specs=[
            pl.BlockSpec((tokens, group), lambda g: (0, g)),
            pl.BlockSpec((tokens, group), lambda g: (0, g)),
            pl.BlockSpec((tokens, group), lambda g: (0, g)),
            pl.BlockSpec((seq_len, head_dim), lambda g: (0, g)),
            pl.BlockSpec((seq_len, head_dim), lambda g: (0, key_heads + g)),
            whole((1, head_dim)),
            whole((tokens, head_dim)),
            whole((tokens, head_dim)),
            whole((1, head_dim)),
            whole((seq_len, head_dim)),
            whole((seq_len, head_dim)),
            whole((1, tokens)),
            whole((1, tokens)),
            whole((seq_len, 1)),
            whole((seq_len, 1)),
        ],
        out_specs=[
            pl.BlockSpec((tokens, group), lambda g: (0, g)),
            pl.BlockSpec((seq_len, 2 * head_dim), lambda g: (0, g)),
            pl.BlockSpec((heads, head_dim), lambda g: (g, 0)),
        ],
        out_shape=[
            jax.ShapeDtypeStruct((tokens, q_width), jnp.bfloat16),
            jax.ShapeDtypeStruct((seq_len, pair_width), jnp.bfloat16),
            jax.ShapeDtypeStruct((key_heads * heads, head_dim), jnp.float32),
        ],
        scratch_shapes=[
            pltpu.VMEM((seq_len, tokens), jnp.float32),
            pltpu.VMEM((seq_len, head_dim), jnp.float32),
            pltpu.VMEM((seq_len, head_dim), jnp.float32),
        ],
        compiler_params=pltpu.CompilerParams(vmem_limit_bytes=56 << 20),
        cost_estimate=pl.CostEstimate(
            flops=flops, bytes_accessed=12 * tokens * q_width, transcendentals=0
        ),
        name="attend_back",
    )(
        query_sum,
        query_low,
        cots,
        pair_sums,
        pair_sums,
        gains[0][None, :],
        *tables[:2],
        gains[1][None, :],
        *tables[2:],
        *(row[None, :] for row in query_rows),
        *(row[:, None] for row in key_rows),
    )


def sum_everywhere(own_parts, vector):
    devices = own_parts.shape[0]
    sent = jnp.concatenate(
        [own_parts, jnp.broadcast_to(vector[None, :], (devices, vector.shape[0]))], axis=1
    )
    sums = jnp.sum(
        lax.all_to_all(sent, ("ctx", "wt"), split_axis=0, concat_axis=0, tiled=True), axis=0
    )
    return sums


def on_device(
    hidden_in,
    doc_lengths,
    routes,
    gain_attn,
    w_query,
    key_weight,
    value_weight,
    gain_query,
    gain_key,
    w_out,
    gain_moe,
    w_router,
    expert_gate,
    expert_up,
    expert_down,
    out_grad,
):
    tokens = hidden_in.shape[1]
    model_width = hidden_in.shape[2]
    ctx_size = lax.axis_size("ctx")
    wt_size = lax.axis_size("wt")
    devices = ctx_size * wt_size
    seq_len = tokens * ctx_size
    head_dim = gain_query.shape[0]
    q_width = w_query.shape[1]
    kv_width = key_weight.shape[1]
    key_heads = kv_width // head_dim
    expert_count = w_router.shape[1]
    top_count = routes.shape[2]
    assert expert_gate.shape[0] == 1 and expert_count == devices
    capacity = tokens * top_count // wt_size
    ctx_index = lax.axis_index("ctx")
    wt_index = lax.axis_index("wt")
    both = ("ctx", "wt")
    by_stream = ("wt", "ctx")

    def gather(value, axes):
        return lax.all_gather(value, axes, axis=0, tiled=True)

    def exchange(value, axes):
        return lax.all_to_all(value, axes, split_axis=0, concat_axis=0, tiled=True)

    def scatter_sum(value, axes):
        return lax.psum_scatter(value, axes, scatter_dimension=0, tiled=True)

    def cut(blocks):
        return [
            lax.dynamic_index_in_dim(blocks, lax.rem(wt_index + step, wt_size), keepdims=False)
            for step in range(wt_size)
        ]

    def pass_on(cuts):
        arrived = cuts[:1]
        for step in range(1, wt_size):
            pairs = [(w, (w + step) % wt_size) for w in range(wt_size)]
            arrived.append(lax.ppermute(cuts[step], "wt", pairs))
        return arrived

    def turn(blocks):
        return pass_on(cut(blocks))

    def add_up(blocks):
        return sum(block.astype(jnp.float32) for block in blocks)

    doc_ends = jnp.cumsum(doc_lengths[0])
    all_positions = jnp.arange(seq_len, dtype=jnp.int32)
    doc_all = jnp.sum((doc_ends[None, :] <= all_positions[:, None]).astype(jnp.int32), axis=1)
    first_pos = ctx_index * tokens
    my_positions = first_pos + jnp.arange(tokens, dtype=jnp.int32)
    my_docs = lax.dynamic_slice_in_dim(doc_all, first_pos, tokens)
    cosine_all, sine_all = rotary_tables(all_positions, head_dim)

    def mine_of(rows):
        return lax.dynamic_slice_in_dim(rows, first_pos, tokens)

    cosine_table, sine_table = mine_of(cosine_all), mine_of(sine_all)
    first_half = jnp.arange(head_dim) < head_dim // 2
    turned_all = jnp.where(first_half[None, :], -sine_all[:, 0, :], sine_all[:, 0, :])
    tables = (mine_of(cosine_all[:, 0, :]), mine_of(turned_all), cosine_all[:, 0, :], turned_all)

    expert_ids = jnp.arange(expert_count, dtype=jnp.int32)
    hits = jnp.sum((routes[0][:, :, None] == expert_ids[None, None, :]).astype(jnp.int32), axis=1)
    local_rank = jnp.cumsum(hits, axis=0) - hits
    assert expert_count <= tokens
    counts = jnp.pad(jnp.sum(hits, axis=0), (0, tokens - expert_count))
    plane_mine = jnp.concatenate(
        [
            hits.T.reshape(ctx_size, wt_size, tokens),
            jnp.broadcast_to(counts, (ctx_size, 1, tokens)),
        ],
        axis=1,
    )
    plane = exchange(plane_mine, "ctx")
    earlier = jnp.arange(ctx_size, dtype=jnp.int32)[:, None] < ctx_index
    offsets = jnp.sum(jnp.where(earlier, plane[:, wt_size, :expert_count], 0), axis=0)
    kept = (hits > 0) & (local_rank + offsets[None, :] < capacity)
    rank_lines = exchange(
        jnp.where(kept, local_rank, -1).T.reshape(ctx_size, wt_size, tokens).transpose(1, 0, 2),
        "wt",
    )
    keep_float = kept.astype(jnp.float32)
    hits_float = hits.astype(jnp.float32)

    def to_owner_rows(table):
        return table.reshape(tokens, ctx_size, wt_size).transpose(2, 1, 0).reshape(devices, tokens)

    def from_owner_rows(table):
        return table.reshape(wt_size, ctx_size, tokens).transpose(2, 1, 0).reshape(tokens, devices)

    hit_mine = exchange(to_owner_rows(hits), by_stream).reshape(wt_size, seq_len)
    slot_mine = jnp.cumsum(hit_mine, axis=1) - hit_mine
    slot_mine = jnp.where((hit_mine > 0) & (slot_mine < capacity), slot_mine, -1)
    send_slots = 2 * tokens * top_count // expert_count
    send_ids = jnp.arange(send_slots, dtype=jnp.int32)
    block_hits = jnp.sum(hit_mine.reshape(wt_size, ctx_size, tokens), axis=2)
    block_first = jnp.cumsum(block_hits, axis=1) - block_hits
    slot_ids = jnp.arange(capacity, dtype=jnp.int32)
    place = slot_mine[:, None, :] == slot_ids[None, :, None]
    place_low = after(place.astype(jnp.bfloat16), rank_lines)
    hit_plane = plane[:, :wt_size].transpose(1, 0, 2).reshape(wt_size, seq_len)
    hit_plane = hit_plane[(wt_index - jnp.arange(wt_size)) % wt_size]
    slot_plane = jnp.cumsum(hit_plane, axis=1) - hit_plane
    slot_plane = jnp.where((hit_plane > 0) & (slot_plane < capacity), slot_plane, -1)
    spread_low = (slot_plane[:, None, :] == slot_ids[None, :, None]).astype(jnp.bfloat16)

    resid_in = hidden_in[0].astype(jnp.float32)
    normed_in = norm_rows(resid_in, gain_attn).astype(jnp.bfloat16)
    router_pad = -expert_count % head_dim
    normed_in_all = gather(normed_in, "ctx")
    side_mine = jnp.concatenate(
        [key_weight, value_weight, jnp.pad(w_router, ((0, 0), (0, router_pad)))], axis=1
    )
    small_plane = ctx_size == 8
    if small_plane:
        side_weights, query_full, out_full = spread(
            [side_mine, w_query, w_out], (2, 4, 4), (False,) * 3, 1
        )
    else:
        side_weights = gather(side_mine, both)
        query_full = gather(w_query, both)
        out_full = gather(w_out, both)
    router_full = side_weights[:, 2 * kv_width : 2 * kv_width + expert_count]
    pair_sums = lax.optimization_barrier(
        matmul(normed_in_all, side_weights[:, : 2 * kv_width])
    )
    key_sum = mine_of(pair_sums)[:, :kv_width].reshape(tokens, key_heads, head_dim)
    if small_plane:
        cot_all = gather(after(out_grad[0], query_full), by_stream)
    query_sum = lax.optimization_barrier(matmul(normed_in, query_full))
    gains = (gain_query, gain_key)
    query_rows, key_rows = (my_positions, my_docs), (all_positions, doc_all)
    mixed_low, query_low = attend(query_sum, pair_sums, gains, tables, query_rows, key_rows)
    resid_mid = resid_in + matmul(mixed_low, out_full)
    normed_mid = norm_rows(resid_mid, gain_moe).astype(jnp.bfloat16)

    if small_plane:
        (mid_all,) = spread([normed_mid], (4,), (True,), 2)
    else:
        mid_all = gather(normed_mid, by_stream)
    mid_all = mid_all.reshape(wt_size, seq_len, model_width)
    logits = matmul(normed_mid, router_full)
    logit_exp = jnp.exp(logits - jnp.max(logits, axis=-1, keepdims=True))
    router_probs = logit_exp / jnp.sum(logit_exp, axis=-1, keepdims=True)
    chosen_total = jnp.sum(hits_float * router_probs, axis=1, keepdims=True)
    gate_kept = jnp.where(kept, router_probs / chosen_total, 0.0)
    gate_mine = exchange(to_owner_rows(gate_kept), by_stream).reshape(wt_size, seq_len)

    def column_blocks(value):
        width = value.shape[1] // ctx_size
        blocks = value.reshape(tokens, ctx_size, width).transpose(1, 0, 2)
        return exchange(blocks, "ctx").reshape(seq_len, width)

    def pick_rows(table):
        return (
            jnp.einsum("wkt,wtd->wkd", place_low, table, preferred_element_type=jnp.float32)
            .astype(jnp.bfloat16)
            .reshape(wt_size * capacity, model_width)
        )

    filled = pick_rows(mid_all)
    if not small_plane:
        cot_all = gather(after(out_grad[0], filled), by_stream)
    cot_all = cot_all.reshape(wt_size, seq_len, model_width)
    mixed_columns = column_blocks(mixed_low)
    gate_h = matmul(filled, expert_gate[0])
    up_h = matmul(filled, expert_up[0])
    sigma_h = jax.nn.sigmoid(gate_h)
    hidden_h = (gate_h * sigma_h * up_h).astype(jnp.bfloat16)
    result_rows = lax.optimization_barrier(
        matmul(hidden_h, expert_down[0]).astype(jnp.bfloat16)
    )
    cot_rows = pick_rows(cot_all)
    gate_rows = jnp.sum(jnp.where(place, gate_mine[:, None, :], 0.0), axis=2).reshape(-1)
    mixed_rows = (gate_rows[:, None] * result_rows.astype(jnp.float32)).astype(jnp.bfloat16)
    blocks_shape = (wt_size, capacity, -1)
    half = model_width // 2
    stream_mixed = turn(mixed_rows[:, :half].reshape(blocks_shape))
    gate_cot_rows = jnp.sum(
        result_rows.astype(jnp.float32) * cot_rows.astype(jnp.float32), axis=1
    ).reshape(wt_size, capacity)
    gate_cot_mine = jnp.sum(jnp.where(place, gate_cot_rows[:, :, None], 0.0), axis=1)
    out_rows_cot = (gate_rows[:, None] * cot_rows.astype(jnp.float32)).astype(jnp.bfloat16)
    hidden_cot = contract_cols(out_rows_cot, expert_down[0])
    gate_cot_h = (hidden_cot * up_h * sigma_h * (1.0 + gate_h * (1.0 - sigma_h))).astype(
        jnp.bfloat16
    )
    up_cot_h = (hidden_cot * gate_h * sigma_h).astype(jnp.bfloat16)
    gate_part = contract_cols(gate_cot_h, expert_gate[0])
    in_rows_cot = (
        gate_part + contract_cols(up_cot_h, expert_up[0])
    ).astype(jnp.bfloat16)

    def add_pairs(table, stream_rows):
        return contract_rows(
            table.reshape(wt_size * capacity, seq_len), jnp.concatenate(stream_rows, axis=0)
        ).astype(jnp.bfloat16)

    gate_cot = exchange(gate_cot_mine.reshape(devices, tokens), by_stream)
    in_rows_cot, mixed_columns, gate_cot = lax.optimization_barrier(
        (in_rows_cot, mixed_columns, gate_cot)
    )
    gate_cot = from_owner_rows(gate_cot)

    stream_cots = turn(in_rows_cot[:, :half].reshape(blocks_shape))
    send_slot = jnp.where(
        send_ids[None, None, :] < block_hits[:, :, None],
        block_first[:, :, None] + send_ids[None, None, :],
        -1,
    ).reshape(wt_size, ctx_size * send_slots)
    send_low = (send_slot[:, :, None] == slot_ids[None, None, :]).astype(jnp.bfloat16)
    plane_sent = (
        jnp.einsum(
            "wjk,wkd->wjd",
            send_low,
            in_rows_cot[:, half:].reshape(blocks_shape),
            preferred_element_type=jnp.float32,
        )
        .astype(jnp.bfloat16)
        .reshape(wt_size, ctx_size, send_slots, half)
        .transpose(1, 0, 2, 3)
    )
    plane_cots = exchange(plane_sent, "ctx")
    first_part = scatter_sum(add_pairs(spread_low, stream_cots), "ctx")
    line_low = (rank_lines[:, :, :, None] == send_ids).astype(jnp.bfloat16)
    line_sent = jnp.einsum(
        "sctj,csjd->std", line_low, plane_cots, preferred_element_type=jnp.float32
    ).astype(jnp.bfloat16)
    line_cots = turn(line_sent)
    mixed_cuts = cut(after(mixed_rows[:, half:], line_cots).reshape(blocks_shape))
    stream_mixed_late = pass_on(mixed_cuts)
    returned_cot = jnp.concatenate(
        [first_part.astype(jnp.float32), add_up(line_cots)], axis=1
    )
    out_cot = out_grad[0].astype(jnp.float32)

    kept_cot = gate_cot * keep_float
    chosen_cot = kept_cot / chosen_total - jnp.sum(
        kept_cot * router_probs, axis=1, keepdims=True
    ) / (chosen_total * chosen_total)
    probs_cot = hits_float * chosen_cot
    logit_cot = (
        router_probs * (probs_cot - jnp.sum(router_probs * probs_cot, axis=1, keepdims=True))
    ).astype(jnp.bfloat16)
    mid_cot = returned_cot + contract_cols(logit_cot, router_full)
    mid_norm_cot, gain_moe_terms = norm_back(resid_mid, gain_moe, mid_cot)
    resid_cot = out_cot + mid_norm_cot
    attn_cot = resid_cot.astype(jnp.bfloat16)

    mixed_cot = contract_cols(attn_cot, out_full)
    attn_cot_all = gather(attn_cot, "ctx")
    query_cot_low, pair_cots, gain_query_terms = attend_back(
        query_sum,
        query_low,
        mixed_cot.astype(jnp.bfloat16),
        pair_sums,
        gains,
        tables,
        query_rows,
        key_rows,
    )
    query_columns = column_blocks(query_cot_low)
    normed_mid = after(normed_mid, query_columns)
    router_parts = contract_rows(normed_mid, logit_cot).reshape(devices, -1)
    out_block = contract_rows(after(mixed_columns, query_cot_low), attn_cot_all)
    spread_late = after(spread_low, out_block)
    mixed_partial = jnp.concatenate(
        [add_pairs(spread_late, part) for part in (stream_mixed, stream_mixed_late)], axis=1
    )
    mixed_mine = scatter_sum(mixed_partial, "ctx").astype(jnp.float32)
    out_parts = turn(out_block.astype(jnp.bfloat16).reshape(wt_size, -1, model_width))
    pair_mine = scatter_sum(pair_cots, "ctx").reshape(tokens, key_heads, 2, head_dim)
    key_mine = pair_mine[:, :, 0].astype(jnp.float32)
    value_cot_low = pair_mine[:, :, 1].reshape(tokens, kv_width)
    key_pre, gain_key_terms = norm_back(
        key_sum,
        gain_key,
        rotate(key_mine, cosine_table, -sine_table),
    )
    key_cot_low = key_pre.reshape(tokens, kv_width).astype(jnp.bfloat16)
    pair_cot_low = jnp.concatenate([key_cot_low, value_cot_low], axis=1)

    def weight_parts(columns):
        width = columns.shape[1]
        block = contract_rows(normed_in_all, columns).astype(jnp.bfloat16)
        block = block.reshape(ctx_size, wt_size, -1, width).transpose(1, 0, 2, 3)
        return turn(block), block

    query_parts, query_block = weight_parts(after(query_columns, (out_block, mixed_partial)))
    filled, hidden_h = after((filled, hidden_h), query_block)
    grad_gate = contract_rows(filled, gate_cot_h)
    grad_up = contract_rows(filled, up_cot_h)
    grad_down = contract_rows(hidden_h, out_rows_cot)
    pair_parts, pair_block = weight_parts(column_blocks(after(pair_cot_low, query_block)))
    in_cot = contract_cols(after(query_cot_low, query_block), query_full) + contract_cols(
        pair_cot_low, side_weights[:, : 2 * kv_width]
    )
    in_norm_cot, gain_attn_terms = norm_back(resid_in, gain_attn, in_cot)
    grad_in = resid_cot + in_norm_cot
    sums = sum_everywhere(
        router_parts,
        jnp.concatenate(
            [
                jnp.sum(gain_attn_terms, axis=0),
                jnp.sum(gain_query_terms, axis=0),
                jnp.sum(gain_key_terms, axis=(0, 1)),
                jnp.sum(gain_moe_terms, axis=0),
            ]
        ),
    )
    query_parts = after(query_parts, (pair_block, sums))
    router_sums, gain_sums = sums[: router_parts.shape[1]], sums[router_parts.shape[1] :]
    grad_w_out = add_up(after(out_parts, query_parts))
    rows_mine = jnp.concatenate(
        [add_up(query_parts), add_up(after(pair_parts, query_parts))], axis=2
    ).astype(jnp.bfloat16)
    hidden_out = after(resid_mid, rows_mine) + mixed_mine
    rows = exchange(rows_mine, "ctx").transpose(1, 0, 2).astype(jnp.float32)
    query_columns = q_width // ctx_size
    grad_w_query = rows[:, :, :query_columns].reshape(-1, q_width)
    grad_pair = rows[:, :, query_columns:].reshape(-1, 2 * kv_width)
    grad_w_key = grad_pair[:, :kv_width]
    grad_w_value = grad_pair[:, kv_width:]
    grad_w_router = router_sums.reshape(w_router.shape)
    grad_gain_attn = gain_sums[:model_width]
    grad_gain_query = gain_sums[model_width : model_width + head_dim]
    grad_gain_key = gain_sums[model_width + head_dim : model_width + 2 * head_dim]
    grad_gain_moe = gain_sums[model_width + 2 * head_dim :]
    return (
        hidden_out[None],
        grad_in[None],
        grad_gain_attn,
        grad_w_query,
        grad_w_key,
        grad_w_value,
        grad_gain_query,
        grad_gain_key,
        grad_w_out,
        grad_gain_moe,
        grad_w_router,
        grad_gate[None],
        grad_up[None],
        grad_down[None],
    )


def solution(mesh):
    in_specs = (
        P("wt", "ctx", None),
        P("wt", None),
        P("wt", "ctx", None),
        P(),
        P(("ctx", "wt"), None),
        P(("ctx", "wt"), None),
        P(("ctx", "wt"), None),
        P(),
        P(),
        P(("ctx", "wt"), None),
        P(),
        P(("ctx", "wt"), None),
        P(("ctx", "wt"), None, None),
        P(("ctx", "wt"), None, None),
        P(("ctx", "wt"), None, None),
        P("wt", "ctx", None),
    )
    out_specs = (
        P("wt", "ctx", None),
        P("wt", "ctx", None),
        P(),
        P(("ctx", "wt"), None),
        P(("ctx", "wt"), None),
        P(("ctx", "wt"), None),
        P(),
        P(),
        P(("ctx", "wt"), None),
        P(),
        P(("ctx", "wt"), None),
        P(("ctx", "wt"), None, None),
        P(("ctx", "wt"), None, None),
        P(("ctx", "wt"), None, None),
    )

    return jax.shard_map(
        on_device, mesh=mesh, in_specs=in_specs, out_specs=out_specs, check_vma=False
    )
```
